32 devices in a mesh: ctx: 8 (over z, x), head: 4 (over y, core).
Axes of the slice: x: 2, y: 2, z: 4, core: 2. Of those that a mesh axis runs over, the one named last changes fastest.
Arguments:
- queries: bfloat16 [8192, 4096], P('ctx', 'head'), may hold values from -24 to 24
- keys: bfloat16 [8192, 4096], P('ctx', 'head'), may hold values from -4 to 4
- values: bfloat16 [8192, 4096], P('ctx', 'head'), may hold values from -6 to 6
- cluster_of: int32 [32, 8192], P('head', 'ctx'), may hold values from 0 to 255, as said below
- slot_of: int32 [32, 8192], P('head', 'ctx'), may hold values from 0 to 7
- centroids: float32 [32, 256, 128], P('head', 'ctx'), may hold values from -6 to 6
- out_weight: bfloat16 [4096, 4096], P('head'), may hold values from -0.125 to 0.125
Outputs:
- projected: bfloat16 [8192, 4096], P('ctx', 'head')
- new_centroids: float32 [32, 256, 128], P('head', 'ctx')
The draws below stay inside these ranges and needn't reach their ends.
Inputs may be any that keep to these rules, and one draw needn't show every extreme that they name: `cluster_of`: within the tokens of one index of ctx and one head, no two tokens share both cluster and slot, and in every such block some cluster holds all 8 slots; a cluster of a head may hold no token at all.
All inputs are finite; a program needn't handle non-finite values.
Results may differ from the reference program's by a relative error of at most 0.0085.
Values may be sent and summed in bfloat16 or wider, within the bound.
No kernel may reach another device: no remote copies, remote signals or barrier semaphores. Data moves between devices by JAX's collectives and lax.ppermute only.
A program may use at most 128 MiB of HBM per device.

```python
import math
import jax
import jax.numpy as jnp
from jax import lax

HEADS = 32
HD = 128
D = 4096
CLUSTERS = 256
TOK_DEV = 1024
SLOTS = 8
TOKENS = 8192
CAP = 64


hot_count = 4


empty_count = 2


def key_field(key):
    shape = (TOKENS, HEADS * HD)
    return jnp.clip(jax.random.normal(jax.random.fold_in(key, 3), shape, jnp.float32), -4.0, 4.0)


def draw_keys(key, part):
    return key_field(key).astype(jnp.bfloat16)


def draw_queries(key, part):
    shape = (TOKENS, HEADS * HD)
    raw = jax.random.normal(jax.random.fold_in(key, 5), shape, jnp.float32)
    return jnp.clip(raw, -4.0, 4.0).astype(jnp.bfloat16)


def routing_table(key):
    per_head = TOKENS // TOK_DEV
    blocks = HEADS * per_head
    pairs = CLUSTERS * SLOTS
    order_score = jax.random.randint(jax.random.fold_in(key, 14), (HEADS, CLUSTERS), 0, 2 ** 17, dtype=jnp.int32)
    order_score = order_score * CLUSTERS + jnp.arange(CLUSTERS, dtype=jnp.int32)[None, :]
    cluster_rank = jnp.argsort(jnp.argsort(order_score, axis=1), axis=1).astype(jnp.int32)
    pair_rank = jnp.repeat(cluster_rank, SLOTS, axis=1)
    pair_rank = jnp.repeat(pair_rank, per_head, axis=0)
    base = jax.random.randint(jax.random.fold_in(key, 11), (blocks, pairs), 0, 2 ** 17, dtype=jnp.int32)
    hot_rank = jax.random.randint(jax.random.fold_in(key, 12), (blocks, hot_count), empty_count, CLUSTERS, dtype=jnp.int32)
    is_hot = jnp.any(pair_rank[:, :, None] == hot_rank[:, None, :], axis=2)
    pair_index = jnp.arange(pairs, dtype=jnp.int32)[None, :]
    score = (base + jnp.where(is_hot, 2 ** 17, 0)) * pairs + pair_index
    score = jnp.where(pair_rank < empty_count, pair_index - pairs, score)
    top_scores, chosen = lax.top_k(score, TOK_DEV)
    shuffle = jax.random.randint(jax.random.fold_in(key, 13), (blocks, TOK_DEV), 0, 2 ** 17, dtype=jnp.int32) * TOK_DEV
    shuffle = shuffle + jnp.arange(TOK_DEV, dtype=jnp.int32)[None, :]
    order = jnp.argsort(shuffle, axis=1)
    assigned = jnp.take_along_axis(chosen.astype(jnp.int32), order.astype(jnp.int32), axis=1)
    return assigned.reshape(HEADS, TOKENS)


def draw_cluster_of(key, part):
    return (routing_table(key) // SLOTS).astype(jnp.int32)


def draw_slot_of(key, part):
    return (routing_table(key) % SLOTS).astype(jnp.int32)


def spiked(array, stream_key, source, target, blocks, factor):
    owner, partner = [(jnp.arange(array.shape[dim]) // (array.shape[dim] // blocks)).reshape([-1 if axis == dim else 1 for axis in range(array.ndim)]) for dim in (source, target)]
    chosen = jax.random.permutation(stream_key, blocks)[partner]
    strong = (owner == chosen) | (owner == (partner + blocks // 2) % blocks)
    return jnp.where(strong, factor * array, array)


def level_of(key, shape, cuts, least, top_value):
    factor_of, own = 1.0, jax.random.fold_in(key, 6)
    for position, shards_of in cuts:
        draws = jnp.exp(jax.random.uniform(jax.random.fold_in(own, position), (shards_of,), jnp.float32, least / len(cuts), top_value / len(cuts)))
        factor_of = factor_of * jnp.repeat(draws, shape[position] // shards_of).reshape([-1 if axis == position else 1 for axis in range(len(shape))])
    return factor_of


def gaussian(key, extent, width, bound, cuts=(), kind=jnp.bfloat16):
    array = jax.random.normal(key, extent, jnp.float32) * width
    if len(cuts) > 0:
        array = level_of(key, extent, cuts, -0.22, 0.18) * array
    return jnp.clip(array, min=-bound, max=bound).astype(kind)


def bell_draw_with(stream_key, shape, scale, most, split, heavy, held_as=jnp.bfloat16):
    result = scale * jax.random.normal(stream_key, shape, jnp.float32)
    if split:
        result = result * level_of(stream_key, shape, split, -0.22, 0.18)
    return jnp.clip(spiked(result, jax.random.fold_in(stream_key, 3), *heavy), -most, most).astype(held_as)


def setup_inputs(seed: int = 0) -> dict:
    seeds = jax.random.split(jax.random.key(seed), 8)
    return {
        "queries": draw_queries(jax.random.fold_in(seeds[7], 71), 0),
        "keys": draw_keys(jax.random.fold_in(seeds[7], 71), 0),
        "values": gaussian(seeds[2], (TOKENS, HEADS * HD), 1.0, 6.0, ((0, 8), (1, 4))),
        "cluster_of": draw_cluster_of(jax.random.fold_in(seeds[7], 71), 0),
        "slot_of": draw_slot_of(jax.random.fold_in(seeds[7], 71), 0),
        "centroids": gaussian(seeds[5], (HEADS, CLUSTERS, HD), 1.0, 6.0, ((0, 4), (1, 8)), jnp.float32),
        "out_weight": bell_draw_with(seeds[6], (HEADS * HD, D), (HEADS * HD) ** -0.5, 0.125, ((0, 4),), (0, 1, 4, 2.0)),
    }


mix_rate = 0.5
neg_fill = -1e+30

def attend(q_rows, k_rows, v_rows, positions):
    scale = 1.0 / math.sqrt(q_rows.shape[-1])
    scores = jnp.einsum('gqd,gkd->gqk', q_rows.astype(jnp.float32), k_rows.astype(jnp.float32)) * scale
    allowed = (positions[:, None, :] >= 0) & (positions[:, None, :] <= positions[:, :, None])
    scores = jnp.where(allowed, scores, neg_fill)
    top = lax.optimization_barrier(jnp.max(scores, axis=2, keepdims=True))
    weights = jnp.where(allowed, jnp.exp(scores - top), 0.0).astype(jnp.bfloat16)
    total = lax.optimization_barrier(jnp.sum(weights.astype(jnp.float32), axis=2, keepdims=True))
    mixed = jnp.einsum('gqk,gkd->gqd', weights.astype(jnp.float32), v_rows.astype(jnp.float32))
    return (mixed / jnp.where(total > 0.0, total, 1.0)).astype(jnp.bfloat16)

def reference(queries, keys, values, cluster_of, slot_of, centroids, out_weight):
    tokens_all = jnp.arange(TOKENS, dtype=jnp.int32)

    def one_head(head):
        cluster = cluster_of[head]
        where_in = tokens_all // TOK_DEV * SLOTS + slot_of[head]
        index = jnp.full((CLUSTERS, CAP), -1, jnp.int32).at[cluster, where_in].set(tokens_all)
        safe = jnp.maximum(index, 0)
        start = (head * HD).astype(jnp.int32)
        q_head = lax.dynamic_slice_in_dim(queries, start, HD, 1)
        k_head = lax.dynamic_slice_in_dim(keys, start, HD, 1)
        v_head = lax.dynamic_slice_in_dim(values, start, HD, 1)
        live = (index >= 0)[:, :, None]
        q_rows = jnp.where(live, q_head[safe], jnp.zeros((), jnp.bfloat16))
        k_rows = jnp.where(live, k_head[safe], jnp.zeros((), jnp.bfloat16))
        v_rows = jnp.where(live, v_head[safe], jnp.zeros((), jnp.bfloat16))
        mixed = attend(q_rows, k_rows, v_rows, index)
        attended_head = mixed[cluster, where_in]
        both = q_head.astype(jnp.float32) + k_head.astype(jnp.float32)
        sums = jax.ops.segment_sum(both, cluster, num_segments=CLUSTERS)
        counts = jax.ops.segment_sum(jnp.ones((TOKENS,), jnp.float32), cluster, num_segments=CLUSTERS)
        return (attended_head, sums, counts)
    pieces, sums, counts = lax.map(one_head, jnp.arange(HEADS, dtype=jnp.int32))
    attended = jnp.transpose(pieces, (1, 0, 2)).reshape(TOKENS, HEADS * HD)
    projected = jnp.dot(attended, out_weight, preferred_element_type=jnp.float32).astype(jnp.bfloat16)
    means = sums / (2.0 * jnp.maximum(counts, 1.0))[:, :, None]
    new_centroids = mix_rate * centroids + (1.0 - mix_rate) * means
    return (projected, new_centroids)
```

```python
import math

import jax
import jax.numpy as jnp
from jax import lax
from jax.experimental import pallas as pl
from jax.experimental.pallas import tpu as pltpu
from jax.sharding import PartitionSpec as P

CLUSTERS = 256
SLOTS = 8


mix_rate = 0.5
neg_fill = -1e30


def attend(q_rows, k_rows, v_rows, positions):
    scale = 1.0 / math.sqrt(q_rows.shape[-1])
    scores = jnp.einsum("gqd,gkd->gqk", q_rows, k_rows, preferred_element_type=jnp.float32) * scale
    allowed = (positions[:, None, :] >= 0) & (positions[:, None, :] <= positions[:, :, None])
    scores = jnp.where(allowed, scores, neg_fill)
    top = jnp.max(scores, axis=2, keepdims=True)
    weights = jnp.where(allowed, jnp.exp(scores - top), 0.0).astype(jnp.bfloat16)
    total = jnp.sum(weights.astype(jnp.float32), axis=2, keepdims=True)
    mixed = jnp.einsum("gqk,gkd->gqd", weights, v_rows, preferred_element_type=jnp.float32)
    return (mixed / jnp.where(total > 0.0, total, 1.0)).astype(jnp.bfloat16)


def to_clusters(rows, cl_dev):
    senders, width, items = (rows.shape[0], rows.shape[1], rows.shape[2])
    slots = width // cl_dev
    shaped = rows.reshape((senders, cl_dev, slots, items) + rows.shape[3:])
    if rows.ndim == 4:
        order = (3, 1, 0, 2, 4)
    else:
        order = (3, 1, 0, 2)
    return jnp.transpose(shaped, order).reshape((items * cl_dev, senders * slots) + rows.shape[3:])


def from_clusters(mixed, senders, cl_dev, items):
    slots = mixed.shape[1] // senders
    shaped = mixed.reshape(items, cl_dev, senders, slots, mixed.shape[2])
    return jnp.transpose(shaped, (2, 1, 3, 0, 4)).reshape(
        senders, cl_dev * slots, items, mixed.shape[2]
    )


def owner_work(incoming, cl_dev):
    q_in, k_in, v_in, p_in = incoming
    senders, items = (q_in.shape[0], q_in.shape[2])
    q_rows = to_clusters(q_in, cl_dev)
    k_rows = to_clusters(k_in, cl_dev)
    v_rows = to_clusters(v_in, cl_dev)
    p_rows = to_clusters(p_in, cl_dev)
    mixed = attend(q_rows, k_rows, v_rows, p_rows)
    back = from_clusters(mixed, senders, cl_dev, items)
    return back


def body(queries, keys, values, cluster_of, slot_of, centroids, out_weight):
    ranks = lax.axis_size("ctx")
    rank_here = lax.axis_index("ctx")
    tok_rows = queries.shape[0]
    head_rows = cluster_of.shape[0]
    head_size = queries.shape[1] // head_rows
    cl_dev = CLUSTERS // ranks
    width = CLUSTERS * SLOTS
    target = jnp.transpose(cluster_of * SLOTS + slot_of)
    head_ids = jnp.broadcast_to(jnp.arange(head_rows, dtype=jnp.int32)[None, :], target.shape)

    def place(rows):
        shaped = rows.reshape(tok_rows, head_rows, head_size)
        filled = (
            jnp.zeros((width, head_rows, head_size), rows.dtype).at[target, head_ids].set(shaped)
        )
        return filled.reshape(ranks, width // ranks, head_rows, head_size)

    token_pos = rank_here * tok_rows + jnp.arange(tok_rows, dtype=jnp.int32)
    pos_slots = (
        jnp.full((width, head_rows), -1, jnp.int32)
        .at[target, head_ids]
        .set(jnp.broadcast_to(token_pos[:, None], target.shape))
    )
    pos_slots = pos_slots.reshape(ranks, width // ranks, head_rows)
    incoming = (
        lax.all_to_all(place(queries), "ctx", split_axis=0, concat_axis=0, tiled=True),
        lax.all_to_all(place(keys), "ctx", split_axis=0, concat_axis=0, tiled=True),
        lax.all_to_all(place(values), "ctx", split_axis=0, concat_axis=0, tiled=True),
        lax.all_to_all(pos_slots, "ctx", split_axis=0, concat_axis=0, tiled=True),
    )
    worked = owner_work(incoming, cl_dev)
    returned = lax.all_to_all(worked, "ctx", split_axis=0, concat_axis=0, tiled=True)
    rows_back = returned.reshape(width, head_rows, head_size)
    attended = rows_back[target, head_ids].reshape(tok_rows, head_rows * head_size)
    member = (
        cluster_of[:, :, None] == jnp.arange(CLUSTERS, dtype=jnp.int32)[None, None, :]
    ).astype(jnp.bfloat16)
    q_three = queries.reshape(tok_rows, head_rows, head_size)
    k_three = keys.reshape(tok_rows, head_rows, head_size)
    local_sums = jnp.einsum("htc,thd->hcd", member, q_three, preferred_element_type=jnp.float32)
    local_sums = local_sums + jnp.einsum(
        "htc,thd->hcd", member, k_three, preferred_element_type=jnp.float32
    )
    local_counts = jnp.sum(member, axis=1, dtype=jnp.float32)
    totals, counts = (
        lax.psum_scatter(
            local_sums.astype(jnp.bfloat16), "ctx", scatter_dimension=1, tiled=True
        ).astype(jnp.float32),
        lax.psum_scatter(
            local_counts.astype(jnp.bfloat16), "ctx", scatter_dimension=1, tiled=True
        ).astype(jnp.float32),
    )
    means = totals / (2.0 * jnp.maximum(counts, 1.0))[:, :, None]
    new_centroids = mix_rate * centroids + (1.0 - mix_rate) * means
    summed = lax.psum_scatter(
        lax.dot_general(
            out_weight, attended, (((0,), (1,)), ((), ())), preferred_element_type=jnp.float32
        ),
        "head",
        scatter_dimension=0,
        tiled=True,
    )
    projected = jnp.transpose(summed).astype(jnp.bfloat16)
    return (projected, new_centroids)


BF16 = jnp.bfloat16
F32 = jnp.float32
GROUP = 4


def params(limit):
    return pltpu.CompilerParams(
        dimension_semantics=("arbitrary",), vmem_limit_bytes=limit * 1024 * 1024
    )


def pick_rows(first, count, target):
    rows = first + lax.broadcasted_iota(jnp.int32, (count, target.shape[1]), 0)
    return (rows == target).astype(BF16)


def place_pair_kernel(target_ref, q_ref, k_ref, q_out, k_out, p_out, right):
    tokens = q_ref.shape[1]
    slots = q_out.shape[0] * SLOTS
    step = 512
    right[:, :128] = q_ref[0]
    right[:, 128:256] = k_ref[0]
    token = lax.broadcasted_iota(jnp.int32, (tokens, 128), 0)
    lane = lax.broadcasted_iota(jnp.int32, (tokens, 128), 1)
    high, low = (token // 32) * 32, token % 32 + 1
    right[:, 256:] = jnp.where(lane < 64, high, low).astype(F32).astype(BF16)
    base = (pl.program_id(0) * tokens).astype(F32)
    target = target_ref[0]

    def move(i, carry):
        picked = pick_rows(i * step, step, target)
        out = jnp.dot(picked, right[...], preferred_element_type=F32)
        where = pl.ds(i * (step // SLOTS), step // SLOTS)
        q_out[where] = out[:, :128].reshape(step // SLOTS, SLOTS, 128).astype(BF16)
        k_out[where] = out[:, 128:256].reshape(step // SLOTS, SLOTS, 128).astype(BF16)
        at = out[:, 256:]
        at = at + pltpu.roll(at, 64, 1)
        at = jnp.where(at > 0.0, at + base, 0.0)
        p_out[where] = at.reshape(step // SLOTS, SLOTS, 128)
        return carry

    lax.fori_loop(0, slots // step, move, 0)


def place_pair(target, pair, tokens):
    ranks = pair.shape[0]
    spec_out = pl.BlockSpec((CLUSTERS, SLOTS, 128), lambda j: (0, j, 0))
    shape = (CLUSTERS, ranks * SLOTS, 128)
    return pl.pallas_call(
        place_pair_kernel,
        grid=(ranks,),
        in_specs=[
            pl.BlockSpec((1, 1, tokens), lambda j: (j, 0, 0)),
            pl.BlockSpec((1, tokens, 128), lambda j: (j, 0, 0)),
            pl.BlockSpec((1, tokens, 128), lambda j: (j, 1, 0)),
        ],
        out_specs=[spec_out, spec_out, spec_out],
        out_shape=[
            jax.ShapeDtypeStruct(shape, BF16),
            jax.ShapeDtypeStruct(shape, BF16),
            jax.ShapeDtypeStruct(shape, F32),
        ],
        scratch_shapes=[pltpu.VMEM((tokens, 384), BF16)],
        compiler_params=params(40),
        cost_estimate=pl.CostEstimate(
            flops=2 * ranks * CLUSTERS * SLOTS * tokens * 512,
            bytes_accessed=16 * 1024 * 1024,
            transcendentals=0,
        ),
    )(target, pair, pair)


def place_one_kernel(target_ref, v_ref, v_out):
    slots = v_out.shape[0] * SLOTS
    step = 512
    target = target_ref[0]

    def move(i, carry):
        picked = pick_rows(i * step, step, target)
        out = jnp.dot(picked, v_ref[0], preferred_element_type=F32)
        where = pl.ds(i * (step // SLOTS), step // SLOTS)
        v_out[where] = out.reshape(step // SLOTS, SLOTS, 128).astype(BF16)
        return carry

    lax.fori_loop(0, slots // step, move, 0)


def place_one(target, rows, tokens):
    ranks = rows.shape[0]
    return pl.pallas_call(
        place_one_kernel,
        grid=(ranks,),
        in_specs=[
            pl.BlockSpec((1, 1, tokens), lambda j: (j, 0, 0)),
            pl.BlockSpec((1, tokens, 128), lambda j: (j, 0, 0)),
        ],
        out_specs=pl.BlockSpec((CLUSTERS, SLOTS, 128), lambda j: (0, j, 0)),
        out_shape=jax.ShapeDtypeStruct((CLUSTERS, ranks * SLOTS, 128), BF16),
        compiler_params=params(40),
        cost_estimate=pl.CostEstimate(
            flops=2 * ranks * CLUSTERS * SLOTS * tokens * 256,
            bytes_accessed=6 * 1024 * 1024,
            transcendentals=0,
        ),
    )(target, rows)


def weigh_kernel(q_ref, k_ref, p_ref, w_out, mean_out):
    rows = q_ref.shape[1]
    cap = rows // GROUP
    scale = 1.0 / math.sqrt(q_ref.shape[2])
    for n in range(q_ref.shape[0]):
        q, k, at = q_ref[n], k_ref[n], p_ref[n]
        scores = lax.dot_general(q, k, (((1,), (1,)), ((), ())), preferred_element_type=F32) * scale
        own = jnp.tile(at, (1, rows // 128))
        other = jnp.broadcast_to(jnp.transpose(at)[0:1, :], (rows, rows))
        same = (
            lax.broadcasted_iota(jnp.int32, (rows, rows), 0) // cap
            == lax.broadcasted_iota(jnp.int32, (rows, rows), 1) // cap
        )
        allowed = same & (other > 0.0) & (other <= own)
        scores = jnp.where(allowed, scores, neg_fill)
        top = jnp.max(scores, axis=1, keepdims=True)
        w_out[n] = jnp.where(allowed, jnp.exp(scores - top), 0.0).astype(BF16)
        both = q.astype(F32) + k.astype(F32)
        sums = jnp.sum(both.reshape(GROUP, cap, 128), axis=1)
        counts = jnp.sum((at > 0.0).astype(F32).reshape(GROUP, cap, 128), axis=1)
        mean_out[n] = sums / (2.0 * jnp.maximum(counts, 1.0))


def weigh(q_rows, k_rows, at):
    groups, rows = q_rows.shape[0], q_rows.shape[1]
    step = 4
    spec = pl.BlockSpec((step, rows, 128), lambda i: (i, 0, 0))
    return pl.pallas_call(
        weigh_kernel,
        grid=(groups // step,),
        in_specs=[spec, spec, spec],
        out_specs=[
            pl.BlockSpec((step, rows, rows), lambda i: (i, 0, 0)),
            pl.BlockSpec((step, GROUP, 128), lambda i: (i, 0, 0)),
        ],
        out_shape=[
            jax.ShapeDtypeStruct((groups, rows, rows), BF16),
            jax.ShapeDtypeStruct((groups, GROUP, 128), F32),
        ],
        compiler_params=params(40),
        cost_estimate=pl.CostEstimate(
            flops=2 * groups * rows * rows * 256,
            bytes_accessed=24 * 1024 * 1024,
            transcendentals=groups * rows * rows,
        ),
    )(q_rows, k_rows, at)


def mix_kernel(w_ref, v_ref, o_out):
    rows = v_ref.shape[1]
    ones = jnp.ones((rows, 128), BF16)
    for n in range(v_ref.shape[0]):
        right = jnp.concatenate([v_ref[n], ones], axis=1)
        out = jnp.dot(w_ref[n], right, preferred_element_type=F32)
        total = out[:, 128:]
        o_out[n] = (out[:, :128] / jnp.where(total > 0.0, total, 1.0)).astype(BF16)


def mix(weights, v_rows):
    groups, rows = v_rows.shape[0], v_rows.shape[1]
    step = 8
    return pl.pallas_call(
        mix_kernel,
        grid=(groups // step,),
        in_specs=[
            pl.BlockSpec((step, rows, rows), lambda i: (i, 0, 0)),
            pl.BlockSpec((step, rows, 128), lambda i: (i, 0, 0)),
        ],
        out_specs=pl.BlockSpec((step, rows, 128), lambda i: (i, 0, 0)),
        out_shape=jax.ShapeDtypeStruct((groups, rows, 128), BF16),
        compiler_params=params(40),
        cost_estimate=pl.CostEstimate(
            flops=2 * groups * rows * rows * 256,
            bytes_accessed=16 * 1024 * 1024,
            transcendentals=0,
        ),
    )(weights, v_rows)


def unplace_kernel(target_ref, o_ref, mean_ref, out_ref, right):
    tokens = target_ref.shape[1]
    slots = o_ref.shape[0] * SLOTS
    step = 256
    right[...] = o_ref[...].astype(F32).reshape(slots, 128).astype(BF16)

    def move(i, carry):
        target = target_ref[0, pl.ds(i * step, step), :]
        columns = lax.broadcasted_iota(jnp.int32, (step, slots), 1)
        picked = (columns == target).astype(BF16)
        out = jnp.dot(picked, right[...], preferred_element_type=F32)
        out_ref[0, pl.ds(i * step, step), :] = out.astype(BF16)
        return carry

    lax.fori_loop(0, tokens // step, move, 0)
    means = mean_ref[0]
    high = means.astype(BF16)
    count = means.shape[0]
    out_ref[0, tokens : tokens + count, :] = high
    out_ref[0, tokens + count :, :] = (means - high.astype(F32)).astype(BF16)


def unplace(target, mixed, means):
    ranks, tokens = target.shape[0], target.shape[1]
    extra = 2 * means.shape[1]
    return pl.pallas_call(
        unplace_kernel,
        grid=(ranks,),
        in_specs=[
            pl.BlockSpec((1, tokens, 1), lambda j: (j, 0, 0)),
            pl.BlockSpec((CLUSTERS, SLOTS, 128), lambda j: (0, j, 0)),
            pl.BlockSpec((1, means.shape[1], 128), lambda j: (j, 0, 0)),
        ],
        out_specs=pl.BlockSpec((1, tokens + extra, 128), lambda j: (j, 0, 0)),
        out_shape=jax.ShapeDtypeStruct((ranks, tokens + extra, 128), BF16),
        scratch_shapes=[pltpu.VMEM((CLUSTERS * SLOTS, 128), BF16)],
        compiler_params=params(40),
        cost_estimate=pl.CostEstimate(
            flops=2 * ranks * CLUSTERS * SLOTS * tokens * 256,
            bytes_accessed=6 * 1024 * 1024,
            transcendentals=0,
        ),
    )(target, mixed, means)


def head_body(queries, keys, values, cluster_of, slot_of, centroids, out_weight):
    ranks = lax.axis_size("ctx")
    me = lax.axis_index("ctx")
    mine = lax.axis_index("head")
    tokens = queries.shape[0]
    cl_dev = CLUSTERS // ranks
    cap = ranks * SLOTS

    def swap_y(x):
        return lax.ppermute(x, "head", [(0, 2), (1, 3), (2, 0), (3, 1)])

    def swap_core(x):
        return lax.ppermute(x, "head", [(0, 1), (1, 0), (2, 3), (3, 2)])

    def by_head(x):
        return jnp.transpose(x.reshape(tokens, ranks, 128), (1, 0, 2))

    marks = [x.astype(BF16).reshape(ranks, tokens // 128, 128) for x in (cluster_of, slot_of)]
    pair = jnp.concatenate([by_head(queries), by_head(keys)] + marks, axis=1)
    pair = lax.all_to_all(pair, "ctx", split_axis=0, concat_axis=0, tiled=True)
    rows_v = lax.all_to_all(by_head(values), "ctx", split_axis=0, concat_axis=0, tiled=True)

    lanes = tuple(range(ranks))
    own_w = jnp.concatenate(
        [lax.dynamic_slice_in_dim(out_weight, (me ^ d) * 128, 128, 0) for d in lanes], axis=0
    )
    cols = out_weight.shape[1] // 4
    half = 2 * cols
    y, core = mine // 2, mine % 2
    keep = lax.dynamic_slice_in_dim(own_w, y * half, half, 1)
    across = swap_y(lax.dynamic_slice_in_dim(own_w, (1 - y) * half, half, 1))
    w_parts = [lax.dynamic_slice_in_dim(w, core * cols, cols, 1) for w in (keep, across)]
    w_parts += [
        swap_core(lax.dynamic_slice_in_dim(w, (1 - core) * cols, cols, 1)) for w in (keep, across)
    ]

    marks = pair[:, 2 * tokens :, :].astype(jnp.int32)
    target = marks[:, : tokens // 128, :] * SLOTS + marks[:, tokens // 128 :, :]
    target_row = target.reshape(ranks, 1, tokens)
    target_col = target.reshape(ranks, tokens, 1)
    q_rows, k_rows, at = place_pair(target_row, pair, tokens)

    def grouped(x):
        return x.reshape(CLUSTERS // GROUP, GROUP * cap, 128)

    weights, means = weigh(grouped(q_rows), grouped(k_rows), grouped(at))
    v_rows = place_one(target_row, rows_v, tokens)
    mixed = mix(weights, grouped(v_rows)).reshape(CLUSTERS, cap, 128)
    back = unplace(target_col, mixed, means.reshape(ranks, cl_dev, 128))

    got = {0: lax.dynamic_index_in_dim(back, me, 0, False)}
    for d in (1, 2, 3, 4, 5, 6, 7):
        block = lax.dynamic_index_in_dim(back, me ^ d, 0, False)
        got[d] = lax.ppermute(block, "ctx", [(i, i ^ d) for i in range(ranks)])

    total = 0.0
    for some in ((0, 1, 2, 3), (4, 5), (6, 7)):
        part = jnp.concatenate([got[d][:tokens] for d in some], axis=1)
        there = swap_y(part)
        parts = [part, there, swap_core(part), swap_core(there)]
        left = jnp.concatenate(parts, axis=1)
        first = some[0] * 128
        right = jnp.concatenate([w[first : first + 128 * len(some)] for w in w_parts], axis=0)
        total = total + jnp.dot(left, right, preferred_element_type=F32)
    projected = total.astype(BF16)

    sent = jnp.stack([got[d][tokens:] for d in lanes]).astype(F32)
    sent = sent[:, :cl_dev] + sent[:, cl_dev:]
    sent = jnp.concatenate(
        [lax.dynamic_slice_in_dim(sent, me ^ d, 1, 0) for d in lanes], axis=0
    )
    new_centroids = mix_rate * centroids + (1.0 - mix_rate) * sent
    return (projected, new_centroids)


def solution(mesh):
    in_specs = (
        P("ctx", "head"),
        P("ctx", "head"),
        P("ctx", "head"),
        P("head", "ctx"),
        P("head", "ctx"),
        P("head", "ctx", None),
        P("head", None),
    )
    out_specs = (P("ctx", "head"), P("head", "ctx", None))
    ranks, heads_here = mesh.shape["ctx"], 32 // mesh.shape["head"]
    whole_heads = ranks == heads_here and ranks & (ranks - 1) == 0 and mesh.shape["head"] == 4
    return jax.shard_map(
        head_body if whole_heads else body,
        mesh=mesh,
        in_specs=in_specs,
        out_specs=out_specs,
        check_vma=False,
    )
```

```python
import functools
import math

import jax
import jax.numpy as jnp
from jax import lax
from jax.experimental import pallas as pl
from jax.experimental.pallas import tpu as pltpu
from jax.sharding import PartitionSpec as P

CLUSTERS = 256
SLOTS = 8


mix_rate = 0.5
neg_fill = -1e30


def attend(q_rows, k_rows, v_rows, positions):
    scale = 1.0 / math.sqrt(q_rows.shape[-1])
    scores = jnp.einsum("gqd,gkd->gqk", q_rows, k_rows, preferred_element_type=jnp.float32) * scale
    allowed = (positions[:, None, :] >= 0) & (positions[:, None, :] <= positions[:, :, None])
    scores = jnp.where(allowed, scores, neg_fill)
    top = jnp.max(scores, axis=2, keepdims=True)
    weights = jnp.where(allowed, jnp.exp(scores - top), 0.0).astype(jnp.bfloat16)
    total = jnp.sum(weights.astype(jnp.float32), axis=2, keepdims=True)
    mixed = jnp.einsum("gqk,gkd->gqd", weights, v_rows, preferred_element_type=jnp.float32)
    return (mixed / jnp.where(total > 0.0, total, 1.0)).astype(jnp.bfloat16)


def to_clusters(rows, cl_dev):
    senders, width, items = (rows.shape[0], rows.shape[1], rows.shape[2])
    slots = width // cl_dev
    shaped = rows.reshape((senders, cl_dev, slots, items) + rows.shape[3:])
    if rows.ndim == 4:
        order = (3, 1, 0, 2, 4)
    else:
        order = (3, 1, 0, 2)
    return jnp.transpose(shaped, order).reshape((items * cl_dev, senders * slots) + rows.shape[3:])


def from_clusters(mixed, senders, cl_dev, items):
    slots = mixed.shape[1] // senders
    shaped = mixed.reshape(items, cl_dev, senders, slots, mixed.shape[2])
    return jnp.transpose(shaped, (2, 1, 3, 0, 4)).reshape(
        senders, cl_dev * slots, items, mixed.shape[2]
    )


def owner_work(incoming, cl_dev):
    q_in, k_in, v_in, p_in = incoming
    senders, items = (q_in.shape[0], q_in.shape[2])
    q_rows = to_clusters(q_in, cl_dev)
    k_rows = to_clusters(k_in, cl_dev)
    v_rows = to_clusters(v_in, cl_dev)
    p_rows = to_clusters(p_in, cl_dev)
    mixed = attend(q_rows, k_rows, v_rows, p_rows)
    back = from_clusters(mixed, senders, cl_dev, items)
    return back


def body(queries, keys, values, cluster_of, slot_of, centroids, out_weight):
    ranks = lax.axis_size("ctx")
    rank_here = lax.axis_index("ctx")
    tok_rows = queries.shape[0]
    head_rows = cluster_of.shape[0]
    head_size = queries.shape[1] // head_rows
    cl_dev = CLUSTERS // ranks
    width = CLUSTERS * SLOTS
    target = jnp.transpose(cluster_of * SLOTS + slot_of)
    head_ids = jnp.broadcast_to(jnp.arange(head_rows, dtype=jnp.int32)[None, :], target.shape)

    def place(rows):
        shaped = rows.reshape(tok_rows, head_rows, head_size)
        filled = (
            jnp.zeros((width, head_rows, head_size), rows.dtype).at[target, head_ids].set(shaped)
        )
        return filled.reshape(ranks, width // ranks, head_rows, head_size)

    token_pos = rank_here * tok_rows + jnp.arange(tok_rows, dtype=jnp.int32)
    pos_slots = (
        jnp.full((width, head_rows), -1, jnp.int32)
        .at[target, head_ids]
        .set(jnp.broadcast_to(token_pos[:, None], target.shape))
    )
    pos_slots = pos_slots.reshape(ranks, width // ranks, head_rows)
    incoming = (
        lax.all_to_all(place(queries), "ctx", split_axis=0, concat_axis=0, tiled=True),
        lax.all_to_all(place(keys), "ctx", split_axis=0, concat_axis=0, tiled=True),
        lax.all_to_all(place(values), "ctx", split_axis=0, concat_axis=0, tiled=True),
        lax.all_to_all(pos_slots, "ctx", split_axis=0, concat_axis=0, tiled=True),
    )
    worked = owner_work(incoming, cl_dev)
    returned = lax.all_to_all(worked, "ctx", split_axis=0, concat_axis=0, tiled=True)
    rows_back = returned.reshape(width, head_rows, head_size)
    attended = rows_back[target, head_ids].reshape(tok_rows, head_rows * head_size)
    member = (
        cluster_of[:, :, None] == jnp.arange(CLUSTERS, dtype=jnp.int32)[None, None, :]
    ).astype(jnp.bfloat16)
    q_three = queries.reshape(tok_rows, head_rows, head_size)
    k_three = keys.reshape(tok_rows, head_rows, head_size)
    local_sums = jnp.einsum("htc,thd->hcd", member, q_three, preferred_element_type=jnp.float32)
    local_sums = local_sums + jnp.einsum(
        "htc,thd->hcd", member, k_three, preferred_element_type=jnp.float32
    )
    local_counts = jnp.sum(member, axis=1, dtype=jnp.float32)
    totals, counts = (
        lax.psum_scatter(
            local_sums.astype(jnp.bfloat16), "ctx", scatter_dimension=1, tiled=True
        ).astype(jnp.float32),
        lax.psum_scatter(
            local_counts.astype(jnp.bfloat16), "ctx", scatter_dimension=1, tiled=True
        ).astype(jnp.float32),
    )
    means = totals / (2.0 * jnp.maximum(counts, 1.0))[:, :, None]
    new_centroids = mix_rate * centroids + (1.0 - mix_rate) * means
    summed = lax.psum_scatter(
        lax.dot_general(
            out_weight, attended, (((0,), (1,)), ((), ())), preferred_element_type=jnp.float32
        ),
        "head",
        scatter_dimension=0,
        tiled=True,
    )
    projected = jnp.transpose(summed).astype(jnp.bfloat16)
    return (projected, new_centroids)


BF16 = jnp.bfloat16
F32 = jnp.float32
PAIR = 2
EMPTY = 1e9


def params(limit):
    return pltpu.CompilerParams(
        dimension_semantics=("arbitrary",), vmem_limit_bytes=limit * 1024 * 1024
    )


def cost(flops, nbytes, transcendentals=0):
    return pl.CostEstimate(
        flops=flops, bytes_accessed=nbytes, transcendentals=transcendentals
    )


def pack_first_kernel(q_ref, k_ref, v_ref, marks_ref, out_ref):
    tokens, some = q_ref.shape[0], v_ref.shape[0]
    out_ref[0, :tokens] = q_ref[...]
    out_ref[0, tokens : 2 * tokens] = k_ref[...]
    out_ref[0, 2 * tokens : 2 * tokens + some] = v_ref[...]
    out_ref[0, 2 * tokens + some :] = marks_ref[0]


def pack_first(queries, keys, values, marks, some):
    tokens, heads = queries.shape[0], marks.shape[0]
    rows = 2 * tokens + some + marks.shape[1]
    whole = pl.BlockSpec((tokens, 128), lambda j: (0, j))
    return pl.pallas_call(
        pack_first_kernel,
        grid=(heads,),
        in_specs=[
            whole,
            whole,
            pl.BlockSpec((some, 128), lambda j: (0, j)),
            pl.BlockSpec((1, marks.shape[1], 128), lambda j: (j, 0, 0)),
        ],
        out_specs=pl.BlockSpec((1, rows, 128), lambda j: (j, 0, 0)),
        out_shape=jax.ShapeDtypeStruct((heads, rows, 128), BF16),
        compiler_params=params(60),
        cost_estimate=cost(0, 2 * heads * rows * 256),
    )(queries, keys, values, marks)


def pack_rest_kernel(v_ref, out_ref):
    out_ref[0] = v_ref[...]


def pack_rest(values, heads, some):
    rest = values.shape[0] - some
    return pl.pallas_call(
        pack_rest_kernel,
        grid=(heads,),
        in_specs=[pl.BlockSpec((rest, 128), lambda j: (1, j))],
        out_specs=pl.BlockSpec((1, rest, 128), lambda j: (j, 0, 0)),
        out_shape=jax.ShapeDtypeStruct((heads, rest, 128), BF16),
        compiler_params=params(60),
        cost_estimate=cost(0, 2 * heads * rest * 256),
    )(values)


def match(first, count, target):
    rows = first + lax.broadcasted_iota(jnp.int32, (count, target.shape[1]), 0)
    return rows == target


def by_slot(x):
    return x.reshape(x.shape[0] // SLOTS, SLOTS, 128)


def place_pair_kernel(target_ref, q_ref, k_ref, q_out, k_out, p_out, right):
    tokens = q_ref.shape[1]
    slots = q_out.shape[0] * SLOTS
    step = 1024
    right[:, :128] = q_ref[0]
    right[:, 128:] = k_ref[0]
    base = pl.program_id(0) * tokens
    token = (base + lax.broadcasted_iota(jnp.int32, (1, tokens), 1)).astype(F32)
    target = target_ref[0]

    def move(i, carry):
        picked = match(i * step, step, target)
        out = jnp.dot(picked.astype(BF16), right[...], preferred_element_type=F32)
        where = pl.ds(i * (step // SLOTS), step // SLOTS)
        q_out[where] = by_slot(out[:, :128]).astype(BF16)
        k_out[where] = by_slot(out[:, 128:]).astype(BF16)
        at = jnp.min(jnp.where(picked, token, EMPTY), axis=1, keepdims=True)
        p_out[where] = by_slot(jnp.broadcast_to(at, (step, 128)))
        return carry

    lax.fori_loop(0, slots // step, move, 0)


def place_pair(target, first, tokens):
    ranks = first.shape[0]
    spec_out = pl.BlockSpec((CLUSTERS, SLOTS, 128), lambda j: (0, j, 0))
    shape = (CLUSTERS, ranks * SLOTS, 128)
    return pl.pallas_call(
        place_pair_kernel,
        grid=(ranks,),
        in_specs=[
            pl.BlockSpec((1, 1, tokens), lambda j: (j, 0, 0)),
            pl.BlockSpec((1, tokens, 128), lambda j: (j, 0, 0)),
            pl.BlockSpec((1, tokens, 128), lambda j: (j, 1, 0)),
        ],
        out_specs=[spec_out, spec_out, spec_out],
        out_shape=[
            jax.ShapeDtypeStruct(shape, BF16),
            jax.ShapeDtypeStruct(shape, BF16),
            jax.ShapeDtypeStruct(shape, F32),
        ],
        scratch_shapes=[pltpu.VMEM((tokens, 256), BF16)],
        compiler_params=params(60),
        cost_estimate=cost(2 * ranks * CLUSTERS * SLOTS * tokens * 256, 16 << 20),
    )(target, first, first)


def place_some_kernel(target_ref, v_ref, v_out):
    slots = v_out.shape[0] * SLOTS
    some = v_ref.shape[1]
    picked = match(0, slots, target_ref[0, :, :some]).astype(BF16)
    out = jnp.dot(picked, v_ref[0], preferred_element_type=F32)
    v_out[...] = by_slot(out).astype(BF16)


def place_some(target, first, tokens, some):
    ranks = first.shape[0]
    block = 2 * tokens // some
    return pl.pallas_call(
        place_some_kernel,
        grid=(ranks,),
        in_specs=[
            pl.BlockSpec((1, 1, tokens), lambda j: (j, 0, 0)),
            pl.BlockSpec((1, some, 128), lambda j: (j, block, 0)),
        ],
        out_specs=pl.BlockSpec((CLUSTERS, SLOTS, 128), lambda j: (0, j, 0)),
        out_shape=jax.ShapeDtypeStruct((CLUSTERS, ranks * SLOTS, 128), BF16),
        compiler_params=params(24),
        cost_estimate=cost(2 * ranks * CLUSTERS * SLOTS * some * 256, 6 << 20),
    )(target, first)


def weigh_kernel(q_ref, k_ref, p_ref, w_out, mean_out):
    count, rows = q_ref.shape[0], q_ref.shape[1]
    cap = rows // PAIR
    scale = 1.0 / math.sqrt(q_ref.shape[2])
    same = (
        lax.broadcasted_iota(jnp.int32, (rows, rows), 0) // cap
        == lax.broadcasted_iota(jnp.int32, (rows, rows), 1) // cap
    )
    for n in range(count):
        q, k, own = q_ref[n], k_ref[n], p_ref[n]
        scores = lax.dot_general(q, k, (((1,), (1,)), ((), ())), preferred_element_type=F32) * scale
        allowed = same & (jnp.transpose(own) <= own)
        scores = jnp.where(allowed, scores, neg_fill)
        top = jnp.max(scores, axis=1, keepdims=True)
        w_out[n] = jnp.where(allowed, jnp.exp(scores - top), 0.0).astype(BF16)
    both = (q_ref[...].astype(F32) + k_ref[...].astype(F32)).reshape(count * PAIR, cap, 128)
    held = (p_ref[...] < EMPTY).astype(F32).reshape(count * PAIR, cap, 128)
    mean_out[...] = jnp.sum(both, axis=1) / (2.0 * jnp.maximum(jnp.sum(held, axis=1), 1.0))


def weigh(q_rows, k_rows, at):
    groups, rows = q_rows.shape[0], q_rows.shape[1]
    step = 8
    spec = pl.BlockSpec((step, rows, 128), lambda i: (i, 0, 0))
    return pl.pallas_call(
        weigh_kernel,
        grid=(groups // step,),
        in_specs=[spec, spec, spec],
        out_specs=[
            pl.BlockSpec((step, rows, rows), lambda i: (i, 0, 0)),
            pl.BlockSpec((step * PAIR, 128), lambda i: (i, 0)),
        ],
        out_shape=[
            jax.ShapeDtypeStruct((groups, rows, rows), BF16),
            jax.ShapeDtypeStruct((groups * PAIR, 128), F32),
        ],
        compiler_params=params(24),
        cost_estimate=cost(2 * groups * rows * rows * 256, 20 << 20, groups * rows * rows),
    )(q_rows, k_rows, at)


def mix_kernel(ranks, target_ref, v_ref, part_ref, w_ref, o_out, v_rows):
    i = pl.program_id(0)
    slots = part_ref.shape[0] * SLOTS
    count, rows = w_ref.shape[0], w_ref.shape[1]
    tokens, rest = target_ref.shape[2], v_ref.shape[1]

    @pl.when(i < ranks)
    def _():
        picked = match(0, slots, target_ref[0, :, tokens - rest :]).astype(BF16)
        out = jnp.dot(picked, v_ref[0], preferred_element_type=F32)
        where = pl.ds(pl.multiple_of(i * SLOTS, SLOTS), SLOTS)
        v_rows[:, where, :] = by_slot(out) + part_ref[...].astype(F32)

    @pl.when(i >= ranks)
    def _():
        ones = jnp.ones((rows, 128), BF16)
        for n in range(count):
            own = v_rows[pl.ds(((i - ranks) * count + n) * PAIR, PAIR)]
            right = jnp.concatenate([own.reshape(rows, 128).astype(BF16), ones], axis=1)
            out = jnp.dot(w_ref[n], right, preferred_element_type=F32)
            total = out[:, 128:]
            o_out[n] = (out[:, :128] / jnp.where(total > 0.0, total, 1.0)).astype(BF16)


def mix(target, rows_v, part, weights):
    ranks, rest = rows_v.shape[0], rows_v.shape[1]
    groups, rows = weights.shape[0], weights.shape[1]
    count = groups // ranks

    def sender(i):
        return jnp.minimum(i, ranks - 1)

    def group(i):
        return jnp.maximum(i - ranks, 0)

    return pl.pallas_call(
        functools.partial(mix_kernel, ranks),
        grid=(2 * ranks,),
        in_specs=[
            pl.BlockSpec((1, 1, target.shape[2]), lambda i: (sender(i), 0, 0)),
            pl.BlockSpec((1, rest, 128), lambda i: (sender(i), 0, 0)),
            pl.BlockSpec((CLUSTERS, SLOTS, 128), lambda i: (0, sender(i), 0)),
            pl.BlockSpec((count, rows, rows), lambda i: (group(i), 0, 0)),
        ],
        out_specs=pl.BlockSpec((count, rows, 128), lambda i: (group(i), 0, 0)),
        out_shape=jax.ShapeDtypeStruct((groups, rows, 128), BF16),
        scratch_shapes=[pltpu.VMEM((CLUSTERS, ranks * SLOTS, 128), F32)],
        compiler_params=params(24),
        cost_estimate=cost(2 * ranks * CLUSTERS * SLOTS * rest * 256, 16 << 20),
    )(target, rows_v, part, weights)


def unplace_kernel(who_ref, target_ref, o_ref, mean_ref, out_ref):
    tokens = target_ref.shape[2]
    slots = o_ref.shape[0] * SLOTS
    right = o_ref[...].astype(F32).reshape(slots, 128).astype(BF16)
    target = jnp.transpose(jnp.broadcast_to(target_ref[0], (128, tokens)))
    columns = lax.broadcasted_iota(jnp.int32, (tokens, slots), 1)
    picked = (columns == jnp.tile(target, (1, slots // 128))).astype(BF16)
    out_ref[:tokens] = jnp.dot(picked, right, preferred_element_type=F32).astype(BF16)
    means = mean_ref[...]
    high = means.astype(BF16)
    count = means.shape[0]
    out_ref[tokens : tokens + count] = high
    out_ref[tokens + count :] = (means - high.astype(F32)).astype(BF16)


def unplace(who, target, mixed, means):
    tokens = target.shape[2]
    count = CLUSTERS // target.shape[0]
    return pl.pallas_call(
        unplace_kernel,
        grid_spec=pltpu.PrefetchScalarGridSpec(
            num_scalar_prefetch=1,
            grid=(1,),
            in_specs=[
                pl.BlockSpec((1, 1, tokens), lambda i, who: (who[0], 0, 0)),
                pl.BlockSpec((CLUSTERS, SLOTS, 128), lambda i, who: (0, who[0], 0)),
                pl.BlockSpec((count, 128), lambda i, who: (who[0], 0)),
            ],
            out_specs=pl.BlockSpec((tokens + 2 * count, 128), lambda i, who: (0, 0)),
        ),
        out_shape=jax.ShapeDtypeStruct((tokens + 2 * count, 128), BF16),
        compiler_params=params(24),
        cost_estimate=cost(1, 1),
    )(who, target, mixed, means)


def project_kernel(lanes, has_total, *refs):
    refs = refs[1:]
    atts, ws = refs[:4], refs[4 : 4 + 4 * lanes]
    out_ref = refs[-1]
    left = jnp.concatenate([a[...] for a in atts], axis=1)
    right = jnp.concatenate([w[...] for w in ws], axis=0)
    total = jnp.dot(left, right, preferred_element_type=F32)
    if has_total:
        total = total + refs[4 + 4 * lanes][...]
    out_ref[...] = total.astype(out_ref.dtype)


def project(where, tokens, atts, weights, columns, total, dtype):
    lanes = atts[0].shape[1] // 128
    step = 512
    cols = out_cols = weights[3].shape[1]
    in_specs = [pl.BlockSpec((step, 128 * lanes), lambda i, w: (i, 0)) for _ in atts]
    args = list(atts)
    for part in range(4):
        for lane in range(lanes):
            in_specs.append(
                pl.BlockSpec(
                    (128, cols), lambda i, w, lane=lane, part=part: (w[lane], w[lanes + part])
                )
            )
            args.append(weights[part])
    if total is not None:
        in_specs.append(pl.BlockSpec((step, out_cols), lambda i, w: (i, 0)))
        args.append(total)
    return pl.pallas_call(
        functools.partial(project_kernel, lanes, total is not None),
        grid_spec=pltpu.PrefetchScalarGridSpec(
            num_scalar_prefetch=1,
            grid=(tokens // step,),
            in_specs=in_specs,
            out_specs=pl.BlockSpec((step, out_cols), lambda i, w: (i, 0)),
        ),
        out_shape=jax.ShapeDtypeStruct((tokens, out_cols), dtype),
        compiler_params=params(60),
        cost_estimate=cost(2 * tokens * 512 * lanes * out_cols, 8 << 20),
    )(jnp.stack(list(where) + list(columns)), *args)


def head_body(queries, keys, values, cluster_of, slot_of, centroids, out_weight):
    ranks = lax.axis_size("ctx")
    me = lax.axis_index("ctx")
    mine = lax.axis_index("head")
    tokens = queries.shape[0]
    some = tokens // 2
    cl_dev = CLUSTERS // ranks
    cap = ranks * SLOTS
    y, core = mine // 2, mine % 2

    def swap_y(x):
        return lax.ppermute(x, "head", [(0, 2), (1, 3), (2, 0), (3, 1)])

    def swap_core(x):
        return lax.ppermute(x, "head", [(0, 1), (1, 0), (2, 3), (3, 2)])

    marks = [x.astype(BF16).reshape(ranks, tokens // 128, 128) for x in (cluster_of, slot_of)]
    marks = jnp.concatenate(marks, axis=1)
    first = pack_first(queries, keys, values, marks, some)
    first = lax.all_to_all(first, "ctx", split_axis=0, concat_axis=0, tiled=True)
    rows_v, first = lax.optimization_barrier((pack_rest(values, ranks, some), first))
    rows_v = lax.all_to_all(rows_v, "ctx", split_axis=0, concat_axis=0, tiled=True)

    cols = out_weight.shape[1] // 4
    across = swap_y(lax.dynamic_slice_in_dim(out_weight, (1 - y) * 2 * cols, 2 * cols, 1))
    beside = swap_core(
        lax.dynamic_slice_in_dim(out_weight, (2 * y + 1 - core) * cols, cols, 1)
    )
    corner = swap_core(lax.dynamic_slice_in_dim(across, (1 - core) * cols, cols, 1))
    w_parts = (out_weight, across, beside, corner)
    w_columns = (mine, core, jnp.zeros_like(core), jnp.zeros_like(core))

    marks = first[:, 2 * tokens + some :, :].astype(jnp.int32)
    target = marks[:, : tokens // 128, :] * SLOTS + marks[:, tokens // 128 :, :]
    target = target.reshape(ranks, 1, tokens)
    q_rows, k_rows, at = place_pair(target, first, tokens)

    def paired(x):
        return x.reshape(CLUSTERS // PAIR, PAIR * cap, 128)

    weights, means = weigh(paired(q_rows), paired(k_rows), paired(at))
    part = place_some(target, first, tokens, some)
    rows_v, w_parts = lax.optimization_barrier((rows_v, w_parts))
    mixed = mix(target, rows_v, part, weights).reshape(CLUSTERS, cap, 128)

    got = {}
    after = {6: 4, 7: 5}
    for d in (4, 5, 1, 2, 3, 0, 6, 7):
        who = jnp.reshape(me ^ d, (1,))
        if d in after:
            who, got[after[d]] = lax.optimization_barrier((who, got[after[d]]))
        block = unplace(who, target, mixed, means)
        got[d] = block
        if d:
            got[d] = lax.ppermute(block, "ctx", [(i, i ^ d) for i in range(ranks)])

    total = None
    splits = ((0, 1, 2, 3), (4, 5), (6,), (7,))
    for lanes in splits:
        own = got[lanes[0]]
        if len(lanes) > 1:
            own = jnp.concatenate([got[d][:tokens] for d in lanes], axis=1)
        there = swap_y(own)
        atts = (own, there, swap_core(own), swap_core(there))
        last = lanes == splits[-1]
        total = project(
            [me ^ d for d in lanes], tokens, atts, w_parts, w_columns, total, BF16 if last else F32
        )

    sent = jnp.stack([got[d][tokens:] for d in range(ranks)]).astype(F32)
    sent = sent[:, :cl_dev] + sent[:, cl_dev:]
    sent = jnp.concatenate(
        [lax.dynamic_slice_in_dim(sent, me ^ d, 1, 0) for d in range(ranks)], axis=0
    )
    new_centroids = mix_rate * centroids + (1.0 - mix_rate) * sent
    return (total, new_centroids)


def dispatch(queries, keys, values, cluster_of, *rest):
    ranks, heads = lax.axis_size("ctx"), cluster_of.shape[0]
    whole_heads = ranks == heads == 8 and lax.axis_size("head") == 4
    step = head_body if whole_heads else body
    return step(queries, keys, values, cluster_of, *rest)


def solution(mesh):
    in_specs = (
        P("ctx", "head"),
        P("ctx", "head"),
        P("ctx", "head"),
        P("head", "ctx"),
        P("head", "ctx"),
        P("head", "ctx", None),
        P("head", None),
    )
    out_specs = (P("ctx", "head"), P("head", "ctx", None))
    return jax.shard_map(
        dispatch, mesh=mesh, in_specs=in_specs, out_specs=out_specs, check_vma=False
    )
```

```python
import functools
import math

import jax
import jax.numpy as jnp
from jax import lax
from jax.experimental import pallas as pl
from jax.experimental.pallas import tpu as pltpu
from jax.sharding import PartitionSpec as P

CLUSTERS = 256
SLOTS = 8


mix_rate = 0.5
neg_fill = -1e30


def attend(q_rows, k_rows, v_rows, positions):
    scale = 1.0 / math.sqrt(q_rows.shape[-1])
    scores = jnp.einsum("gqd,gkd->gqk", q_rows, k_rows, preferred_element_type=jnp.float32) * scale
    allowed = (positions[:, None, :] >= 0) & (positions[:, None, :] <= positions[:, :, None])
    scores = jnp.where(allowed, scores, neg_fill)
    top = jnp.max(scores, axis=2, keepdims=True)
    weights = jnp.where(allowed, jnp.exp(scores - top), 0.0).astype(jnp.bfloat16)
    total = jnp.sum(weights.astype(jnp.float32), axis=2, keepdims=True)
    mixed = jnp.einsum("gqk,gkd->gqd", weights, v_rows, preferred_element_type=jnp.float32)
    return (mixed / jnp.where(total > 0.0, total, 1.0)).astype(jnp.bfloat16)


def to_clusters(rows, cl_dev):
    senders, width, items = (rows.shape[0], rows.shape[1], rows.shape[2])
    slots = width // cl_dev
    shaped = rows.reshape((senders, cl_dev, slots, items) + rows.shape[3:])
    if rows.ndim == 4:
        order = (3, 1, 0, 2, 4)
    else:
        order = (3, 1, 0, 2)
    return jnp.transpose(shaped, order).reshape((items * cl_dev, senders * slots) + rows.shape[3:])


def from_clusters(mixed, senders, cl_dev, items):
    slots = mixed.shape[1] // senders
    shaped = mixed.reshape(items, cl_dev, senders, slots, mixed.shape[2])
    return jnp.transpose(shaped, (2, 1, 3, 0, 4)).reshape(
        senders, cl_dev * slots, items, mixed.shape[2]
    )


def owner_work(incoming, cl_dev):
    q_in, k_in, v_in, p_in = incoming
    senders, items = (q_in.shape[0], q_in.shape[2])
    q_rows = to_clusters(q_in, cl_dev)
    k_rows = to_clusters(k_in, cl_dev)
    v_rows = to_clusters(v_in, cl_dev)
    p_rows = to_clusters(p_in, cl_dev)
    mixed = attend(q_rows, k_rows, v_rows, p_rows)
    back = from_clusters(mixed, senders, cl_dev, items)
    return back


def body(queries, keys, values, cluster_of, slot_of, centroids, out_weight):
    ranks = lax.axis_size("ctx")
    rank_here = lax.axis_index("ctx")
    tok_rows = queries.shape[0]
    head_rows = cluster_of.shape[0]
    head_size = queries.shape[1] // head_rows
    cl_dev = CLUSTERS // ranks
    width = CLUSTERS * SLOTS
    target = jnp.transpose(cluster_of * SLOTS + slot_of)
    head_ids = jnp.broadcast_to(jnp.arange(head_rows, dtype=jnp.int32)[None, :], target.shape)

    def place(rows):
        shaped = rows.reshape(tok_rows, head_rows, head_size)
        filled = (
            jnp.zeros((width, head_rows, head_size), rows.dtype).at[target, head_ids].set(shaped)
        )
        return filled.reshape(ranks, width // ranks, head_rows, head_size)

    token_pos = rank_here * tok_rows + jnp.arange(tok_rows, dtype=jnp.int32)
    pos_slots = (
        jnp.full((width, head_rows), -1, jnp.int32)
        .at[target, head_ids]
        .set(jnp.broadcast_to(token_pos[:, None], target.shape))
    )
    pos_slots = pos_slots.reshape(ranks, width // ranks, head_rows)
    incoming = (
        lax.all_to_all(place(queries), "ctx", split_axis=0, concat_axis=0, tiled=True),
        lax.all_to_all(place(keys), "ctx", split_axis=0, concat_axis=0, tiled=True),
        lax.all_to_all(place(values), "ctx", split_axis=0, concat_axis=0, tiled=True),
        lax.all_to_all(pos_slots, "ctx", split_axis=0, concat_axis=0, tiled=True),
    )
    worked = owner_work(incoming, cl_dev)
    returned = lax.all_to_all(worked, "ctx", split_axis=0, concat_axis=0, tiled=True)
    rows_back = returned.reshape(width, head_rows, head_size)
    attended = rows_back[target, head_ids].reshape(tok_rows, head_rows * head_size)
    member = (
        cluster_of[:, :, None] == jnp.arange(CLUSTERS, dtype=jnp.int32)[None, None, :]
    ).astype(jnp.bfloat16)
    q_three = queries.reshape(tok_rows, head_rows, head_size)
    k_three = keys.reshape(tok_rows, head_rows, head_size)
    local_sums = jnp.einsum("htc,thd->hcd", member, q_three, preferred_element_type=jnp.float32)
    local_sums = local_sums + jnp.einsum(
        "htc,thd->hcd", member, k_three, preferred_element_type=jnp.float32
    )
    local_counts = jnp.sum(member, axis=1, dtype=jnp.float32)
    totals, counts = (
        lax.psum_scatter(
            local_sums.astype(jnp.bfloat16), "ctx", scatter_dimension=1, tiled=True
        ).astype(jnp.float32),
        lax.psum_scatter(
            local_counts.astype(jnp.bfloat16), "ctx", scatter_dimension=1, tiled=True
        ).astype(jnp.float32),
    )
    means = totals / (2.0 * jnp.maximum(counts, 1.0))[:, :, None]
    new_centroids = mix_rate * centroids + (1.0 - mix_rate) * means
    summed = lax.psum_scatter(
        lax.dot_general(
            out_weight, attended, (((0,), (1,)), ((), ())), preferred_element_type=jnp.float32
        ),
        "head",
        scatter_dimension=0,
        tiled=True,
    )
    projected = jnp.transpose(summed).astype(jnp.bfloat16)
    return (projected, new_centroids)


BF16 = jnp.bfloat16
F32 = jnp.float32
PAIR = 2
EMPTY = 1e9


def params(limit):
    return pltpu.CompilerParams(
        dimension_semantics=("arbitrary",), vmem_limit_bytes=limit * 1024 * 1024
    )


def cost(flops, nbytes, transcendentals=0):
    return pl.CostEstimate(
        flops=flops, bytes_accessed=nbytes, transcendentals=transcendentals
    )


def pack_kernel(count, *refs):
    sources, marks_ref = refs[:count], refs[count]
    out_ref, sems = refs[count + 1], refs[count + 2]
    tokens, heads = sources[0].shape[0], out_ref.shape[0]
    copies = []
    for n, source in enumerate(sources):
        for j in range(heads):
            copies.append(
                pltpu.make_async_copy(
                    source.at[:, pl.ds(j * 128, 128)],
                    out_ref.at[j, pl.ds(n * tokens, tokens)],
                    sems.at[len(copies)],
                )
            )
    marked = out_ref.at[:, pl.ds(count * tokens, marks_ref.shape[1])]
    copies.append(pltpu.make_async_copy(marks_ref, marked, sems.at[len(copies)]))
    for copy in copies:
        copy.start()
    for copy in copies:
        copy.wait()


def pack(sources, marks):
    tokens, heads = sources[0].shape[0], marks.shape[0]
    rows = len(sources) * tokens + marks.shape[1]
    anywhere = pl.BlockSpec(memory_space=pl.ANY)
    return pl.pallas_call(
        functools.partial(pack_kernel, len(sources)),
        in_specs=[anywhere] * (len(sources) + 1),
        out_specs=anywhere,
        out_shape=jax.ShapeDtypeStruct((heads, rows, 128), BF16),
        scratch_shapes=[pltpu.SemaphoreType.DMA((len(sources) * heads + 1,))],
        compiler_params=pltpu.CompilerParams(vmem_limit_bytes=60 * 1024 * 1024),
        cost_estimate=cost(0, 2 * heads * rows * 256),
    )(*sources, marks)


def split_kernel(v_ref, out_ref):
    out_ref[0] = v_ref[...]


def split(values, heads):
    tokens = values.shape[0]
    return pl.pallas_call(
        split_kernel,
        grid=(heads,),
        in_specs=[pl.BlockSpec((tokens, 128), lambda j: (0, j))],
        out_specs=pl.BlockSpec((1, tokens, 128), lambda j: (j, 0, 0)),
        out_shape=jax.ShapeDtypeStruct((heads, tokens, 128), BF16),
        compiler_params=params(60),
        cost_estimate=cost(0, 2 * heads * tokens * 256),
    )(values)


def match(first, count, target):
    rows = first + lax.broadcasted_iota(jnp.int32, (count, target.shape[1]), 0)
    return rows == target


def by_slot(x):
    return x.reshape(x.shape[0] // SLOTS, SLOTS, 128)


def place_pair_kernel(target_ref, q_ref, k_ref, q_out, k_out, p_out, right):
    tokens = q_ref.shape[1]
    slots = q_out.shape[0] * SLOTS
    step = 1024
    right[:, :128] = q_ref[0]
    right[:, 128:] = k_ref[0]
    base = pl.program_id(0) * tokens
    token = (base + lax.broadcasted_iota(jnp.int32, (1, tokens), 1)).astype(F32)
    target = target_ref[0]

    def move(i, carry):
        picked = match(i * step, step, target)
        out = jnp.dot(picked.astype(BF16), right[...], preferred_element_type=F32)
        where = pl.ds(i * (step // SLOTS), step // SLOTS)
        q_out[where] = by_slot(out[:, :128]).astype(BF16)
        k_out[where] = by_slot(out[:, 128:]).astype(BF16)
        at = jnp.min(jnp.where(picked, token, EMPTY), axis=1, keepdims=True)
        p_out[where] = by_slot(jnp.broadcast_to(at, (step, 128)))
        return carry

    lax.fori_loop(0, slots // step, move, 0)


def place_pair(target, first, tokens):
    ranks = first.shape[0]
    spec_out = pl.BlockSpec((CLUSTERS, SLOTS, 128), lambda j: (0, j, 0))
    shape = (CLUSTERS, ranks * SLOTS, 128)
    return pl.pallas_call(
        place_pair_kernel,
        grid=(ranks,),
        in_specs=[
            pl.BlockSpec((1, 1, tokens), lambda j: (j, 0, 0)),
            pl.BlockSpec((1, tokens, 128), lambda j: (j, 0, 0)),
            pl.BlockSpec((1, tokens, 128), lambda j: (j, 1, 0)),
        ],
        out_specs=[spec_out, spec_out, spec_out],
        out_shape=[
            jax.ShapeDtypeStruct(shape, BF16),
            jax.ShapeDtypeStruct(shape, BF16),
            jax.ShapeDtypeStruct(shape, F32),
        ],
        scratch_shapes=[pltpu.VMEM((tokens, 256), BF16)],
        compiler_params=params(60),
        cost_estimate=cost(1, 1),
    )(target, first, first)


def place_one_kernel(who_ref, target_ref, v_ref, *refs):
    v_out = refs[-1]
    slots = v_out.shape[0] * SLOTS
    picked = match(0, slots, target_ref[0]).astype(BF16)
    out = jnp.dot(picked, v_ref[...], preferred_element_type=F32)
    v_out[...] = by_slot(out).astype(BF16)


def place_one(who, target, rows, placed):
    ranks, tokens = target.shape[0], target.shape[2]
    in_specs = [
        pl.BlockSpec((1, 1, tokens), lambda i, who: (who[0], 0, 0)),
        pl.BlockSpec((tokens, 128), lambda i, who: (0, 0)),
    ]
    args = [who, target, rows]
    aliases = {}
    if placed is not None:
        in_specs.append(pl.BlockSpec(memory_space=pl.ANY))
        args.append(placed)
        aliases = {3: 0}
    return pl.pallas_call(
        place_one_kernel,
        grid_spec=pltpu.PrefetchScalarGridSpec(
            num_scalar_prefetch=1,
            grid=(1,),
            in_specs=in_specs,
            out_specs=pl.BlockSpec((CLUSTERS, SLOTS, 128), lambda i, who: (0, who[0], 0)),
        ),
        out_shape=jax.ShapeDtypeStruct((CLUSTERS, ranks * SLOTS, 128), BF16),
        input_output_aliases=aliases,
        compiler_params=params(60),
        cost_estimate=cost(1, 1),
    )(*args)


def weigh_kernel(q_ref, k_ref, p_ref, w_out, mean_out):
    count, rows = q_ref.shape[0], q_ref.shape[1]
    cap = rows // PAIR
    scale = 1.0 / math.sqrt(q_ref.shape[2])
    same = (
        lax.broadcasted_iota(jnp.int32, (rows, rows), 0) // cap
        == lax.broadcasted_iota(jnp.int32, (rows, rows), 1) // cap
    )
    for n in range(count):
        q, k, own = q_ref[n], k_ref[n], p_ref[n]
        scores = lax.dot_general(q, k, (((1,), (1,)), ((), ())), preferred_element_type=F32) * scale
        allowed = same & (jnp.transpose(own) <= own)
        scores = jnp.where(allowed, scores, neg_fill)
        top = jnp.max(scores, axis=1, keepdims=True)
        w_out[n] = jnp.where(allowed, jnp.exp(scores - top), 0.0).astype(BF16)
    both = (q_ref[...].astype(F32) + k_ref[...].astype(F32)).reshape(count * PAIR, cap, 128)
    held = (p_ref[...] < EMPTY).astype(F32).reshape(count * PAIR, cap, 128)
    mean_out[...] = jnp.sum(both, axis=1) / (2.0 * jnp.maximum(jnp.sum(held, axis=1), 1.0))


def weigh(q_rows, k_rows, at):
    groups, rows = q_rows.shape[0], q_rows.shape[1]
    step = 8
    spec = pl.BlockSpec((step, rows, 128), lambda i: (i, 0, 0))
    return pl.pallas_call(
        weigh_kernel,
        grid=(groups // step,),
        in_specs=[spec, spec, spec],
        out_specs=[
            pl.BlockSpec((step, rows, rows), lambda i: (i, 0, 0)),
            pl.BlockSpec((step * PAIR, 128), lambda i: (i, 0)),
        ],
        out_shape=[
            jax.ShapeDtypeStruct((groups, rows, rows), BF16),
            jax.ShapeDtypeStruct((groups * PAIR, 128), F32),
        ],
        compiler_params=params(60),
        cost_estimate=cost(1, 1),
    )(q_rows, k_rows, at)


def mix_kernel(w_ref, v_ref, o_out):
    count, rows = w_ref.shape[0], w_ref.shape[1]
    ones = jnp.ones((rows, 128), BF16)
    for n in range(count):
        right = jnp.concatenate([v_ref[n], ones], axis=1)
        out = jnp.dot(w_ref[n], right, preferred_element_type=F32)
        total = out[:, 128:]
        o_out[n] = (out[:, :128] / jnp.where(total > 0.0, total, 1.0)).astype(BF16)


def mix(weights, v_rows):
    groups, rows = weights.shape[0], weights.shape[1]
    step = 16

    def spec(width):
        return pl.BlockSpec((step, rows, width), lambda i: (i, 0, 0))

    return pl.pallas_call(
        mix_kernel,
        grid=(groups // step,),
        in_specs=[spec(rows), spec(128)],
        out_specs=spec(128),
        out_shape=jax.ShapeDtypeStruct((groups, rows, 128), BF16),
        compiler_params=params(60),
        cost_estimate=cost(1, 1),
    )(weights, v_rows)


def unplace_kernel(who_ref, target_ref, o_ref, mean_ref, out_ref):
    tokens = target_ref.shape[2]
    slots = o_ref.shape[0] * SLOTS
    right = o_ref[...].astype(F32).reshape(slots, 128).astype(BF16)
    target = jnp.transpose(jnp.broadcast_to(target_ref[0], (128, tokens)))
    columns = lax.broadcasted_iota(jnp.int32, (tokens, slots), 1)
    picked = (columns == jnp.tile(target, (1, slots // 128))).astype(BF16)
    out_ref[:tokens] = jnp.dot(picked, right, preferred_element_type=F32).astype(BF16)
    means = mean_ref[...]
    high = means.astype(BF16)
    count = means.shape[0]
    out_ref[tokens : tokens + count] = high
    out_ref[tokens + count :] = (means - high.astype(F32)).astype(BF16)


def unplace(who, target, mixed, means):
    tokens = target.shape[2]
    count = CLUSTERS // target.shape[0]
    return pl.pallas_call(
        unplace_kernel,
        grid_spec=pltpu.PrefetchScalarGridSpec(
            num_scalar_prefetch=1,
            grid=(1,),
            in_specs=[
                pl.BlockSpec((1, 1, tokens), lambda i, who: (who[0], 0, 0)),
                pl.BlockSpec((CLUSTERS, SLOTS, 128), lambda i, who: (0, who[0], 0)),
                pl.BlockSpec((count, 128), lambda i, who: (who[0], 0)),
            ],
            out_specs=pl.BlockSpec((tokens + 2 * count, 128), lambda i, who: (0, 0)),
        ),
        out_shape=jax.ShapeDtypeStruct((tokens + 2 * count, 128), BF16),
        compiler_params=params(60),
        cost_estimate=cost(1, 1),
    )(who, target, mixed, means)


def project_kernel(pieces, lanes, has_total, *refs):
    refs = refs[1:]
    atts, ws = refs[:pieces], refs[pieces : pieces + 4 * lanes]
    out_ref = refs[-1]
    left = jnp.concatenate([a[...] for a in atts], axis=1)
    right = jnp.concatenate([w[...] for w in ws], axis=0)
    total = jnp.dot(left, right, preferred_element_type=F32)
    if has_total:
        total = total + refs[pieces + 4 * lanes][...]
    out_ref[...] = total.astype(out_ref.dtype)


def project(where, tokens, atts, weights, columns, total, dtype):
    lanes, pieces = len(where), sum(len(group) for group in atts)
    step = 256
    cols = weights[3].shape[1]
    args = [a for group in atts for a in group]
    in_specs = [pl.BlockSpec((step, a.shape[1]), lambda i, w: (i, 0)) for a in args]
    for part in range(4):
        for lane in range(lanes):
            in_specs.append(
                pl.BlockSpec(
                    (128, cols), lambda i, w, lane=lane, part=part: (w[lane], w[lanes + part])
                )
            )
            args.append(weights[part])
    if total is not None:
        in_specs.append(pl.BlockSpec((step, cols), lambda i, w: (i, 0)))
        args.append(total)
    return pl.pallas_call(
        functools.partial(project_kernel, pieces, lanes, total is not None),
        grid_spec=pltpu.PrefetchScalarGridSpec(
            num_scalar_prefetch=1,
            grid=(tokens // step,),
            in_specs=in_specs,
            out_specs=pl.BlockSpec((step, cols), lambda i, w: (i, 0)),
        ),
        out_shape=jax.ShapeDtypeStruct((tokens, cols), dtype),
        compiler_params=params(60),
        cost_estimate=cost(1, 1),
    )(jnp.stack(list(where) + list(columns)), *args)


def head_body(queries, keys, values, cluster_of, slot_of, centroids, out_weight):
    ranks = lax.axis_size("ctx")
    me = lax.axis_index("ctx")
    mine = lax.axis_index("head")
    tokens = queries.shape[0]
    cl_dev = CLUSTERS // ranks
    cap = ranks * SLOTS
    y, core = mine // 2, mine % 2

    def swap_y(x):
        return lax.ppermute(x, "head", [(0, 2), (1, 3), (2, 0), (3, 1)])

    def swap_core(x):
        return lax.ppermute(x, "head", [(0, 1), (1, 0), (2, 3), (3, 2)])

    def swap_ctx(x, d):
        return lax.ppermute(x, "ctx", [(i, i ^ d) for i in range(ranks)])

    def who(d):
        return jnp.reshape(me ^ d, (1,))

    def after(x, other):
        return lax.optimization_barrier((x, other))[0]

    marks = [x.astype(BF16).reshape(ranks, tokens // 128, 128) for x in (cluster_of, slot_of)]
    first = pack((queries, keys), jnp.concatenate(marks, axis=1))
    first = lax.all_to_all(first, "ctx", split_axis=0, concat_axis=0, tiled=True)
    v_heads = split(values, ranks)
    v_heads = {d: lax.dynamic_index_in_dim(v_heads, me ^ d, 0, False) for d in range(ranks)}

    cols = out_weight.shape[1] // 4
    across = swap_y(lax.dynamic_slice_in_dim(out_weight, (1 - y) * 2 * cols, 2 * cols, 1))
    beside = swap_core(
        lax.dynamic_slice_in_dim(out_weight, (2 * y + 1 - core) * cols, cols, 1)
    )
    corner = swap_core(lax.dynamic_slice_in_dim(across, (1 - core) * cols, cols, 1))
    w_columns = (mine, core, jnp.zeros_like(core), jnp.zeros_like(core))

    v_heads = after(v_heads, (first, across, beside))
    rows_v = {0: v_heads[0]}
    for d in (4, 5, 6, 1):
        rows_v[d] = swap_ctx(v_heads[d], d)

    marks = first[:, 2 * tokens :, :].astype(jnp.int32)
    target = marks[:, : tokens // 128, :] * SLOTS + marks[:, tokens // 128 :, :]
    target = target.reshape(ranks, 1, tokens)
    q_rows, k_rows, at = place_pair(target, first, tokens)

    def paired(x):
        return x.reshape(CLUSTERS // PAIR, PAIR * cap, 128)

    rows_v[2] = swap_ctx(after(v_heads[2], (rows_v[1], q_rows)), 2)
    q_rows = after(q_rows, corner)
    weights, means = weigh(paired(q_rows), paired(k_rows), paired(at))
    for d in (7, 3):
        rows_v[d] = swap_ctx(after(v_heads[d], (rows_v[2], weights)), d)
    placed = None
    for d in (0, 1, 2, 4, 5, 3, 6, 7):
        placed = place_one(who(d), target, rows_v[d], placed)
    w_parts = (out_weight, across, beside, corner)
    mixed = mix(weights, paired(placed)).reshape(CLUSTERS, cap, 128)

    def leave(d, *others):
        return unplace(after(who(d), others) if others else who(d), target, mixed, means)

    def side(blocks):
        return jnp.concatenate([block[:tokens] for block in blocks], axis=1)

    got = {d: swap_ctx(leave(d), d) for d in (4, 5)}
    got[0] = leave(0)
    y_0 = swap_y(got[0])
    got[1] = swap_ctx(leave(1), 1)
    got[2] = swap_ctx(leave(2, y_0), 2)
    got[3] = swap_ctx(leave(3, got[1]), 3)
    own_123 = side([got[d] for d in (1, 2, 3)])
    y_123 = swap_y(own_123)
    got[6] = swap_ctx(leave(6, got[4], got[3]), 6)
    got[7] = swap_ctx(leave(7, got[5]), 7)
    own_45 = side([got[d] for d in (4, 5)])
    y_45 = swap_y(own_45)
    own_0123 = side([got[0], own_123])
    core_0123 = swap_core(after(own_0123, y_123))
    both_0123 = side([y_0, y_123])
    core_both_0123 = swap_core(both_0123)
    y_6 = swap_y(after(got[6], y_123))
    core_45 = swap_core(after(own_45, core_both_0123))
    y_7 = swap_y(got[7])
    core_both_45 = swap_core(after(y_45, core_45))

    def add(total, lanes, atts, dtype):
        heads = [me ^ d for d in lanes]
        return project(heads, tokens, atts, w_parts, w_columns, total, dtype)

    total = add(
        None, (0, 1, 2, 3), [[own_0123], [both_0123], [core_0123], [core_both_0123]], F32
    )
    total = add(total, (4, 5), [[own_45], [y_45], [core_45], [core_both_45]], F32)
    core_67 = swap_core(side([got[6], got[7]]))
    core_y_6, core_y_7 = swap_core(y_6), swap_core(y_7)
    total = add(
        total, (6, 7), [[got[6], got[7]], [y_6, y_7], [core_67], [core_y_6, core_y_7]], BF16
    )

    sent = jnp.stack([got[d][tokens:] for d in range(ranks)]).astype(F32)
    sent = sent[:, :cl_dev] + sent[:, cl_dev:]
    sent = jnp.concatenate(
        [lax.dynamic_slice_in_dim(sent, me ^ d, 1, 0) for d in range(ranks)], axis=0
    )
    new_centroids = mix_rate * centroids + (1.0 - mix_rate) * sent
    return (total, new_centroids)


def dispatch(queries, keys, values, cluster_of, *rest):
    ranks, heads = lax.axis_size("ctx"), cluster_of.shape[0]
    whole_heads = ranks == heads == 8 and lax.axis_size("head") == 4
    step = head_body if whole_heads else body
    return step(queries, keys, values, cluster_of, *rest)


def solution(mesh):
    in_specs = (
        P("ctx", "head"),
        P("ctx", "head"),
        P("ctx", "head"),
        P("head", "ctx"),
        P("head", "ctx"),
        P("head", "ctx", None),
        P("head", None),
    )
    out_specs = (P("ctx", "head"), P("head", "ctx", None))
    return jax.shard_map(
        dispatch, mesh=mesh, in_specs=in_specs, out_specs=out_specs, check_vma=False
    )
```

```python
import functools
import math

import jax
import jax.numpy as jnp
from jax import lax
from jax.experimental import pallas as pl
from jax.experimental.pallas import tpu as pltpu
from jax.sharding import PartitionSpec as P

CLUSTERS = 256
SLOTS = 8


mix_rate = 0.5
neg_fill = -1e30


def attend(q_rows, k_rows, v_rows, positions):
    scale = 1.0 / math.sqrt(q_rows.shape[-1])
    scores = jnp.einsum("gqd,gkd->gqk", q_rows, k_rows, preferred_element_type=jnp.float32) * scale
    allowed = (positions[:, None, :] >= 0) & (positions[:, None, :] <= positions[:, :, None])
    scores = jnp.where(allowed, scores, neg_fill)
    top = jnp.max(scores, axis=2, keepdims=True)
    weights = jnp.where(allowed, jnp.exp(scores - top), 0.0).astype(jnp.bfloat16)
    total = jnp.sum(weights.astype(jnp.float32), axis=2, keepdims=True)
    mixed = jnp.einsum("gqk,gkd->gqd", weights, v_rows, preferred_element_type=jnp.float32)
    return (mixed / jnp.where(total > 0.0, total, 1.0)).astype(jnp.bfloat16)


def to_clusters(rows, cl_dev):
    senders, width, items = (rows.shape[0], rows.shape[1], rows.shape[2])
    slots = width // cl_dev
    shaped = rows.reshape((senders, cl_dev, slots, items) + rows.shape[3:])
    if rows.ndim == 4:
        order = (3, 1, 0, 2, 4)
    else:
        order = (3, 1, 0, 2)
    return jnp.transpose(shaped, order).reshape((items * cl_dev, senders * slots) + rows.shape[3:])


def from_clusters(mixed, senders, cl_dev, items):
    slots = mixed.shape[1] // senders
    shaped = mixed.reshape(items, cl_dev, senders, slots, mixed.shape[2])
    return jnp.transpose(shaped, (2, 1, 3, 0, 4)).reshape(
        senders, cl_dev * slots, items, mixed.shape[2]
    )


def owner_work(incoming, cl_dev):
    q_in, k_in, v_in, p_in = incoming
    senders, items = (q_in.shape[0], q_in.shape[2])
    q_rows = to_clusters(q_in, cl_dev)
    k_rows = to_clusters(k_in, cl_dev)
    v_rows = to_clusters(v_in, cl_dev)
    p_rows = to_clusters(p_in, cl_dev)
    mixed = attend(q_rows, k_rows, v_rows, p_rows)
    back = from_clusters(mixed, senders, cl_dev, items)
    return back


def body(queries, keys, values, cluster_of, slot_of, centroids, out_weight):
    ranks = lax.axis_size("ctx")
    rank_here = lax.axis_index("ctx")
    tok_rows = queries.shape[0]
    head_rows = cluster_of.shape[0]
    head_size = queries.shape[1] // head_rows
    cl_dev = CLUSTERS // ranks
    width = CLUSTERS * SLOTS
    target = jnp.transpose(cluster_of * SLOTS + slot_of)
    head_ids = jnp.broadcast_to(jnp.arange(head_rows, dtype=jnp.int32)[None, :], target.shape)

    def place(rows):
        shaped = rows.reshape(tok_rows, head_rows, head_size)
        filled = (
            jnp.zeros((width, head_rows, head_size), rows.dtype).at[target, head_ids].set(shaped)
        )
        return filled.reshape(ranks, width // ranks, head_rows, head_size)

    token_pos = rank_here * tok_rows + jnp.arange(tok_rows, dtype=jnp.int32)
    pos_slots = (
        jnp.full((width, head_rows), -1, jnp.int32)
        .at[target, head_ids]
        .set(jnp.broadcast_to(token_pos[:, None], target.shape))
    )
    pos_slots = pos_slots.reshape(ranks, width // ranks, head_rows)
    incoming = (
        lax.all_to_all(place(queries), "ctx", split_axis=0, concat_axis=0, tiled=True),
        lax.all_to_all(place(keys), "ctx", split_axis=0, concat_axis=0, tiled=True),
        lax.all_to_all(place(values), "ctx", split_axis=0, concat_axis=0, tiled=True),
        lax.all_to_all(pos_slots, "ctx", split_axis=0, concat_axis=0, tiled=True),
    )
    worked = owner_work(incoming, cl_dev)
    returned = lax.all_to_all(worked, "ctx", split_axis=0, concat_axis=0, tiled=True)
    rows_back = returned.reshape(width, head_rows, head_size)
    attended = rows_back[target, head_ids].reshape(tok_rows, head_rows * head_size)
    member = (
        cluster_of[:, :, None] == jnp.arange(CLUSTERS, dtype=jnp.int32)[None, None, :]
    ).astype(jnp.bfloat16)
    q_three = queries.reshape(tok_rows, head_rows, head_size)
    k_three = keys.reshape(tok_rows, head_rows, head_size)
    local_sums = jnp.einsum("htc,thd->hcd", member, q_three, preferred_element_type=jnp.float32)
    local_sums = local_sums + jnp.einsum(
        "htc,thd->hcd", member, k_three, preferred_element_type=jnp.float32
    )
    local_counts = jnp.sum(member, axis=1, dtype=jnp.float32)
    totals, counts = (
        lax.psum_scatter(
            local_sums.astype(jnp.bfloat16), "ctx", scatter_dimension=1, tiled=True
        ).astype(jnp.float32),
        lax.psum_scatter(
            local_counts.astype(jnp.bfloat16), "ctx", scatter_dimension=1, tiled=True
        ).astype(jnp.float32),
    )
    means = totals / (2.0 * jnp.maximum(counts, 1.0))[:, :, None]
    new_centroids = mix_rate * centroids + (1.0 - mix_rate) * means
    summed = lax.psum_scatter(
        lax.dot_general(
            out_weight, attended, (((0,), (1,)), ((), ())), preferred_element_type=jnp.float32
        ),
        "head",
        scatter_dimension=0,
        tiled=True,
    )
    projected = jnp.transpose(summed).astype(jnp.bfloat16)
    return (projected, new_centroids)


BF16 = jnp.bfloat16
F32 = jnp.float32
PAIR = 2
EMPTY = 1e9


def params(limit):
    return pltpu.CompilerParams(
        dimension_semantics=("arbitrary",), vmem_limit_bytes=limit * 1024 * 1024
    )


def cost(flops, nbytes, transcendentals=0):
    return pl.CostEstimate(
        flops=flops, bytes_accessed=nbytes, transcendentals=transcendentals
    )


def pack_first_kernel(q_ref, k_ref, v_ref, marks_ref, out_ref):
    tokens, some = q_ref.shape[0], v_ref.shape[0]
    out_ref[0, :tokens] = q_ref[...]
    out_ref[0, tokens : 2 * tokens] = k_ref[...]
    out_ref[0, 2 * tokens : 2 * tokens + some] = v_ref[...]
    out_ref[0, 2 * tokens + some :] = marks_ref[0]


def pack_first(queries, keys, values, marks, some):
    tokens, heads = queries.shape[0], marks.shape[0]
    rows = 2 * tokens + some + marks.shape[1]
    whole = pl.BlockSpec((tokens, 128), lambda j: (0, j))
    return pl.pallas_call(
        pack_first_kernel,
        grid=(heads,),
        in_specs=[
            whole,
            whole,
            pl.BlockSpec((some, 128), lambda j: (0, j)),
            pl.BlockSpec((1, marks.shape[1], 128), lambda j: (j, 0, 0)),
        ],
        out_specs=pl.BlockSpec((1, rows, 128), lambda j: (j, 0, 0)),
        out_shape=jax.ShapeDtypeStruct((heads, rows, 128), BF16),
        compiler_params=params(60),
        cost_estimate=cost(0, 2 * heads * rows * 256),
    )(queries, keys, values, marks)


def pack_rest_kernel(v_ref, out_ref):
    out_ref[0] = v_ref[...]


def pack_rest(values, heads, some):
    rest = values.shape[0] - some
    return pl.pallas_call(
        pack_rest_kernel,
        grid=(heads,),
        in_specs=[pl.BlockSpec((rest, 128), lambda j: (1, j))],
        out_specs=pl.BlockSpec((1, rest, 128), lambda j: (j, 0, 0)),
        out_shape=jax.ShapeDtypeStruct((heads, rest, 128), BF16),
        compiler_params=params(60),
        cost_estimate=cost(0, 2 * heads * rest * 256),
    )(values)


def match(first, count, target):
    rows = first + lax.broadcasted_iota(jnp.int32, (count, target.shape[1]), 0)
    return rows == target


def by_slot(x):
    return x.reshape(x.shape[0] // SLOTS, SLOTS, 128)


def place_pair_kernel(target_ref, q_ref, k_ref, q_out, k_out, p_out, right):
    tokens = q_ref.shape[1]
    slots = q_out.shape[0] * SLOTS
    step = 1024
    right[:, :128] = q_ref[0]
    right[:, 128:] = k_ref[0]
    base = pl.program_id(0) * tokens
    token = (base + lax.broadcasted_iota(jnp.int32, (1, tokens), 1)).astype(F32)
    target = target_ref[0]

    def move(i, carry):
        picked = match(i * step, step, target)
        out = jnp.dot(picked.astype(BF16), right[...], preferred_element_type=F32)
        where = pl.ds(i * (step // SLOTS), step // SLOTS)
        q_out[where] = by_slot(out[:, :128]).astype(BF16)
        k_out[where] = by_slot(out[:, 128:]).astype(BF16)
        at = jnp.min(jnp.where(picked, token, EMPTY), axis=1, keepdims=True)
        p_out[where] = by_slot(jnp.broadcast_to(at, (step, 128)))
        return carry

    lax.fori_loop(0, slots // step, move, 0)


def place_pair(target, first, tokens):
    ranks = first.shape[0]
    spec_out = pl.BlockSpec((CLUSTERS, SLOTS, 128), lambda j: (0, j, 0))
    shape = (CLUSTERS, ranks * SLOTS, 128)
    return pl.pallas_call(
        place_pair_kernel,
        grid=(ranks,),
        in_specs=[
            pl.BlockSpec((1, 1, tokens), lambda j: (j, 0, 0)),
            pl.BlockSpec((1, tokens, 128), lambda j: (j, 0, 0)),
            pl.BlockSpec((1, tokens, 128), lambda j: (j, 1, 0)),
        ],
        out_specs=[spec_out, spec_out, spec_out],
        out_shape=[
            jax.ShapeDtypeStruct(shape, BF16),
            jax.ShapeDtypeStruct(shape, BF16),
            jax.ShapeDtypeStruct(shape, F32),
        ],
        scratch_shapes=[pltpu.VMEM((tokens, 256), BF16)],
        compiler_params=params(16),
        cost_estimate=cost(2 * ranks * CLUSTERS * SLOTS * tokens * 256, 16 << 20),
    )(target, first, first)


def place_some_kernel(target_ref, v_ref, v_out):
    slots = v_out.shape[0] * SLOTS
    some = v_ref.shape[1]
    picked = match(0, slots, target_ref[0, :, :some]).astype(BF16)
    out = jnp.dot(picked, v_ref[0], preferred_element_type=F32)
    v_out[...] = by_slot(out).astype(BF16)


def place_some(target, first, tokens, some):
    ranks = first.shape[0]
    block = 2 * tokens // some
    return pl.pallas_call(
        place_some_kernel,
        grid=(ranks,),
        in_specs=[
            pl.BlockSpec((1, 1, tokens), lambda j: (j, 0, 0)),
            pl.BlockSpec((1, some, 128), lambda j: (j, block, 0)),
        ],
        out_specs=pl.BlockSpec((CLUSTERS, SLOTS, 128), lambda j: (0, j, 0)),
        out_shape=pltpu.HBM((CLUSTERS, ranks * SLOTS, 128), BF16),
        compiler_params=params(10),
        cost_estimate=cost(2 * ranks * CLUSTERS * SLOTS * some * 256, 6 << 20),
    )(target, first)


def weigh_kernel(q_ref, k_ref, p_ref, w_out, mean_out):
    count, rows = q_ref.shape[0], q_ref.shape[1]
    cap = rows // PAIR
    scale = 1.0 / math.sqrt(q_ref.shape[2])
    same = (
        lax.broadcasted_iota(jnp.int32, (rows, rows), 0) // cap
        == lax.broadcasted_iota(jnp.int32, (rows, rows), 1) // cap
    )
    for n in range(count):
        q, k, own = q_ref[n], k_ref[n], p_ref[n]
        scores = lax.dot_general(q, k, (((1,), (1,)), ((), ())), preferred_element_type=F32) * scale
        allowed = same & (jnp.transpose(own) <= own)
        scores = jnp.where(allowed, scores, neg_fill)
        top = jnp.max(scores, axis=1, keepdims=True)
        w_out[n] = jnp.where(allowed, jnp.exp(scores - top), 0.0).astype(BF16)
    both = (q_ref[...].astype(F32) + k_ref[...].astype(F32)).reshape(count * PAIR, cap, 128)
    held = (p_ref[...] < EMPTY).astype(F32).reshape(count * PAIR, cap, 128)
    mean_out[...] = jnp.sum(both, axis=1) / (2.0 * jnp.maximum(jnp.sum(held, axis=1), 1.0))


def weigh(q_rows, k_rows, at):
    groups, rows = q_rows.shape[0], q_rows.shape[1]
    step = 8
    spec = pl.BlockSpec((step, rows, 128), lambda i: (i, 0, 0))
    return pl.pallas_call(
        weigh_kernel,
        grid=(groups // step,),
        in_specs=[spec, spec, spec],
        out_specs=[
            pl.BlockSpec((step, rows, rows), lambda i: (i, 0, 0)),
            pl.BlockSpec((step * PAIR, 128), lambda i: (i, 0)),
        ],
        out_shape=[
            pltpu.HBM((groups, rows, rows), BF16),
            jax.ShapeDtypeStruct((groups * PAIR, 128), F32),
        ],
        compiler_params=params(12),
        cost_estimate=cost(2 * groups * rows * rows * 256, 20 << 20, groups * rows * rows),
    )(q_rows, k_rows, at)


def mix_kernel(ranks, target_ref, v_ref, part_ref, w_ref, o_out, v_rows):
    i = pl.program_id(0)
    slots = part_ref.shape[0] * SLOTS
    count, rows = w_ref.shape[0], w_ref.shape[1]
    tokens, rest = target_ref.shape[2], v_ref.shape[1]

    @pl.when(i < ranks)
    def _():
        picked = match(0, slots, target_ref[0, :, tokens - rest :]).astype(BF16)
        out = jnp.dot(picked, v_ref[0], preferred_element_type=F32)
        where = pl.ds(pl.multiple_of(i * SLOTS, SLOTS), SLOTS)
        v_rows[:, where, :] = by_slot(out) + part_ref[...].astype(F32)

    @pl.when(i >= ranks)
    def _():
        ones = jnp.ones((rows, 128), BF16)
        for n in range(count):
            own = v_rows[pl.ds(((i - ranks) * count + n) * PAIR, PAIR)]
            right = jnp.concatenate([own.reshape(rows, 128).astype(BF16), ones], axis=1)
            out = jnp.dot(w_ref[n], right, preferred_element_type=F32)
            total = out[:, 128:]
            o_out[n] = (out[:, :128] / jnp.where(total > 0.0, total, 1.0)).astype(BF16)


def mix(target, rows_v, part, weights):
    ranks, rest = rows_v.shape[0], rows_v.shape[1]
    groups, rows = weights.shape[0], weights.shape[1]
    count = groups // ranks

    def sender(i):
        return jnp.minimum(i, ranks - 1)

    def group(i):
        return jnp.maximum(i - ranks, 0)

    return pl.pallas_call(
        functools.partial(mix_kernel, ranks),
        grid=(2 * ranks,),
        in_specs=[
            pl.BlockSpec((1, 1, target.shape[2]), lambda i: (sender(i), 0, 0)),
            pl.BlockSpec((1, rest, 128), lambda i: (sender(i), 0, 0)),
            pl.BlockSpec((CLUSTERS, SLOTS, 128), lambda i: (0, sender(i), 0)),
            pl.BlockSpec((count, rows, rows), lambda i: (group(i), 0, 0)),
        ],
        out_specs=pl.BlockSpec((count, rows, 128), lambda i: (group(i), 0, 0)),
        out_shape=jax.ShapeDtypeStruct((groups, rows, 128), BF16),
        scratch_shapes=[pltpu.VMEM((CLUSTERS, ranks * SLOTS, 128), F32)],
        compiler_params=params(18),
        cost_estimate=cost(2 * ranks * CLUSTERS * SLOTS * rest * 256, 16 << 20),
    )(target, rows_v, part, weights)


def unplace_kernel(who_ref, target_ref, o_ref, mean_ref, out_ref):
    tokens = target_ref.shape[2]
    slots = o_ref.shape[0] * SLOTS
    right = o_ref[...].astype(F32).reshape(slots, 128).astype(BF16)
    target = jnp.transpose(jnp.broadcast_to(target_ref[0], (128, tokens)))
    columns = lax.broadcasted_iota(jnp.int32, (tokens, slots), 1)
    picked = (columns == jnp.tile(target, (1, slots // 128))).astype(BF16)
    out_ref[0, :tokens] = jnp.dot(picked, right, preferred_element_type=F32).astype(BF16)
    means = mean_ref[...]
    high = means.astype(BF16)
    count = means.shape[0]
    out_ref[0, tokens : tokens + count] = high
    out_ref[0, tokens + count :] = (means - high.astype(F32)).astype(BF16)


def unplace(who, target, mixed, means):
    tokens, partners = target.shape[2], who.shape[0]
    count = CLUSTERS // target.shape[0]
    return pl.pallas_call(
        unplace_kernel,
        grid_spec=pltpu.PrefetchScalarGridSpec(
            num_scalar_prefetch=1,
            grid=(partners,),
            in_specs=[
                pl.BlockSpec((1, 1, tokens), lambda i, who: (who[i], 0, 0)),
                pl.BlockSpec((CLUSTERS, SLOTS, 128), lambda i, who: (0, who[i], 0)),
                pl.BlockSpec((count, 128), lambda i, who: (who[i], 0)),
            ],
            out_specs=pl.BlockSpec((1, tokens + 2 * count, 128), lambda i, who: (i, 0, 0)),
        ),
        out_shape=jax.ShapeDtypeStruct((partners, tokens + 2 * count, 128), BF16),
        compiler_params=params(12),
        cost_estimate=cost(1, 1),
    )(who, target, mixed, means)


def head_body(queries, keys, values, cluster_of, slot_of, centroids, out_weight):
    ranks = lax.axis_size("ctx")
    me = lax.axis_index("ctx")
    mine = lax.axis_index("head")
    tokens = queries.shape[0]
    some = tokens // 2
    near = ranks // 2
    cl_dev = CLUSTERS // ranks
    cap = ranks * SLOTS
    y, core = mine // 2, mine % 2

    def swap_y(x):
        return lax.ppermute(x, "head", [(0, 2), (1, 3), (2, 0), (3, 1)])

    def swap_core(x):
        return lax.ppermute(x, "head", [(0, 1), (1, 0), (2, 3), (3, 2)])

    def after(x, *others):
        return lax.optimization_barrier((x, others))[0]

    marks = [x.astype(BF16).reshape(ranks, tokens // 128, 128) for x in (cluster_of, slot_of)]
    marks = jnp.concatenate(marks, axis=1)
    first = pack_first(queries, keys, values, marks, some)
    first = lax.all_to_all(first, "ctx", split_axis=0, concat_axis=0, tiled=True)

    cols = out_weight.shape[1] // 4
    across = swap_y(lax.dynamic_slice_in_dim(out_weight, (1 - y) * 2 * cols, 2 * cols, 1))
    beside = swap_core(
        lax.dynamic_slice_in_dim(out_weight, (2 * y + 1 - core) * cols, cols, 1)
    )
    corner = swap_core(lax.dynamic_slice_in_dim(across, (1 - core) * cols, cols, 1))
    w_parts = ((out_weight, mine * cols), (across, core * cols), (beside, 0), (corner, 0))

    def w_rows(*lanes):
        picked = [
            lax.dynamic_slice(w, ((me ^ d) * 128, column), (128, cols))
            for w, column in w_parts
            for d in lanes
        ]
        return jnp.concatenate(picked, axis=0)

    w_first, w_second, w_third = w_rows(0, 1, 2, 3), w_rows(4, 5), w_rows(6, 7)

    rows_v = after(pack_rest(values, ranks, some), first, w_first, w_second, w_third)
    rows_v = lax.all_to_all(rows_v, "ctx", split_axis=0, concat_axis=0, tiled=True)

    marks = first[:, 2 * tokens + some :, :].astype(jnp.int32)
    target = marks[:, : tokens // 128, :] * SLOTS + marks[:, tokens // 128 :, :]
    target = target.reshape(ranks, 1, tokens)
    q_rows, k_rows, at = place_pair(target, first, tokens)

    def paired(x):
        return x.reshape(CLUSTERS // PAIR, PAIR * cap, 128)

    weights, means = weigh(paired(q_rows), paired(k_rows), paired(at))
    part = place_some(target, first, tokens, some)
    part, weights = (pltpu.with_memory_space_constraint(x, pltpu.HBM) for x in (part, weights))
    mixed = mix(target, rows_v, part, weights).reshape(CLUSTERS, cap, 128)

    got = {}
    previous = mixed
    base = me // near * near

    def far(d):
        block = unplace(after(jnp.reshape(me ^ d, (1,)), previous), target, mixed, means)
        block = block.reshape(block.shape[1:])
        got[d] = lax.ppermute(block, "ctx", [(i, i ^ d) for i in range(ranks)])
        return block

    previous = far(4)
    previous = far(5)
    close = after(base + jnp.arange(near, dtype=jnp.int32), previous)
    close = unplace(close, target, mixed, means)
    previous = close
    own_0 = lax.dynamic_index_in_dim(close, me % near, 0, False)[:tokens]
    halves = [list(range(h * near, (h + 1) * near)) for h in range(2)]
    close = lax.all_to_all(
        close, "ctx", split_axis=0, concat_axis=0, axis_index_groups=halves, tiled=True
    )
    y_0 = swap_y(own_0)

    def side(*blocks):
        return jnp.concatenate([block[:tokens] for block in blocks], axis=1)

    own_123 = side(
        *[lax.dynamic_index_in_dim(close, (me % near) ^ d, 0, False) for d in (1, 2, 3)]
    )
    y_123 = swap_y(own_123)
    previous = own_123
    previous = far(6)
    far(7)
    own_45 = side(got[4], got[5])
    y_45 = swap_y(after(own_45, own_123))
    core_a = swap_core(side(own_0, own_123, y_0))
    own_67 = side(got[6], got[7])
    y_67 = swap_y(own_67)
    core_67 = swap_core(own_67)
    core_b = swap_core(y_123)

    def dot(left, right):
        return jnp.dot(left, right, preferred_element_type=F32)

    total = dot(side(own_0, own_123, y_0, y_123, core_a, core_b), w_first)
    more_45 = side(own_45, y_45)
    total = total + dot(side(more_45, swap_core(more_45)), w_second)
    most = 6 * 128
    total = total + dot(side(own_67, y_67, core_67), w_third[:most])
    total = total + dot(swap_core(y_67), w_third[most:])
    projected = total.astype(BF16)

    def tails(blocks):
        sent = blocks[:, tokens:].astype(F32)
        return sent[:, :cl_dev] + sent[:, cl_dev:]

    other = tails(jnp.stack([got[d] for d in (4, 5, 6, 7)]))
    other = jnp.concatenate(
        [lax.dynamic_slice_in_dim(other, (me % near) ^ j, 1, 0) for j in range(near)], axis=0
    )
    this = tails(close)
    low = base == 0
    sent = jnp.concatenate([jnp.where(low, this, other), jnp.where(low, other, this)], axis=0)
    new_centroids = mix_rate * centroids + (1.0 - mix_rate) * sent
    return (projected, new_centroids)


def dispatch(queries, keys, values, cluster_of, *rest):
    ranks, heads = lax.axis_size("ctx"), cluster_of.shape[0]
    whole_heads = ranks == heads == 8 and lax.axis_size("head") == 4
    step = head_body if whole_heads else body
    return step(queries, keys, values, cluster_of, *rest)


def solution(mesh):
    in_specs = (
        P("ctx", "head"),
        P("ctx", "head"),
        P("ctx", "head"),
        P("head", "ctx"),
        P("head", "ctx"),
        P("head", "ctx", None),
        P("head", None),
    )
    out_specs = (P("ctx", "head"), P("head", "ctx", None))
    return jax.shard_map(
        dispatch, mesh=mesh, in_specs=in_specs, out_specs=out_specs, check_vma=False
    )
```

```python
import functools
import math

import jax
import jax.numpy as jnp
from jax import lax
from jax.experimental import pallas as pl
from jax.experimental.pallas import tpu as pltpu
from jax.sharding import PartitionSpec as P

CLUSTERS = 256
SLOTS = 8


mix_rate = 0.5
neg_fill = -1e30


def attend(q_rows, k_rows, v_rows, positions):
    scale = 1.0 / math.sqrt(q_rows.shape[-1])
    scores = jnp.einsum("gqd,gkd->gqk", q_rows, k_rows, preferred_element_type=jnp.float32) * scale
    allowed = (positions[:, None, :] >= 0) & (positions[:, None, :] <= positions[:, :, None])
    scores = jnp.where(allowed, scores, neg_fill)
    top = jnp.max(scores, axis=2, keepdims=True)
    weights = jnp.where(allowed, jnp.exp(scores - top), 0.0).astype(jnp.bfloat16)
    total = jnp.sum(weights.astype(jnp.float32), axis=2, keepdims=True)
    mixed = jnp.einsum("gqk,gkd->gqd", weights, v_rows, preferred_element_type=jnp.float32)
    return (mixed / jnp.where(total > 0.0, total, 1.0)).astype(jnp.bfloat16)


def to_clusters(rows, cl_dev):
    senders, width, items = (rows.shape[0], rows.shape[1], rows.shape[2])
    slots = width // cl_dev
    shaped = rows.reshape((senders, cl_dev, slots, items) + rows.shape[3:])
    if rows.ndim == 4:
        order = (3, 1, 0, 2, 4)
    else:
        order = (3, 1, 0, 2)
    return jnp.transpose(shaped, order).reshape((items * cl_dev, senders * slots) + rows.shape[3:])


def from_clusters(mixed, senders, cl_dev, items):
    slots = mixed.shape[1] // senders
    shaped = mixed.reshape(items, cl_dev, senders, slots, mixed.shape[2])
    return jnp.transpose(shaped, (2, 1, 3, 0, 4)).reshape(
        senders, cl_dev * slots, items, mixed.shape[2]
    )


def owner_work(incoming, cl_dev):
    q_in, k_in, v_in, p_in = incoming
    senders, items = (q_in.shape[0], q_in.shape[2])
    q_rows = to_clusters(q_in, cl_dev)
    k_rows = to_clusters(k_in, cl_dev)
    v_rows = to_clusters(v_in, cl_dev)
    p_rows = to_clusters(p_in, cl_dev)
    mixed = attend(q_rows, k_rows, v_rows, p_rows)
    back = from_clusters(mixed, senders, cl_dev, items)
    return back


def body(queries, keys, values, cluster_of, slot_of, centroids, out_weight):
    ranks = lax.axis_size("ctx")
    rank_here = lax.axis_index("ctx")
    tok_rows = queries.shape[0]
    head_rows = cluster_of.shape[0]
    head_size = queries.shape[1] // head_rows
    cl_dev = CLUSTERS // ranks
    width = CLUSTERS * SLOTS
    target = jnp.transpose(cluster_of * SLOTS + slot_of)
    head_ids = jnp.broadcast_to(jnp.arange(head_rows, dtype=jnp.int32)[None, :], target.shape)

    def place(rows):
        shaped = rows.reshape(tok_rows, head_rows, head_size)
        filled = (
            jnp.zeros((width, head_rows, head_size), rows.dtype).at[target, head_ids].set(shaped)
        )
        return filled.reshape(ranks, width // ranks, head_rows, head_size)

    token_pos = rank_here * tok_rows + jnp.arange(tok_rows, dtype=jnp.int32)
    pos_slots = (
        jnp.full((width, head_rows), -1, jnp.int32)
        .at[target, head_ids]
        .set(jnp.broadcast_to(token_pos[:, None], target.shape))
    )
    pos_slots = pos_slots.reshape(ranks, width // ranks, head_rows)
    incoming = (
        lax.all_to_all(place(queries), "ctx", split_axis=0, concat_axis=0, tiled=True),
        lax.all_to_all(place(keys), "ctx", split_axis=0, concat_axis=0, tiled=True),
        lax.all_to_all(place(values), "ctx", split_axis=0, concat_axis=0, tiled=True),
        lax.all_to_all(pos_slots, "ctx", split_axis=0, concat_axis=0, tiled=True),
    )
    worked = owner_work(incoming, cl_dev)
    returned = lax.all_to_all(worked, "ctx", split_axis=0, concat_axis=0, tiled=True)
    rows_back = returned.reshape(width, head_rows, head_size)
    attended = rows_back[target, head_ids].reshape(tok_rows, head_rows * head_size)
    member = (
        cluster_of[:, :, None] == jnp.arange(CLUSTERS, dtype=jnp.int32)[None, None, :]
    ).astype(jnp.bfloat16)
    q_three = queries.reshape(tok_rows, head_rows, head_size)
    k_three = keys.reshape(tok_rows, head_rows, head_size)
    local_sums = jnp.einsum("htc,thd->hcd", member, q_three, preferred_element_type=jnp.float32)
    local_sums = local_sums + jnp.einsum(
        "htc,thd->hcd", member, k_three, preferred_element_type=jnp.float32
    )
    local_counts = jnp.sum(member, axis=1, dtype=jnp.float32)
    totals, counts = (
        lax.psum_scatter(
            local_sums.astype(jnp.bfloat16), "ctx", scatter_dimension=1, tiled=True
        ).astype(jnp.float32),
        lax.psum_scatter(
            local_counts.astype(jnp.bfloat16), "ctx", scatter_dimension=1, tiled=True
        ).astype(jnp.float32),
    )
    means = totals / (2.0 * jnp.maximum(counts, 1.0))[:, :, None]
    new_centroids = mix_rate * centroids + (1.0 - mix_rate) * means
    summed = lax.psum_scatter(
        lax.dot_general(
            out_weight, attended, (((0,), (1,)), ((), ())), preferred_element_type=jnp.float32
        ),
        "head",
        scatter_dimension=0,
        tiled=True,
    )
    projected = jnp.transpose(summed).astype(jnp.bfloat16)
    return (projected, new_centroids)


BF16 = jnp.bfloat16
F32 = jnp.float32
PAIR = 2
EMPTY = 1e9


def params(limit):
    return pltpu.CompilerParams(
        dimension_semantics=("arbitrary",), vmem_limit_bytes=limit * 1024 * 1024
    )


def cost(flops, nbytes, transcendentals=0):
    return pl.CostEstimate(
        flops=flops, bytes_accessed=nbytes, transcendentals=transcendentals
    )


def pack_kernel(steps, *refs):
    out_ref = refs[-1]
    i = pl.program_id(0)
    for n, source in enumerate(refs[:-1]):

        @pl.when(i // steps == n)
        def _(source=source):
            for j in range(out_ref.shape[0]):
                out_ref[j] = source[:, j * 128 : (j + 1) * 128]


def pack(sources):
    tokens, width = sources[0].shape
    heads, rows = width // 128, 256
    steps = tokens // rows

    def block(n):
        return lambda i: (jnp.clip(i - n * steps, 0, steps - 1), 0)

    total = len(sources) * tokens
    return pl.pallas_call(
        functools.partial(pack_kernel, steps),
        grid=(len(sources) * steps,),
        in_specs=[pl.BlockSpec((rows, width), block(n)) for n in range(len(sources))],
        out_specs=pl.BlockSpec((heads, rows, 128), lambda i: (0, i, 0)),
        out_shape=pltpu.HBM((heads, total, 128), BF16),
        compiler_params=params(60),
        cost_estimate=cost(0, 2 * heads * total * 256),
    )(*sources)


def pick_kernel(where_ref, one_ref, two_ref, out_ref):
    i = pl.program_id(0)
    steps = pl.num_programs(0)

    @pl.when(where_ref[2 * steps + i] == 0)
    def _():
        out_ref[...] = one_ref[...]

    @pl.when(where_ref[2 * steps + i] == 1)
    def _():
        out_ref[...] = two_ref[...]


def pick(heads, one, two, columns, groups, cols):
    first, second, which = [], [], []
    for group in groups:
        first += list(group) + [group[-1]] * len(group)
        second += [group[0]] * len(group) + list(group)
        which += [0] * len(group) + [1] * len(group)
    steps = len(which)
    table = jnp.concatenate(
        [
            heads[jnp.array(first)],
            heads[jnp.array(second)],
            jnp.array(which, jnp.int32),
            jnp.stack(columns),
        ]
    )
    return pl.pallas_call(
        pick_kernel,
        grid_spec=pltpu.PrefetchScalarGridSpec(
            num_scalar_prefetch=1,
            grid=(steps,),
            in_specs=[
                pl.BlockSpec((128, cols), lambda i, w: (w[i], w[3 * steps])),
                pl.BlockSpec((128, cols), lambda i, w: (w[steps + i], w[3 * steps + 1])),
            ],
            out_specs=pl.BlockSpec((128, cols), lambda i, w: (i, 0)),
        ),
        out_shape=pltpu.HBM((128 * steps, cols), BF16),
        compiler_params=params(60),
        cost_estimate=cost(1, 1),
    )(table, one, two)


def match(first, count, target):
    rows = first + lax.broadcasted_iota(jnp.int32, (count, target.shape[1]), 0)
    return rows == target


def by_slot(x):
    return x.reshape(x.shape[0] // SLOTS, SLOTS, 128)


def positions_kernel(target_ref, p_out):
    slots = p_out.shape[0] * SLOTS
    tokens = target_ref.shape[2]
    step = 512
    base = pl.program_id(0) * tokens
    token = (base + lax.broadcasted_iota(jnp.int32, (1, tokens), 1)).astype(F32)
    target = target_ref[0]

    def move(i, carry):
        at = jnp.where(match(i * step, step, target), token, EMPTY)
        at = jnp.min(at, axis=1, keepdims=True)
        where = pl.ds(i * (step // SLOTS), step // SLOTS)
        p_out[where] = by_slot(jnp.broadcast_to(at, (step, 128)))
        return carry

    lax.fori_loop(0, slots // step, move, 0)


def positions(target):
    ranks, tokens = target.shape[0], target.shape[2]
    return pl.pallas_call(
        positions_kernel,
        grid=(ranks,),
        in_specs=[pl.BlockSpec((1, 1, tokens), lambda j: (j, 0, 0))],
        out_specs=pl.BlockSpec((CLUSTERS, SLOTS, 128), lambda j: (0, j, 0)),
        out_shape=pltpu.HBM((CLUSTERS, ranks * SLOTS, 128), F32),
        compiler_params=params(16),
        cost_estimate=cost(1, 1),
    )(target)


def place_pair_kernel(target_ref, q_ref, k_ref, q_out, k_out, right):
    slots = q_out.shape[0] * SLOTS
    step = 1024
    right[:, :128] = q_ref[0]
    right[:, 128:] = k_ref[0]
    target = target_ref[0]

    def move(i, carry):
        picked = match(i * step, step, target).astype(BF16)
        out = jnp.dot(picked, right[...], preferred_element_type=F32)
        where = pl.ds(i * (step // SLOTS), step // SLOTS)
        q_out[where] = by_slot(out[:, :128]).astype(BF16)
        k_out[where] = by_slot(out[:, 128:]).astype(BF16)
        return carry

    lax.fori_loop(0, slots // step, move, 0)


def place_pair(target, first, tokens):
    ranks = first.shape[0]
    spec_out = pl.BlockSpec((CLUSTERS, SLOTS, 128), lambda j: (0, j, 0))
    shape = (CLUSTERS, ranks * SLOTS, 128)
    return pl.pallas_call(
        place_pair_kernel,
        grid=(ranks,),
        in_specs=[
            pl.BlockSpec((1, 1, tokens), lambda j: (j, 0, 0)),
            pl.BlockSpec((1, tokens, 128), lambda j: (j, 0, 0)),
            pl.BlockSpec((1, tokens, 128), lambda j: (j, 1, 0)),
        ],
        out_specs=[spec_out, spec_out],
        out_shape=[jax.ShapeDtypeStruct(shape, BF16), jax.ShapeDtypeStruct(shape, BF16)],
        scratch_shapes=[pltpu.VMEM((tokens, 256), BF16)],
        compiler_params=params(16),
        cost_estimate=cost(1, 1),
    )(target, first, first)


def weigh_kernel(q_ref, k_ref, p_ref, w_out, mean_out):
    count, rows = q_ref.shape[0], q_ref.shape[1]
    cap = rows // PAIR
    scale = 1.0 / math.sqrt(q_ref.shape[2])
    same = (
        lax.broadcasted_iota(jnp.int32, (rows, rows), 0) // cap
        == lax.broadcasted_iota(jnp.int32, (rows, rows), 1) // cap
    )
    for n in range(count):
        q, k, own = q_ref[n], k_ref[n], p_ref[n]
        scores = lax.dot_general(q, k, (((1,), (1,)), ((), ())), preferred_element_type=F32) * scale
        allowed = same & (jnp.transpose(own) <= own)
        scores = jnp.where(allowed, scores, neg_fill)
        top = jnp.max(scores, axis=1, keepdims=True)
        w_out[n] = jnp.where(allowed, jnp.exp(scores - top), 0.0).astype(BF16)
    both = (q_ref[...].astype(F32) + k_ref[...].astype(F32)).reshape(count * PAIR, cap, 128)
    held = (p_ref[...] < EMPTY).astype(F32).reshape(count * PAIR, cap, 128)
    mean_out[...] = jnp.sum(both, axis=1) / (2.0 * jnp.maximum(jnp.sum(held, axis=1), 1.0))


def weigh(q_rows, k_rows, at):
    groups, rows = q_rows.shape[0], q_rows.shape[1]
    step = 8
    spec = pl.BlockSpec((step, rows, 128), lambda i: (i, 0, 0))
    return pl.pallas_call(
        weigh_kernel,
        grid=(groups // step,),
        in_specs=[spec, spec, spec],
        out_specs=[
            pl.BlockSpec((step, rows, rows), lambda i: (i, 0, 0)),
            pl.BlockSpec((step * PAIR, 128), lambda i: (i, 0)),
        ],
        out_shape=[
            pltpu.HBM((groups, rows, rows), BF16),
            jax.ShapeDtypeStruct((groups * PAIR, 128), F32),
        ],
        compiler_params=params(12),
        cost_estimate=cost(1, 1),
    )(q_rows, k_rows, at)


def mix_kernel(ranks, target_ref, v_ref, w_ref, o_out, v_rows):
    i = pl.program_id(0)
    slots = v_rows.shape[0] * SLOTS
    count, rows = w_ref.shape[0], w_ref.shape[1]

    @pl.when(i < ranks)
    def _():
        picked = match(0, slots, target_ref[0]).astype(BF16)
        out = jnp.dot(picked, v_ref[0], preferred_element_type=F32)
        where = pl.ds(pl.multiple_of(i * SLOTS, SLOTS), SLOTS)
        v_rows[:, where, :] = by_slot(out)

    @pl.when(i >= ranks)
    def _():
        ones = jnp.ones((rows, 128), BF16)
        for n in range(count):
            own = v_rows[pl.ds(((i - ranks) * count + n) * PAIR, PAIR)]
            right = jnp.concatenate([own.reshape(rows, 128).astype(BF16), ones], axis=1)
            out = jnp.dot(w_ref[n], right, preferred_element_type=F32)
            total = out[:, 128:]
            o_out[n] = (out[:, :128] / jnp.where(total > 0.0, total, 1.0)).astype(BF16)


def mix(target, rows_v, weights):
    ranks, tokens = rows_v.shape[0], rows_v.shape[1]
    groups, rows = weights.shape[0], weights.shape[1]
    count = groups // ranks

    def sender(i):
        return jnp.minimum(i, ranks - 1)

    def group(i):
        return jnp.maximum(i - ranks, 0)

    return pl.pallas_call(
        functools.partial(mix_kernel, ranks),
        grid=(2 * ranks,),
        in_specs=[
            pl.BlockSpec((1, 1, tokens), lambda i: (sender(i), 0, 0)),
            pl.BlockSpec((1, tokens, 128), lambda i: (sender(i), 0, 0)),
            pl.BlockSpec((count, rows, rows), lambda i: (group(i), 0, 0)),
        ],
        out_specs=pl.BlockSpec((count, rows, 128), lambda i: (group(i), 0, 0)),
        out_shape=jax.ShapeDtypeStruct((groups, rows, 128), BF16),
        scratch_shapes=[pltpu.VMEM((CLUSTERS, ranks * SLOTS, 128), F32)],
        compiler_params=params(20),
        cost_estimate=cost(1, 1),
    )(target, rows_v, weights)


def unplace_kernel(who_ref, target_ref, o_ref, mean_ref, out_ref):
    tokens = target_ref.shape[2]
    slots = o_ref.shape[0] * SLOTS
    right = o_ref[...].astype(F32).reshape(slots, 128).astype(BF16)
    target = jnp.transpose(jnp.broadcast_to(target_ref[0], (128, tokens)))
    columns = lax.broadcasted_iota(jnp.int32, (tokens, slots), 1)
    picked = (columns == jnp.tile(target, (1, slots // 128))).astype(BF16)
    out_ref[0, :tokens] = jnp.dot(picked, right, preferred_element_type=F32).astype(BF16)
    means = mean_ref[...]
    high = means.astype(BF16)
    count = means.shape[0]
    out_ref[0, tokens : tokens + count] = high
    out_ref[0, tokens + count :] = (means - high.astype(F32)).astype(BF16)


def unplace(who, target, mixed, means):
    tokens, partners = target.shape[2], who.shape[0]
    count = CLUSTERS // target.shape[0]
    return pl.pallas_call(
        unplace_kernel,
        grid_spec=pltpu.PrefetchScalarGridSpec(
            num_scalar_prefetch=1,
            grid=(partners,),
            in_specs=[
                pl.BlockSpec((1, 1, tokens), lambda i, who: (who[i], 0, 0)),
                pl.BlockSpec((CLUSTERS, SLOTS, 128), lambda i, who: (0, who[i], 0)),
                pl.BlockSpec((count, 128), lambda i, who: (who[i], 0)),
            ],
            out_specs=pl.BlockSpec((1, tokens + 2 * count, 128), lambda i, who: (i, 0, 0)),
        ),
        out_shape=jax.ShapeDtypeStruct((partners, tokens + 2 * count, 128), BF16),
        compiler_params=params(12),
        cost_estimate=cost(1, 1),
    )(who, target, mixed, means)


def head_body(queries, keys, values, cluster_of, slot_of, centroids, out_weight):
    ranks = lax.axis_size("ctx")
    me = lax.axis_index("ctx")
    mine = lax.axis_index("head")
    tokens = queries.shape[0]
    cl_dev = CLUSTERS // ranks
    cap = ranks * SLOTS
    y, core = mine // 2, mine % 2

    def swap_y(x):
        return lax.ppermute(x, "head", [(0, 2), (1, 3), (2, 0), (3, 1)])

    def swap_core(x):
        return lax.ppermute(x, "head", [(0, 1), (1, 0), (2, 3), (3, 2)])

    def after(x, *others):
        return lax.optimization_barrier((x, others))[0]

    def swap_ctx(x, d):
        return lax.ppermute(x, "ctx", [(i, i ^ d) for i in range(ranks)])

    def exchange(x):
        return lax.all_to_all(x, "ctx", split_axis=0, concat_axis=0, tiled=True)

    places = lax.all_gather(cluster_of * SLOTS + slot_of, "ctx", axis=0, tiled=False)
    target = lax.dynamic_index_in_dim(places, me, 1, True)
    first = exchange(pack((queries, keys)))
    at = positions(target)

    cols = out_weight.shape[1] // 4
    heads = me ^ jnp.arange(ranks, dtype=jnp.int32)
    across = swap_y(lax.dynamic_slice_in_dim(out_weight, (1 - y) * 2 * cols, 2 * cols, 1))
    beside = swap_core(
        lax.dynamic_slice_in_dim(out_weight, (2 * y + 1 - core) * cols, cols, 1)
    )
    corner = swap_core(lax.dynamic_slice_in_dim(across, (1 - core) * cols, cols, 1))
    groups = ((0, 1, 2, 3), (4, 5), (6, 7))
    w_same = pick(heads, out_weight, across, (mine, core), groups, cols)
    w_core = pick(heads, beside, corner, (0 * core, 0 * core), groups, cols)

    rows_v = exchange(after(pack((values,)), first, at))

    def paired(x):
        return x.reshape(CLUSTERS // PAIR, PAIR * cap, 128)

    q_rows, k_rows = place_pair(target, first, tokens)
    at = pltpu.with_memory_space_constraint(paired(at), pltpu.HBM)
    weights, means = weigh(paired(q_rows), paired(k_rows), at)
    weights = pltpu.with_memory_space_constraint(weights, pltpu.HBM)
    rows_v = after(rows_v, w_same, w_core)
    mixed = mix(target, rows_v, weights).reshape(CLUSTERS, cap, 128)

    got, sent = {}, {}

    def leave(d, *others):
        block = unplace(after(jnp.reshape(me ^ d, (1,)), *others), target, mixed, means)
        sent[d] = block.reshape(block.shape[1:])

    def go(d):
        got[d] = swap_ctx(sent[d], d)

    def side(*blocks):
        return jnp.concatenate([block[:tokens] for block in blocks], axis=1)

    leave(4)
    go(4)
    leave(5, sent[4])
    go(5)
    leave(0, sent[5])
    got[0] = sent[0]
    y_0 = swap_y(got[0])
    leave(1, sent[0])
    go(1)
    leave(2, sent[1])
    go(2)
    leave(3, sent[2], y_0)
    go(3)
    leave(6, sent[3], got[4])
    go(6)
    own_123 = side(*[got[d] for d in (1, 2, 3)])
    leave(7, sent[6], got[5], own_123)
    go(7)
    own, there = {}, {}
    y_123 = swap_y(own_123)
    own[2] = side(got[4], got[5])
    there[2] = swap_y(own[2])
    own[3] = side(got[6], got[7])
    there[3] = swap_y(own[3])
    same = {1: side(got[0], own_123, y_0, y_123), 2: side(own[2], there[2])}

    def add(total, left, weight, row):
        more = jnp.dot(left, weight[row : row + left.shape[1]], preferred_element_type=F32)
        return more if total is None else total + more

    total = None
    for n, row in ((1, 0), (2, 1024)):
        total = add(total, same[n], w_same, row)
        total = add(total, swap_core(same[n]), w_core, row)
    row = 1536
    total = add(total, swap_core(own[3]), w_core, row)
    last = swap_core(after(there[3], total))
    total = add(total, side(own[3], there[3]), w_same, row)
    projected = add(total, last, w_core, row + 256).astype(BF16)

    tails = jnp.stack([got[d][tokens:] for d in range(ranks)]).astype(F32)
    tails = tails[:, :cl_dev] + tails[:, cl_dev:]
    tails = jnp.concatenate(
        [lax.dynamic_slice_in_dim(tails, me ^ d, 1, 0) for d in range(ranks)], axis=0
    )
    new_centroids = mix_rate * centroids + (1.0 - mix_rate) * tails
    return (projected, new_centroids)


def dispatch(queries, keys, values, cluster_of, *rest):
    ranks, heads = lax.axis_size("ctx"), cluster_of.shape[0]
    whole_heads = ranks == heads == 8 and lax.axis_size("head") == 4
    step = head_body if whole_heads else body
    return step(queries, keys, values, cluster_of, *rest)


def solution(mesh):
    in_specs = (
        P("ctx", "head"),
        P("ctx", "head"),
        P("ctx", "head"),
        P("head", "ctx"),
        P("head", "ctx"),
        P("head", "ctx", None),
        P("head", None),
    )
    out_specs = (P("ctx", "head"), P("head", "ctx", None))
    return jax.shard_map(
        dispatch, mesh=mesh, in_specs=in_specs, out_specs=out_specs, check_vma=False
    )
```

```python
import functools
import math

import jax
import jax.numpy as jnp
from jax import lax
from jax.experimental import pallas as pl
from jax.experimental.pallas import tpu as pltpu
from jax.sharding import PartitionSpec as P

CLUSTERS = 256
SLOTS = 8


mix_rate = 0.5
neg_fill = -1e30


def attend(q_rows, k_rows, v_rows, positions):
    scale = 1.0 / math.sqrt(q_rows.shape[-1])
    scores = jnp.einsum("gqd,gkd->gqk", q_rows, k_rows, preferred_element_type=jnp.float32) * scale
    allowed = (positions[:, None, :] >= 0) & (positions[:, None, :] <= positions[:, :, None])
    scores = jnp.where(allowed, scores, neg_fill)
    top = jnp.max(scores, axis=2, keepdims=True)
    weights = jnp.where(allowed, jnp.exp(scores - top), 0.0).astype(jnp.bfloat16)
    total = jnp.sum(weights.astype(jnp.float32), axis=2, keepdims=True)
    mixed = jnp.einsum("gqk,gkd->gqd", weights, v_rows, preferred_element_type=jnp.float32)
    return (mixed / jnp.where(total > 0.0, total, 1.0)).astype(jnp.bfloat16)


def to_clusters(rows, cl_dev):
    senders, width, items = (rows.shape[0], rows.shape[1], rows.shape[2])
    slots = width // cl_dev
    shaped = rows.reshape((senders, cl_dev, slots, items) + rows.shape[3:])
    if rows.ndim == 4:
        order = (3, 1, 0, 2, 4)
    else:
        order = (3, 1, 0, 2)
    return jnp.transpose(shaped, order).reshape((items * cl_dev, senders * slots) + rows.shape[3:])


def from_clusters(mixed, senders, cl_dev, items):
    slots = mixed.shape[1] // senders
    shaped = mixed.reshape(items, cl_dev, senders, slots, mixed.shape[2])
    return jnp.transpose(shaped, (2, 1, 3, 0, 4)).reshape(
        senders, cl_dev * slots, items, mixed.shape[2]
    )


def owner_work(incoming, cl_dev):
    q_in, k_in, v_in, p_in = incoming
    senders, items = (q_in.shape[0], q_in.shape[2])
    q_rows = to_clusters(q_in, cl_dev)
    k_rows = to_clusters(k_in, cl_dev)
    v_rows = to_clusters(v_in, cl_dev)
    p_rows = to_clusters(p_in, cl_dev)
    mixed = attend(q_rows, k_rows, v_rows, p_rows)
    back = from_clusters(mixed, senders, cl_dev, items)
    return back


def body(queries, keys, values, cluster_of, slot_of, centroids, out_weight):
    ranks = lax.axis_size("ctx")
    rank_here = lax.axis_index("ctx")
    tok_rows = queries.shape[0]
    head_rows = cluster_of.shape[0]
    head_size = queries.shape[1] // head_rows
    cl_dev = CLUSTERS // ranks
    width = CLUSTERS * SLOTS
    target = jnp.transpose(cluster_of * SLOTS + slot_of)
    head_ids = jnp.broadcast_to(jnp.arange(head_rows, dtype=jnp.int32)[None, :], target.shape)

    def place(rows):
        shaped = rows.reshape(tok_rows, head_rows, head_size)
        filled = (
            jnp.zeros((width, head_rows, head_size), rows.dtype).at[target, head_ids].set(shaped)
        )
        return filled.reshape(ranks, width // ranks, head_rows, head_size)

    token_pos = rank_here * tok_rows + jnp.arange(tok_rows, dtype=jnp.int32)
    pos_slots = (
        jnp.full((width, head_rows), -1, jnp.int32)
        .at[target, head_ids]
        .set(jnp.broadcast_to(token_pos[:, None], target.shape))
    )
    pos_slots = pos_slots.reshape(ranks, width // ranks, head_rows)
    incoming = (
        lax.all_to_all(place(queries), "ctx", split_axis=0, concat_axis=0, tiled=True),
        lax.all_to_all(place(keys), "ctx", split_axis=0, concat_axis=0, tiled=True),
        lax.all_to_all(place(values), "ctx", split_axis=0, concat_axis=0, tiled=True),
        lax.all_to_all(pos_slots, "ctx", split_axis=0, concat_axis=0, tiled=True),
    )
    worked = owner_work(incoming, cl_dev)
    returned = lax.all_to_all(worked, "ctx", split_axis=0, concat_axis=0, tiled=True)
    rows_back = returned.reshape(width, head_rows, head_size)
    attended = rows_back[target, head_ids].reshape(tok_rows, head_rows * head_size)
    member = (
        cluster_of[:, :, None] == jnp.arange(CLUSTERS, dtype=jnp.int32)[None, None, :]
    ).astype(jnp.bfloat16)
    q_three = queries.reshape(tok_rows, head_rows, head_size)
    k_three = keys.reshape(tok_rows, head_rows, head_size)
    local_sums = jnp.einsum("htc,thd->hcd", member, q_three, preferred_element_type=jnp.float32)
    local_sums = local_sums + jnp.einsum(
        "htc,thd->hcd", member, k_three, preferred_element_type=jnp.float32
    )
    local_counts = jnp.sum(member, axis=1, dtype=jnp.float32)
    totals, counts = (
        lax.psum_scatter(
            local_sums.astype(jnp.bfloat16), "ctx", scatter_dimension=1, tiled=True
        ).astype(jnp.float32),
        lax.psum_scatter(
            local_counts.astype(jnp.bfloat16), "ctx", scatter_dimension=1, tiled=True
        ).astype(jnp.float32),
    )
    means = totals / (2.0 * jnp.maximum(counts, 1.0))[:, :, None]
    new_centroids = mix_rate * centroids + (1.0 - mix_rate) * means
    summed = lax.psum_scatter(
        lax.dot_general(
            out_weight, attended, (((0,), (1,)), ((), ())), preferred_element_type=jnp.float32
        ),
        "head",
        scatter_dimension=0,
        tiled=True,
    )
    projected = jnp.transpose(summed).astype(jnp.bfloat16)
    return (projected, new_centroids)


BF16 = jnp.bfloat16
F32 = jnp.float32
PAIR = 2
EMPTY = 1e9


def params(limit):
    return pltpu.CompilerParams(
        dimension_semantics=("arbitrary",), vmem_limit_bytes=limit * 1024 * 1024
    )


def cost(flops, nbytes, transcendentals=0):
    return pl.CostEstimate(
        flops=flops, bytes_accessed=nbytes, transcendentals=transcendentals
    )


def pack_kernel(count, marked, *refs):
    sources = refs[:count]
    out_ref, held, sems_in, sems_out = refs[count + marked :]
    heads = out_ref.shape[0]
    tokens = sources[0].shape[0]
    parts = 2
    rows = tokens // parts
    reads = []
    for n, source in enumerate(sources):
        for p in range(parts):
            here = pl.ds(p * rows, rows)
            reads.append(
                pltpu.make_async_copy(
                    source.at[here], held.at[n, here], sems_in.at[n * parts + p]
                )
            )
    for copy in reads:
        copy.start()
    writes = []
    if marked:
        marks_ref = refs[count]
        there = out_ref.at[:, pl.ds(count * tokens, marks_ref.shape[1])]
        writes.append(pltpu.make_async_copy(marks_ref, there, sems_out.at[0]))
        writes[0].start()
    for n in range(count):
        for p in range(parts):
            reads[n * parts + p].wait()
            for j in range(heads):
                copy = pltpu.make_async_copy(
                    held.at[n, pl.ds(p * rows, rows), pl.ds(j * 128, 128)],
                    out_ref.at[j, pl.ds(n * tokens + p * rows, rows)],
                    sems_out.at[1 + (n * parts + p) * heads + j],
                )
                copy.start()
                writes.append(copy)
    for copy in writes:
        copy.wait()


def pack(sources, marks=None):
    tokens, width = sources[0].shape
    heads, count = width // 128, len(sources)
    marked = marks is not None
    rows = count * tokens + (marks.shape[1] if marked else 0)
    anywhere = pl.BlockSpec(memory_space=pl.ANY)
    args = list(sources)
    in_specs = [anywhere] * count
    if marked:
        args.append(marks)
        in_specs.append(pl.BlockSpec(memory_space=pltpu.VMEM))
    return pl.pallas_call(
        functools.partial(pack_kernel, count, marked),
        in_specs=in_specs,
        out_specs=anywhere,
        out_shape=pltpu.HBM((heads, rows, 128), BF16),
        scratch_shapes=[
            pltpu.VMEM((count, tokens, width), BF16),
            pltpu.SemaphoreType.DMA((2 * count,)),
            pltpu.SemaphoreType.DMA((2 * count * heads + 1,)),
        ],
        compiler_params=pltpu.CompilerParams(vmem_limit_bytes=60 * 1024 * 1024),
        cost_estimate=cost(0, 2 * heads * rows * 256),
    )(*args)


def pick_kernel(plan, where_ref, *refs):
    sources, out_ref, sems = refs[:-2], refs[-2], refs[-1]
    count = where_ref.shape[0] - len(sources)
    cols = out_ref.shape[1]
    copies = []
    for n, (part, lane) in enumerate(plan):
        row = pl.multiple_of(where_ref[lane] * 128, 128)
        column = pl.multiple_of(where_ref[count + part] * cols, cols)
        copies.append(
            pltpu.make_async_copy(
                sources[part].at[pl.ds(row, 128), pl.ds(column, cols)],
                out_ref.at[pl.ds(n * 128, 128)],
                sems.at[n],
            )
        )
    for copy in copies:
        copy.start()
    for copy in copies:
        copy.wait()


def pick(heads, weights, columns, groups, cols):
    plan = [(part, d) for group in groups for part in range(len(weights)) for d in group]
    where = jnp.concatenate([heads, jnp.stack(columns)])
    return pl.pallas_call(
        functools.partial(pick_kernel, plan),
        in_specs=[pl.BlockSpec(memory_space=pltpu.SMEM)]
        + [pl.BlockSpec(memory_space=pl.ANY)] * len(weights),
        out_specs=pl.BlockSpec(memory_space=pltpu.VMEM),
        out_shape=jax.ShapeDtypeStruct((128 * len(plan), cols), BF16),
        scratch_shapes=[pltpu.SemaphoreType.DMA((len(plan),))],
        compiler_params=pltpu.CompilerParams(vmem_limit_bytes=56 * 1024 * 1024),
        cost_estimate=cost(1, 1),
    )(where, *weights)


def match(first, count, target):
    rows = first + lax.broadcasted_iota(jnp.int32, (count, target.shape[1]), 0)
    return rows == target


def by_slot(x):
    return x.reshape(x.shape[0] // SLOTS, SLOTS, 128)


def place_pair_kernel(target_ref, q_ref, k_ref, q_out, k_out, p_out, right):
    tokens = q_ref.shape[1]
    slots = q_out.shape[0] * SLOTS
    step = 1024
    right[:, :128] = q_ref[0]
    right[:, 128:] = k_ref[0]
    base = pl.program_id(0) * tokens
    token = (base + lax.broadcasted_iota(jnp.int32, (1, tokens), 1)).astype(F32)
    target = target_ref[0]

    def move(i, carry):
        picked = match(i * step, step, target)
        out = jnp.dot(picked.astype(BF16), right[...], preferred_element_type=F32)
        where = pl.ds(i * (step // SLOTS), step // SLOTS)
        q_out[where] = by_slot(out[:, :128]).astype(BF16)
        k_out[where] = by_slot(out[:, 128:]).astype(BF16)
        at = jnp.min(jnp.where(picked, token, EMPTY), axis=1, keepdims=True)
        p_out[where] = by_slot(jnp.broadcast_to(at, (step, 128)))
        return carry

    lax.fori_loop(0, slots // step, move, 0)


def place_pair(target, first, tokens):
    ranks = first.shape[0]
    spec_out = pl.BlockSpec((CLUSTERS, SLOTS, 128), lambda j: (0, j, 0))
    shape = (CLUSTERS, ranks * SLOTS, 128)
    return pl.pallas_call(
        place_pair_kernel,
        grid=(ranks,),
        in_specs=[
            pl.BlockSpec((1, 1, tokens), lambda j: (j, 0, 0)),
            pl.BlockSpec((1, tokens, 128), lambda j: (j, 0, 0)),
            pl.BlockSpec((1, tokens, 128), lambda j: (j, 1, 0)),
        ],
        out_specs=[spec_out, spec_out, spec_out],
        out_shape=[
            jax.ShapeDtypeStruct(shape, BF16),
            jax.ShapeDtypeStruct(shape, BF16),
            jax.ShapeDtypeStruct(shape, F32),
        ],
        scratch_shapes=[pltpu.VMEM((tokens, 256), BF16)],
        compiler_params=params(16),
        cost_estimate=cost(1, 1),
    )(target, first, first)


def weigh_kernel(q_ref, k_ref, p_ref, w_out, mean_out):
    count, rows = q_ref.shape[0], q_ref.shape[1]
    cap = rows // PAIR
    scale = 1.0 / math.sqrt(q_ref.shape[2])
    same = (
        lax.broadcasted_iota(jnp.int32, (rows, rows), 0) // cap
        == lax.broadcasted_iota(jnp.int32, (rows, rows), 1) // cap
    )
    for n in range(count):
        q, k, own = q_ref[n], k_ref[n], p_ref[n]
        scores = lax.dot_general(q, k, (((1,), (1,)), ((), ())), preferred_element_type=F32) * scale
        allowed = same & (jnp.transpose(own) <= own)
        scores = jnp.where(allowed, scores, neg_fill)
        top = jnp.max(scores, axis=1, keepdims=True)
        w_out[n] = jnp.where(allowed, jnp.exp(scores - top), 0.0).astype(BF16)
    both = (q_ref[...].astype(F32) + k_ref[...].astype(F32)).reshape(count * PAIR, cap, 128)
    held = (p_ref[...] < EMPTY).astype(F32).reshape(count * PAIR, cap, 128)
    mean_out[...] = jnp.sum(both, axis=1) / (2.0 * jnp.maximum(jnp.sum(held, axis=1), 1.0))


def weigh(q_rows, k_rows, at):
    groups, rows = q_rows.shape[0], q_rows.shape[1]
    step = 8
    spec = pl.BlockSpec((step, rows, 128), lambda i: (i, 0, 0))
    return pl.pallas_call(
        weigh_kernel,
        grid=(groups // step,),
        in_specs=[spec, spec, spec],
        out_specs=[
            pl.BlockSpec((step, rows, rows), lambda i: (i, 0, 0)),
            pl.BlockSpec((step * PAIR, 128), lambda i: (i, 0)),
        ],
        out_shape=[
            pltpu.HBM((groups, rows, rows), BF16),
            jax.ShapeDtypeStruct((groups * PAIR, 128), F32),
        ],
        compiler_params=params(12),
        cost_estimate=cost(1, 1),
    )(q_rows, k_rows, at)


def mix_kernel(ranks, target_ref, v_ref, w_ref, o_out, v_rows):
    i = pl.program_id(0)
    slots = v_rows.shape[0] * SLOTS
    count, rows = w_ref.shape[0], w_ref.shape[1]

    @pl.when(i < ranks)
    def _():
        picked = match(0, slots, target_ref[0]).astype(BF16)
        out = jnp.dot(picked, v_ref[0], preferred_element_type=F32)
        where = pl.ds(pl.multiple_of(i * SLOTS, SLOTS), SLOTS)
        v_rows[:, where, :] = by_slot(out)

    @pl.when(i >= ranks)
    def _():
        ones = jnp.ones((rows, 128), BF16)
        for n in range(count):
            own = v_rows[pl.ds(((i - ranks) * count + n) * PAIR, PAIR)]
            right = jnp.concatenate([own.reshape(rows, 128).astype(BF16), ones], axis=1)
            out = jnp.dot(w_ref[n], right, preferred_element_type=F32)
            total = out[:, 128:]
            o_out[n] = (out[:, :128] / jnp.where(total > 0.0, total, 1.0)).astype(BF16)


def mix(target, rows_v, weights):
    ranks, tokens = rows_v.shape[0], rows_v.shape[1]
    groups, rows = weights.shape[0], weights.shape[1]
    count = groups // ranks

    def sender(i):
        return jnp.minimum(i, ranks - 1)

    def group(i):
        return jnp.maximum(i - ranks, 0)

    return pl.pallas_call(
        functools.partial(mix_kernel, ranks),
        grid=(2 * ranks,),
        in_specs=[
            pl.BlockSpec((1, 1, tokens), lambda i: (sender(i), 0, 0)),
            pl.BlockSpec((1, tokens, 128), lambda i: (sender(i), 0, 0)),
            pl.BlockSpec((count, rows, rows), lambda i: (group(i), 0, 0)),
        ],
        out_specs=pl.BlockSpec((count, rows, 128), lambda i: (group(i), 0, 0)),
        out_shape=jax.ShapeDtypeStruct((groups, rows, 128), BF16),
        scratch_shapes=[pltpu.VMEM((CLUSTERS, ranks * SLOTS, 128), F32)],
        compiler_params=params(20),
        cost_estimate=cost(1, 1),
    )(target, rows_v, weights)


def unplace_kernel(who_ref, target_ref, o_ref, mean_ref, out_ref):
    tokens = target_ref.shape[2]
    slots = o_ref.shape[0] * SLOTS
    right = o_ref[...].astype(F32).reshape(slots, 128).astype(BF16)
    target = jnp.transpose(jnp.broadcast_to(target_ref[0], (128, tokens)))
    columns = lax.broadcasted_iota(jnp.int32, (tokens, slots), 1)
    picked = (columns == jnp.tile(target, (1, slots // 128))).astype(BF16)
    out_ref[0, :tokens] = jnp.dot(picked, right, preferred_element_type=F32).astype(BF16)
    means = mean_ref[...]
    high = means.astype(BF16)
    count = means.shape[0]
    out_ref[0, tokens : tokens + count] = high
    out_ref[0, tokens + count :] = (means - high.astype(F32)).astype(BF16)


def unplace(who, target, mixed, means):
    tokens, partners = target.shape[2], who.shape[0]
    count = CLUSTERS // target.shape[0]
    return pl.pallas_call(
        unplace_kernel,
        grid_spec=pltpu.PrefetchScalarGridSpec(
            num_scalar_prefetch=1,
            grid=(partners,),
            in_specs=[
                pl.BlockSpec((1, 1, tokens), lambda i, who: (who[i], 0, 0)),
                pl.BlockSpec((CLUSTERS, SLOTS, 128), lambda i, who: (0, who[i], 0)),
                pl.BlockSpec((count, 128), lambda i, who: (who[i], 0)),
            ],
            out_specs=pl.BlockSpec((1, tokens + 2 * count, 128), lambda i, who: (i, 0, 0)),
        ),
        out_shape=jax.ShapeDtypeStruct((partners, tokens + 2 * count, 128), BF16),
        compiler_params=params(12),
        cost_estimate=cost(1, 1),
    )(who, target, mixed, means)


def head_body(queries, keys, values, cluster_of, slot_of, centroids, out_weight):
    ranks = lax.axis_size("ctx")
    me = lax.axis_index("ctx")
    mine = lax.axis_index("head")
    tokens = queries.shape[0]
    cl_dev = CLUSTERS // ranks
    cap = ranks * SLOTS
    y, core = mine // 2, mine % 2

    def swap_y(x):
        return lax.ppermute(x, "head", [(0, 2), (1, 3), (2, 0), (3, 1)])

    def swap_core(x):
        return lax.ppermute(x, "head", [(0, 1), (1, 0), (2, 3), (3, 2)])

    def after(x, *others):
        return lax.optimization_barrier((x, others))[0]

    def swap_ctx(x, d):
        return lax.ppermute(x, "ctx", [(i, i ^ d) for i in range(ranks)])

    def exchange(x):
        return lax.all_to_all(x, "ctx", split_axis=0, concat_axis=0, tiled=True)

    marks = [x.astype(BF16).reshape(ranks, tokens // 128, 128) for x in (cluster_of, slot_of)]
    first = exchange(pack((queries, keys), jnp.concatenate(marks, axis=1)))
    marks = first[:, 2 * tokens :, :].astype(jnp.int32)
    target = marks[:, : tokens // 128, :] * SLOTS + marks[:, tokens // 128 :, :]
    target = target.reshape(ranks, 1, tokens)

    cols = out_weight.shape[1] // 4
    heads = me ^ jnp.arange(ranks, dtype=jnp.int32)
    across = swap_y(lax.dynamic_slice_in_dim(out_weight, (1 - y) * 2 * cols, 2 * cols, 1))
    beside = swap_core(
        lax.dynamic_slice_in_dim(out_weight, (2 * y + 1 - core) * cols, cols, 1)
    )
    corner = swap_core(lax.dynamic_slice_in_dim(across, (1 - core) * cols, cols, 1))
    groups = ((0, 1, 2, 3), (4, 5), (6, 7))
    zero = jnp.zeros_like(core)
    weight = pick(
        heads, (out_weight, across, beside, corner), (mine, core, zero, zero), groups, cols
    )
    rows_v = exchange(after(pack((values,)), first))

    def paired(x):
        return x.reshape(CLUSTERS // PAIR, PAIR * cap, 128)

    q_rows, k_rows, at = place_pair(target, first, tokens)
    weights, means = weigh(paired(q_rows), paired(k_rows), paired(at))
    weights = pltpu.with_memory_space_constraint(weights, pltpu.HBM)
    rows_v = after(rows_v, weight)
    mixed = mix(target, rows_v, weights).reshape(CLUSTERS, cap, 128)

    got, sent = {}, {}

    def leave(d, *others):
        block = unplace(after(jnp.reshape(me ^ d, (1,)), *others), target, mixed, means)
        sent[d] = block.reshape(block.shape[1:])

    def go(d):
        got[d] = swap_ctx(sent[d], d)

    def side(*blocks):
        return jnp.concatenate([block[:tokens] for block in blocks], axis=1)

    leave(4)
    go(4)
    leave(5, sent[4])
    go(5)
    leave(0, sent[5])
    got[0] = sent[0]
    y_0 = swap_y(got[0])
    leave(1, sent[0])
    go(1)
    leave(2, sent[1])
    go(2)
    leave(3, sent[2], y_0)
    go(3)
    leave(6, sent[3], got[4])
    go(6)
    own_123 = side(*[got[d] for d in (1, 2, 3)])
    leave(7, sent[6], got[5], own_123)
    go(7)
    own, there = {}, {}
    y_123 = swap_y(own_123)
    own[2] = side(got[4], got[5])
    there[2] = swap_y(own[2])
    own[3] = side(got[6], got[7])
    there[3] = swap_y(own[3])
    same = {1: side(got[0], own_123, y_0, y_123), 2: side(own[2], there[2])}

    def add(total, left, row):
        more = jnp.dot(left, weight[row : row + left.shape[1]], preferred_element_type=F32)
        return more if total is None else total + more

    total = None
    for n, row in ((1, 0), (2, 2048)):
        total = add(total, jnp.concatenate([same[n], swap_core(same[n])], axis=1), row)
    row = 3072
    total = add(total, swap_core(own[3]), row + 512)
    last = swap_core(after(there[3], total))
    total = add(total, side(own[3], there[3]), row)
    projected = add(total, last, row + 768).astype(BF16)

    tails = jnp.stack([got[d][tokens:] for d in range(ranks)]).astype(F32)
    tails = tails[:, :cl_dev] + tails[:, cl_dev:]
    tails = jnp.concatenate(
        [lax.dynamic_slice_in_dim(tails, me ^ d, 1, 0) for d in range(ranks)], axis=0
    )
    new_centroids = mix_rate * centroids + (1.0 - mix_rate) * tails
    return (projected, new_centroids)


def dispatch(queries, keys, values, cluster_of, *rest):
    ranks, heads = lax.axis_size("ctx"), cluster_of.shape[0]
    whole_heads = ranks == heads == 8 and lax.axis_size("head") == 4
    step = head_body if whole_heads else body
    return step(queries, keys, values, cluster_of, *rest)


def solution(mesh):
    in_specs = (
        P("ctx", "head"),
        P("ctx", "head"),
        P("ctx", "head"),
        P("head", "ctx"),
        P("head", "ctx"),
        P("head", "ctx", None),
        P("head", None),
    )
    out_specs = (P("ctx", "head"), P("head", "ctx", None))
    return jax.shard_map(
        dispatch, mesh=mesh, in_specs=in_specs, out_specs=out_specs, check_vma=False
    )
```

```python
import functools
import math

import jax
import jax.numpy as jnp
from jax import lax
from jax.experimental import pallas as pl
from jax.experimental.pallas import tpu as pltpu
from jax.sharding import PartitionSpec as P

CLUSTERS = 256
SLOTS = 8


mix_rate = 0.5
neg_fill = -1e30


def attend(q_rows, k_rows, v_rows, positions):
    scale = 1.0 / math.sqrt(q_rows.shape[-1])
    scores = jnp.einsum("gqd,gkd->gqk", q_rows, k_rows, preferred_element_type=jnp.float32) * scale
    allowed = (positions[:, None, :] >= 0) & (positions[:, None, :] <= positions[:, :, None])
    scores = jnp.where(allowed, scores, neg_fill)
    top = jnp.max(scores, axis=2, keepdims=True)
    weights = jnp.where(allowed, jnp.exp(scores - top), 0.0).astype(jnp.bfloat16)
    total = jnp.sum(weights.astype(jnp.float32), axis=2, keepdims=True)
    mixed = jnp.einsum("gqk,gkd->gqd", weights, v_rows, preferred_element_type=jnp.float32)
    return (mixed / jnp.where(total > 0.0, total, 1.0)).astype(jnp.bfloat16)


def to_clusters(rows, cl_dev):
    senders, width, items = (rows.shape[0], rows.shape[1], rows.shape[2])
    slots = width // cl_dev
    shaped = rows.reshape((senders, cl_dev, slots, items) + rows.shape[3:])
    if rows.ndim == 4:
        order = (3, 1, 0, 2, 4)
    else:
        order = (3, 1, 0, 2)
    return jnp.transpose(shaped, order).reshape((items * cl_dev, senders * slots) + rows.shape[3:])


def from_clusters(mixed, senders, cl_dev, items):
    slots = mixed.shape[1] // senders
    shaped = mixed.reshape(items, cl_dev, senders, slots, mixed.shape[2])
    return jnp.transpose(shaped, (2, 1, 3, 0, 4)).reshape(
        senders, cl_dev * slots, items, mixed.shape[2]
    )


def owner_work(incoming, cl_dev):
    q_in, k_in, v_in, p_in = incoming
    senders, items = (q_in.shape[0], q_in.shape[2])
    q_rows = to_clusters(q_in, cl_dev)
    k_rows = to_clusters(k_in, cl_dev)
    v_rows = to_clusters(v_in, cl_dev)
    p_rows = to_clusters(p_in, cl_dev)
    mixed = attend(q_rows, k_rows, v_rows, p_rows)
    back = from_clusters(mixed, senders, cl_dev, items)
    return back


def body(queries, keys, values, cluster_of, slot_of, centroids, out_weight):
    ranks = lax.axis_size("ctx")
    rank_here = lax.axis_index("ctx")
    tok_rows = queries.shape[0]
    head_rows = cluster_of.shape[0]
    head_size = queries.shape[1] // head_rows
    cl_dev = CLUSTERS // ranks
    width = CLUSTERS * SLOTS
    target = jnp.transpose(cluster_of * SLOTS + slot_of)
    head_ids = jnp.broadcast_to(jnp.arange(head_rows, dtype=jnp.int32)[None, :], target.shape)

    def place(rows):
        shaped = rows.reshape(tok_rows, head_rows, head_size)
        filled = (
            jnp.zeros((width, head_rows, head_size), rows.dtype).at[target, head_ids].set(shaped)
        )
        return filled.reshape(ranks, width // ranks, head_rows, head_size)

    token_pos = rank_here * tok_rows + jnp.arange(tok_rows, dtype=jnp.int32)
    pos_slots = (
        jnp.full((width, head_rows), -1, jnp.int32)
        .at[target, head_ids]
        .set(jnp.broadcast_to(token_pos[:, None], target.shape))
    )
    pos_slots = pos_slots.reshape(ranks, width // ranks, head_rows)
    incoming = (
        lax.all_to_all(place(queries), "ctx", split_axis=0, concat_axis=0, tiled=True),
        lax.all_to_all(place(keys), "ctx", split_axis=0, concat_axis=0, tiled=True),
        lax.all_to_all(place(values), "ctx", split_axis=0, concat_axis=0, tiled=True),
        lax.all_to_all(pos_slots, "ctx", split_axis=0, concat_axis=0, tiled=True),
    )
    worked = owner_work(incoming, cl_dev)
    returned = lax.all_to_all(worked, "ctx", split_axis=0, concat_axis=0, tiled=True)
    rows_back = returned.reshape(width, head_rows, head_size)
    attended = rows_back[target, head_ids].reshape(tok_rows, head_rows * head_size)
    member = (
        cluster_of[:, :, None] == jnp.arange(CLUSTERS, dtype=jnp.int32)[None, None, :]
    ).astype(jnp.bfloat16)
    q_three = queries.reshape(tok_rows, head_rows, head_size)
    k_three = keys.reshape(tok_rows, head_rows, head_size)
    local_sums = jnp.einsum("htc,thd->hcd", member, q_three, preferred_element_type=jnp.float32)
    local_sums = local_sums + jnp.einsum(
        "htc,thd->hcd", member, k_three, preferred_element_type=jnp.float32
    )
    local_counts = jnp.sum(member, axis=1, dtype=jnp.float32)
    totals, counts = (
        lax.psum_scatter(
            local_sums.astype(jnp.bfloat16), "ctx", scatter_dimension=1, tiled=True
        ).astype(jnp.float32),
        lax.psum_scatter(
            local_counts.astype(jnp.bfloat16), "ctx", scatter_dimension=1, tiled=True
        ).astype(jnp.float32),
    )
    means = totals / (2.0 * jnp.maximum(counts, 1.0))[:, :, None]
    new_centroids = mix_rate * centroids + (1.0 - mix_rate) * means
    summed = lax.psum_scatter(
        lax.dot_general(
            out_weight, attended, (((0,), (1,)), ((), ())), preferred_element_type=jnp.float32
        ),
        "head",
        scatter_dimension=0,
        tiled=True,
    )
    projected = jnp.transpose(summed).astype(jnp.bfloat16)
    return (projected, new_centroids)


BF16 = jnp.bfloat16
F32 = jnp.float32
PAIR = 2
EMPTY = 1e9


def params(limit):
    return pltpu.CompilerParams(
        dimension_semantics=("arbitrary",), vmem_limit_bytes=limit * 1024 * 1024
    )


def cost(flops, nbytes, transcendentals=0):
    return pl.CostEstimate(
        flops=flops, bytes_accessed=nbytes, transcendentals=transcendentals
    )


def pack_kernel(count, marked, *refs):
    sources = refs[:count]
    out_ref, held, sems_in, sems_out = refs[count + marked :]
    heads = out_ref.shape[0]
    tokens = sources[0].shape[0]
    parts = 2
    rows = tokens // parts
    reads = []
    for n, source in enumerate(sources):
        for p in range(parts):
            here = pl.ds(p * rows, rows)
            reads.append(
                pltpu.make_async_copy(
                    source.at[here], held.at[n, here], sems_in.at[n * parts + p]
                )
            )
    for copy in reads:
        copy.start()
    writes = []
    if marked:
        marks_ref = refs[count]
        there = out_ref.at[:, pl.ds(count * tokens, marks_ref.shape[1])]
        writes.append(pltpu.make_async_copy(marks_ref, there, sems_out.at[0]))
        writes[0].start()
    for n in range(count):
        for p in range(parts):
            reads[n * parts + p].wait()
            for j in range(heads):
                copy = pltpu.make_async_copy(
                    held.at[n, pl.ds(p * rows, rows), pl.ds(j * 128, 128)],
                    out_ref.at[j, pl.ds(n * tokens + p * rows, rows)],
                    sems_out.at[1 + (n * parts + p) * heads + j],
                )
                copy.start()
                writes.append(copy)
    for copy in writes:
        copy.wait()


def pack(sources, marks=None):
    tokens, width = sources[0].shape
    heads, count = width // 128, len(sources)
    marked = marks is not None
    rows = count * tokens + (marks.shape[1] if marked else 0)
    anywhere = pl.BlockSpec(memory_space=pl.ANY)
    args = list(sources)
    in_specs = [anywhere] * count
    if marked:
        args.append(marks)
        in_specs.append(pl.BlockSpec(memory_space=pltpu.VMEM))
    return pl.pallas_call(
        functools.partial(pack_kernel, count, marked),
        in_specs=in_specs,
        out_specs=anywhere,
        out_shape=pltpu.HBM((heads, rows, 128), BF16),
        scratch_shapes=[
            pltpu.VMEM((count, tokens, width), BF16),
            pltpu.SemaphoreType.DMA((2 * count,)),
            pltpu.SemaphoreType.DMA((2 * count * heads + 1,)),
        ],
        compiler_params=pltpu.CompilerParams(vmem_limit_bytes=60 * 1024 * 1024),
        cost_estimate=cost(0, 2 * heads * rows * 256),
    )(*args)


def pick_kernel(plan, where_ref, *refs):
    sources, out_ref, sems = refs[:-2], refs[-2], refs[-1]
    count = where_ref.shape[0] - len(sources)
    cols = out_ref.shape[1]
    copies = []
    for n, (part, lane) in enumerate(plan):
        row = pl.multiple_of(where_ref[lane] * 128, 128)
        column = pl.multiple_of(where_ref[count + part] * cols, cols)
        copies.append(
            pltpu.make_async_copy(
                sources[part].at[pl.ds(row, 128), pl.ds(column, cols)],
                out_ref.at[pl.ds(n * 128, 128)],
                sems.at[n],
            )
        )
    for copy in copies:
        copy.start()
    for copy in copies:
        copy.wait()


def pick(heads, weights, columns, groups, cols):
    plan = [(part, d) for group in groups for part in range(len(weights)) for d in group]
    where = jnp.concatenate([heads, jnp.stack(columns)])
    return pl.pallas_call(
        functools.partial(pick_kernel, plan),
        in_specs=[pl.BlockSpec(memory_space=pltpu.SMEM)]
        + [pl.BlockSpec(memory_space=pl.ANY)] * len(weights),
        out_specs=pl.BlockSpec(memory_space=pltpu.VMEM),
        out_shape=jax.ShapeDtypeStruct((128 * len(plan), cols), BF16),
        scratch_shapes=[pltpu.SemaphoreType.DMA((len(plan),))],
        compiler_params=pltpu.CompilerParams(vmem_limit_bytes=56 * 1024 * 1024),
        cost_estimate=cost(1, 1),
    )(where, *weights)


def match(first, count, target):
    rows = first + lax.broadcasted_iota(jnp.int32, (count, target.shape[1]), 0)
    return rows == target


def by_slot(x):
    return x.reshape(x.shape[0] // SLOTS, SLOTS, 128)


def place_pair_kernel(target_ref, q_ref, k_ref, q_out, k_out, p_out, right):
    tokens = q_ref.shape[1]
    slots = q_out.shape[0] * SLOTS
    step = 1024
    right[:, :128] = q_ref[0]
    right[:, 128:] = k_ref[0]
    base = pl.program_id(0) * tokens
    token = (base + lax.broadcasted_iota(jnp.int32, (1, tokens), 1)).astype(F32)
    target = target_ref[0]

    def move(i, carry):
        picked = match(i * step, step, target)
        out = jnp.dot(picked.astype(BF16), right[...], preferred_element_type=F32)
        where = pl.ds(i * (step // SLOTS), step // SLOTS)
        q_out[where] = by_slot(out[:, :128]).astype(BF16)
        k_out[where] = by_slot(out[:, 128:]).astype(BF16)
        at = jnp.min(jnp.where(picked, token, EMPTY), axis=1, keepdims=True)
        p_out[where] = by_slot(jnp.broadcast_to(at, (step, 128)))
        return carry

    lax.fori_loop(0, slots // step, move, 0)


def place_pair(target, first, tokens):
    ranks = first.shape[0]
    spec_out = pl.BlockSpec((CLUSTERS, SLOTS, 128), lambda j: (0, j, 0))
    shape = (CLUSTERS, ranks * SLOTS, 128)
    return pl.pallas_call(
        place_pair_kernel,
        grid=(ranks,),
        in_specs=[
            pl.BlockSpec((1, 1, tokens), lambda j: (j, 0, 0)),
            pl.BlockSpec((1, tokens, 128), lambda j: (j, 0, 0)),
            pl.BlockSpec((1, tokens, 128), lambda j: (j, 1, 0)),
        ],
        out_specs=[spec_out, spec_out, spec_out],
        out_shape=[
            jax.ShapeDtypeStruct(shape, BF16),
            jax.ShapeDtypeStruct(shape, BF16),
            jax.ShapeDtypeStruct(shape, F32),
        ],
        scratch_shapes=[pltpu.VMEM((tokens, 256), BF16)],
        compiler_params=params(16),
        cost_estimate=cost(1, 1),
    )(target, first, first)


def weigh_kernel(tokens, q_ref, k_ref, p_ref, w_out, mean_out, early_out):
    count, rows = q_ref.shape[0], q_ref.shape[1]
    cap = rows // PAIR
    scale = 1.0 / math.sqrt(q_ref.shape[2])
    same = (
        lax.broadcasted_iota(jnp.int32, (rows, rows), 0) // cap
        == lax.broadcasted_iota(jnp.int32, (rows, rows), 1) // cap
    )
    for n in range(count):
        q, k, own = q_ref[n], k_ref[n], p_ref[n]
        scores = lax.dot_general(q, k, (((1,), (1,)), ((), ())), preferred_element_type=F32) * scale
        allowed = same & (jnp.transpose(own) <= own)
        scores = jnp.where(allowed, scores, neg_fill)
        top = jnp.max(scores, axis=1, keepdims=True)
        w_out[n] = jnp.where(allowed, jnp.exp(scores - top), 0.0).astype(BF16)
    share = p_ref[...] * (1.0 / tokens)
    early_out[...] = (share - jnp.floor(share) < 0.5).astype(BF16)
    both = (q_ref[...].astype(F32) + k_ref[...].astype(F32)).reshape(count * PAIR, cap, 128)
    held = (p_ref[...] < EMPTY).astype(F32).reshape(count * PAIR, cap, 128)
    mean_out[...] = jnp.sum(both, axis=1) / (2.0 * jnp.maximum(jnp.sum(held, axis=1), 1.0))


def weigh(q_rows, k_rows, at, tokens):
    groups, rows = q_rows.shape[0], q_rows.shape[1]
    step = 8
    spec = pl.BlockSpec((step, rows, 128), lambda i: (i, 0, 0))
    return pl.pallas_call(
        functools.partial(weigh_kernel, tokens),
        grid=(groups // step,),
        in_specs=[spec, spec, spec],
        out_specs=[
            pl.BlockSpec((step, rows, rows), lambda i: (i, 0, 0)),
            pl.BlockSpec((step * PAIR, 128), lambda i: (i, 0)),
            spec,
        ],
        out_shape=[
            pltpu.HBM((groups, rows, rows), BF16),
            jax.ShapeDtypeStruct((groups * PAIR, 128), F32),
            pltpu.HBM((groups, rows, 128), BF16),
        ],
        compiler_params=params(12),
        cost_estimate=cost(1, 1),
    )(q_rows, k_rows, at)


def mix_kernel(ranks, target_ref, v_ref, early_ref, w_ref, o_out, v_rows):
    i = pl.program_id(0)
    slots = v_rows.shape[0] * SLOTS
    count, rows = w_ref.shape[0], w_ref.shape[1]
    tokens = v_ref.shape[1]
    half = tokens // 2

    @pl.when(i < ranks)
    def _():
        target = target_ref[0]
        picked = match(0, slots, target[:, :half]) | match(0, slots, target[:, half:])
        both = jnp.concatenate([v_ref[0, :half], v_ref[0, half:]], axis=1)
        out = jnp.dot(picked.astype(BF16), both, preferred_element_type=F32)
        early = early_ref[...].astype(F32) > 0.0
        where = pl.ds(pl.multiple_of(i * SLOTS, SLOTS), SLOTS)
        v_rows[:, where, :] = jnp.where(early, by_slot(out[:, :128]), by_slot(out[:, 128:]))

    @pl.when(i >= ranks)
    def _():
        ones = jnp.ones((rows, 128), BF16)
        for n in range(count):
            own = v_rows[pl.ds(((i - ranks) * count + n) * PAIR, PAIR)]
            right = jnp.concatenate([own.reshape(rows, 128).astype(BF16), ones], axis=1)
            out = jnp.dot(w_ref[n], right, preferred_element_type=F32)
            total = out[:, 128:]
            o_out[n] = (out[:, :128] / jnp.where(total > 0.0, total, 1.0)).astype(BF16)


def mix(target, rows_v, early, weights):
    ranks, tokens = rows_v.shape[0], rows_v.shape[1]
    groups, rows = weights.shape[0], weights.shape[1]
    count = groups // ranks

    def sender(i):
        return jnp.minimum(i, ranks - 1)

    def group(i):
        return jnp.maximum(i - ranks, 0)

    return pl.pallas_call(
        functools.partial(mix_kernel, ranks),
        grid=(2 * ranks,),
        in_specs=[
            pl.BlockSpec((1, 1, tokens), lambda i: (sender(i), 0, 0)),
            pl.BlockSpec((1, tokens, 128), lambda i: (sender(i), 0, 0)),
            pl.BlockSpec((CLUSTERS, SLOTS, 128), lambda i: (0, sender(i), 0)),
            pl.BlockSpec((count, rows, rows), lambda i: (group(i), 0, 0)),
        ],
        out_specs=pl.BlockSpec((count, rows, 128), lambda i: (group(i), 0, 0)),
        out_shape=jax.ShapeDtypeStruct((groups, rows, 128), BF16),
        scratch_shapes=[pltpu.VMEM((CLUSTERS, ranks * SLOTS, 128), F32)],
        compiler_params=params(20),
        cost_estimate=cost(1, 1),
    )(target, rows_v, early, weights)


def unplace_kernel(who_ref, target_ref, o_ref, mean_ref, out_ref):
    tokens = target_ref.shape[2]
    half = o_ref.shape[0] // 2 * SLOTS
    right = o_ref[...].astype(F32).reshape(2 * half, 128).astype(BF16)
    right = jnp.concatenate([right[:half], right[half:]], axis=1)
    target = jnp.transpose(jnp.broadcast_to(target_ref[0], (128, tokens)))
    low = jnp.where(target < half, target, target - half)
    columns = lax.broadcasted_iota(jnp.int32, (tokens, half), 1)
    picked = (columns == jnp.tile(low, (1, half // 128))).astype(BF16)
    out = jnp.dot(picked, right, preferred_element_type=F32)
    out_ref[0, :tokens] = jnp.where(target < half, out[:, :128], out[:, 128:]).astype(BF16)
    means = mean_ref[...]
    high = means.astype(BF16)
    count = means.shape[0]
    out_ref[0, tokens : tokens + count] = high
    out_ref[0, tokens + count :] = (means - high.astype(F32)).astype(BF16)


def unplace(who, target, mixed, means):
    tokens, partners = target.shape[2], who.shape[0]
    count = CLUSTERS // target.shape[0]
    return pl.pallas_call(
        unplace_kernel,
        grid_spec=pltpu.PrefetchScalarGridSpec(
            num_scalar_prefetch=1,
            grid=(partners,),
            in_specs=[
                pl.BlockSpec((1, 1, tokens), lambda i, who: (who[i], 0, 0)),
                pl.BlockSpec((CLUSTERS, SLOTS, 128), lambda i, who: (0, who[i], 0)),
                pl.BlockSpec((count, 128), lambda i, who: (who[i], 0)),
            ],
            out_specs=pl.BlockSpec((1, tokens + 2 * count, 128), lambda i, who: (i, 0, 0)),
        ),
        out_shape=jax.ShapeDtypeStruct((partners, tokens + 2 * count, 128), BF16),
        compiler_params=params(12),
        cost_estimate=cost(1, 1),
    )(who, target, mixed, means)


def head_body(queries, keys, values, cluster_of, slot_of, centroids, out_weight):
    ranks = lax.axis_size("ctx")
    me = lax.axis_index("ctx")
    mine = lax.axis_index("head")
    tokens = queries.shape[0]
    cl_dev = CLUSTERS // ranks
    cap = ranks * SLOTS
    y, core = mine // 2, mine % 2

    def swap_y(x):
        return lax.ppermute(x, "head", [(0, 2), (1, 3), (2, 0), (3, 1)])

    def swap_core(x):
        return lax.ppermute(x, "head", [(0, 1), (1, 0), (2, 3), (3, 2)])

    def after(x, *others):
        return lax.optimization_barrier((x, others))[0]

    def swap_ctx(x, d):
        return lax.ppermute(x, "ctx", [(i, i ^ d) for i in range(ranks)])

    def exchange(x):
        return lax.all_to_all(x, "ctx", split_axis=0, concat_axis=0, tiled=True)

    marks = [x.astype(BF16).reshape(ranks, tokens // 128, 128) for x in (cluster_of, slot_of)]
    first = exchange(pack((queries, keys), jnp.concatenate(marks, axis=1)))
    marks = first[:, 2 * tokens :, :].astype(jnp.int32)
    target = marks[:, : tokens // 128, :] * SLOTS + marks[:, tokens // 128 :, :]
    target = target.reshape(ranks, 1, tokens)

    cols = out_weight.shape[1] // 4
    heads = me ^ jnp.arange(ranks, dtype=jnp.int32)
    across = swap_y(lax.dynamic_slice_in_dim(out_weight, (1 - y) * 2 * cols, 2 * cols, 1))
    beside = swap_core(
        lax.dynamic_slice_in_dim(out_weight, (2 * y + 1 - core) * cols, cols, 1)
    )
    corner = swap_core(lax.dynamic_slice_in_dim(across, (1 - core) * cols, cols, 1))
    groups = ((0, 2, 3, 1), (4, 5), (6, 7))
    zero = jnp.zeros_like(core)
    weight = pick(
        heads,
        [
            pltpu.with_memory_space_constraint(w, pltpu.HBM)
            for w in (out_weight, across, beside, corner)
        ],
        (mine, core, zero, zero),
        groups,
        cols,
    )
    rows_v = exchange(after(pack((values,)), first))

    def paired(x):
        return x.reshape(CLUSTERS // PAIR, PAIR * cap, 128)

    q_rows, k_rows, at = place_pair(target, first, tokens)
    weights, means, early = weigh(paired(q_rows), paired(k_rows), paired(at), tokens)
    early = early.reshape(CLUSTERS, cap, 128)
    early, weights = (pltpu.with_memory_space_constraint(x, pltpu.HBM) for x in (early, weights))
    rows_v = after(rows_v, weight)
    mixed = mix(target, rows_v, early, weights).reshape(CLUSTERS, cap, 128)

    got, sent = {}, {}

    def leave(d, *others):
        block = unplace(after(jnp.reshape(me ^ d, (1,)), *others), target, mixed, means)
        sent[d] = block.reshape(block.shape[1:])

    def go(d):
        got[d] = swap_ctx(sent[d], d)

    def side(*blocks):
        return jnp.concatenate([block[:tokens] for block in blocks], axis=1)

    leave(4)
    go(4)
    leave(5, sent[4])
    go(5)
    leave(0, sent[5])
    got[0] = sent[0]
    y_0 = swap_y(got[0])
    leave(2, sent[0])
    go(2)
    leave(3, sent[2])
    go(3)
    leave(1, sent[3], y_0)
    go(1)
    leave(6, sent[1], got[4])
    go(6)
    own_231 = side(*[got[d] for d in (2, 3, 1)])
    leave(7, sent[6], got[5], own_231)
    go(7)
    own, there = {}, {}
    y_231 = swap_y(own_231)
    own[2] = side(got[4], got[5])
    there[2] = swap_y(own[2])
    own[3] = side(got[6], got[7])
    there[3] = swap_y(own[3])
    same = {1: side(got[0], own_231, y_0, y_231), 2: side(own[2], there[2])}

    def add(total, left, row):
        more = jnp.dot(left, weight[row : row + left.shape[1]], preferred_element_type=F32)
        return more if total is None else total + more

    total = None
    for n, row in ((1, 0), (2, 2048)):
        total = add(total, jnp.concatenate([same[n], swap_core(same[n])], axis=1), row)
    row = 3072
    total = add(total, swap_core(own[3]), row + 512)
    last = swap_core(after(there[3], total))
    total = add(total, side(own[3], there[3]), row)
    projected = add(total, last, row + 768).astype(BF16)

    tails = jnp.stack([got[d][tokens:] for d in range(ranks)]).astype(F32)
    tails = tails[:, :cl_dev] + tails[:, cl_dev:]
    tails = jnp.concatenate(
        [lax.dynamic_slice_in_dim(tails, me ^ d, 1, 0) for d in range(ranks)], axis=0
    )
    new_centroids = mix_rate * centroids + (1.0 - mix_rate) * tails
    return (projected, new_centroids)


def dispatch(queries, keys, values, cluster_of, *rest):
    ranks, heads = lax.axis_size("ctx"), cluster_of.shape[0]
    whole_heads = ranks == heads == 8 and lax.axis_size("head") == 4
    step = head_body if whole_heads else body
    return step(queries, keys, values, cluster_of, *rest)


def solution(mesh):
    in_specs = (
        P("ctx", "head"),
        P("ctx", "head"),
        P("ctx", "head"),
        P("head", "ctx"),
        P("head", "ctx"),
        P("head", "ctx", None),
        P("head", None),
    )
    out_specs = (P("ctx", "head"), P("head", "ctx", None))
    return jax.shard_map(
        dispatch, mesh=mesh, in_specs=in_specs, out_specs=out_specs, check_vma=False
    )
```

```python
import functools
import math

import jax
import jax.numpy as jnp
from jax import lax
from jax.experimental import pallas as pl
from jax.experimental.pallas import tpu as pltpu
from jax.sharding import PartitionSpec as P

CLUSTERS = 256
SLOTS = 8


mix_rate = 0.5
neg_fill = -1e30


def attend(q_rows, k_rows, v_rows, positions):
    scale = 1.0 / math.sqrt(q_rows.shape[-1])
    scores = jnp.einsum("gqd,gkd->gqk", q_rows, k_rows, preferred_element_type=jnp.float32) * scale
    allowed = (positions[:, None, :] >= 0) & (positions[:, None, :] <= positions[:, :, None])
    scores = jnp.where(allowed, scores, neg_fill)
    top = jnp.max(scores, axis=2, keepdims=True)
    weights = jnp.where(allowed, jnp.exp(scores - top), 0.0).astype(jnp.bfloat16)
    total = jnp.sum(weights.astype(jnp.float32), axis=2, keepdims=True)
    mixed = jnp.einsum("gqk,gkd->gqd", weights, v_rows, preferred_element_type=jnp.float32)
    return (mixed / jnp.where(total > 0.0, total, 1.0)).astype(jnp.bfloat16)


def to_clusters(rows, cl_dev):
    senders, width, items = (rows.shape[0], rows.shape[1], rows.shape[2])
    slots = width // cl_dev
    shaped = rows.reshape((senders, cl_dev, slots, items) + rows.shape[3:])
    if rows.ndim == 4:
        order = (3, 1, 0, 2, 4)
    else:
        order = (3, 1, 0, 2)
    return jnp.transpose(shaped, order).reshape((items * cl_dev, senders * slots) + rows.shape[3:])


def from_clusters(mixed, senders, cl_dev, items):
    slots = mixed.shape[1] // senders
    shaped = mixed.reshape(items, cl_dev, senders, slots, mixed.shape[2])
    return jnp.transpose(shaped, (2, 1, 3, 0, 4)).reshape(
        senders, cl_dev * slots, items, mixed.shape[2]
    )


def owner_work(incoming, cl_dev):
    q_in, k_in, v_in, p_in = incoming
    senders, items = (q_in.shape[0], q_in.shape[2])
    q_rows = to_clusters(q_in, cl_dev)
    k_rows = to_clusters(k_in, cl_dev)
    v_rows = to_clusters(v_in, cl_dev)
    p_rows = to_clusters(p_in, cl_dev)
    mixed = attend(q_rows, k_rows, v_rows, p_rows)
    back = from_clusters(mixed, senders, cl_dev, items)
    return back


def body(queries, keys, values, cluster_of, slot_of, centroids, out_weight):
    ranks = lax.axis_size("ctx")
    rank_here = lax.axis_index("ctx")
    tok_rows = queries.shape[0]
    head_rows = cluster_of.shape[0]
    head_size = queries.shape[1] // head_rows
    cl_dev = CLUSTERS // ranks
    width = CLUSTERS * SLOTS
    target = jnp.transpose(cluster_of * SLOTS + slot_of)
    head_ids = jnp.broadcast_to(jnp.arange(head_rows, dtype=jnp.int32)[None, :], target.shape)

    def place(rows):
        shaped = rows.reshape(tok_rows, head_rows, head_size)
        filled = (
            jnp.zeros((width, head_rows, head_size), rows.dtype).at[target, head_ids].set(shaped)
        )
        return filled.reshape(ranks, width // ranks, head_rows, head_size)

    token_pos = rank_here * tok_rows + jnp.arange(tok_rows, dtype=jnp.int32)
    pos_slots = (
        jnp.full((width, head_rows), -1, jnp.int32)
        .at[target, head_ids]
        .set(jnp.broadcast_to(token_pos[:, None], target.shape))
    )
    pos_slots = pos_slots.reshape(ranks, width // ranks, head_rows)
    incoming = (
        lax.all_to_all(place(queries), "ctx", split_axis=0, concat_axis=0, tiled=True),
        lax.all_to_all(place(keys), "ctx", split_axis=0, concat_axis=0, tiled=True),
        lax.all_to_all(place(values), "ctx", split_axis=0, concat_axis=0, tiled=True),
        lax.all_to_all(pos_slots, "ctx", split_axis=0, concat_axis=0, tiled=True),
    )
    worked = owner_work(incoming, cl_dev)
    returned = lax.all_to_all(worked, "ctx", split_axis=0, concat_axis=0, tiled=True)
    rows_back = returned.reshape(width, head_rows, head_size)
    attended = rows_back[target, head_ids].reshape(tok_rows, head_rows * head_size)
    member = (
        cluster_of[:, :, None] == jnp.arange(CLUSTERS, dtype=jnp.int32)[None, None, :]
    ).astype(jnp.bfloat16)
    q_three = queries.reshape(tok_rows, head_rows, head_size)
    k_three = keys.reshape(tok_rows, head_rows, head_size)
    local_sums = jnp.einsum("htc,thd->hcd", member, q_three, preferred_element_type=jnp.float32)
    local_sums = local_sums + jnp.einsum(
        "htc,thd->hcd", member, k_three, preferred_element_type=jnp.float32
    )
    local_counts = jnp.sum(member, axis=1, dtype=jnp.float32)
    totals, counts = (
        lax.psum_scatter(
            local_sums.astype(jnp.bfloat16), "ctx", scatter_dimension=1, tiled=True
        ).astype(jnp.float32),
        lax.psum_scatter(
            local_counts.astype(jnp.bfloat16), "ctx", scatter_dimension=1, tiled=True
        ).astype(jnp.float32),
    )
    means = totals / (2.0 * jnp.maximum(counts, 1.0))[:, :, None]
    new_centroids = mix_rate * centroids + (1.0 - mix_rate) * means
    summed = lax.psum_scatter(
        lax.dot_general(
            out_weight, attended, (((0,), (1,)), ((), ())), preferred_element_type=jnp.float32
        ),
        "head",
        scatter_dimension=0,
        tiled=True,
    )
    projected = jnp.transpose(summed).astype(jnp.bfloat16)
    return (projected, new_centroids)


BF16 = jnp.bfloat16
F32 = jnp.float32
PAIR = 2
EMPTY = 1e9
LANES = (0, 2, 3, 1, 4, 5, 6, 7)


def params(limit):
    return pltpu.CompilerParams(
        dimension_semantics=("arbitrary",), vmem_limit_bytes=limit * 1024 * 1024
    )


def cost(flops, nbytes, transcendentals=0):
    return pl.CostEstimate(
        flops=flops, bytes_accessed=nbytes, transcendentals=transcendentals
    )


def pack_kernel(count, marked, *refs):
    sources = refs[:count]
    out_ref, held, sems_in, sems_out = refs[count + marked :]
    heads = out_ref.shape[0]
    tokens = sources[0].shape[0]
    parts = 2
    rows = tokens // parts
    reads = []
    for n, source in enumerate(sources):
        for p in range(parts):
            here = pl.ds(p * rows, rows)
            reads.append(
                pltpu.make_async_copy(
                    source.at[here], held.at[n, here], sems_in.at[n * parts + p]
                )
            )
    for copy in reads:
        copy.start()
    writes = []
    if marked:
        marks_ref = refs[count]
        there = out_ref.at[:, pl.ds(count * tokens, marks_ref.shape[1])]
        writes.append(pltpu.make_async_copy(marks_ref, there, sems_out.at[0]))
        writes[0].start()
    for n in range(count):
        for p in range(parts):
            reads[n * parts + p].wait()
            for j in range(heads):
                copy = pltpu.make_async_copy(
                    held.at[n, pl.ds(p * rows, rows), pl.ds(j * 128, 128)],
                    out_ref.at[j, pl.ds(n * tokens + p * rows, rows)],
                    sems_out.at[1 + (n * parts + p) * heads + j],
                )
                copy.start()
                writes.append(copy)
    for copy in writes:
        copy.wait()


def pack(sources, marks=None):
    tokens, width = sources[0].shape
    heads, count = width // 128, len(sources)
    marked = marks is not None
    rows = count * tokens + (marks.shape[1] if marked else 0)
    anywhere = pl.BlockSpec(memory_space=pl.ANY)
    args = list(sources)
    in_specs = [anywhere] * count
    if marked:
        args.append(marks)
        in_specs.append(pl.BlockSpec(memory_space=pltpu.VMEM))
    return pl.pallas_call(
        functools.partial(pack_kernel, count, marked),
        in_specs=in_specs,
        out_specs=anywhere,
        out_shape=pltpu.HBM((heads, rows, 128), BF16),
        scratch_shapes=[
            pltpu.VMEM((count, tokens, width), BF16),
            pltpu.SemaphoreType.DMA((2 * count,)),
            pltpu.SemaphoreType.DMA((2 * count * heads + 1,)),
        ],
        compiler_params=pltpu.CompilerParams(vmem_limit_bytes=60 * 1024 * 1024),
        cost_estimate=cost(0, 2 * heads * rows * 256),
    )(*args)


def pick_kernel(where_ref, weight_ref, *refs):
    outs, sems = refs[:-1], refs[-1]
    heads, cols = where_ref.shape[0] - len(refs[:-1]), outs[0].shape[1]
    copies = []
    for n, out_ref in enumerate(outs):
        column = pl.multiple_of(where_ref[heads + n] * cols, cols)
        for lane in range(heads):
            row = pl.multiple_of(where_ref[lane] * 128, 128)
            copies.append(
                pltpu.make_async_copy(
                    weight_ref.at[pl.ds(row, 128), pl.ds(column, cols)],
                    out_ref.at[pl.ds(lane * 128, 128)],
                    sems.at[len(copies)],
                )
            )
    for copy in copies:
        copy.start()
    for copy in copies:
        copy.wait()


def pick(heads, weight, columns, cols):
    where = jnp.concatenate([heads, jnp.stack(columns)])
    shape = jax.ShapeDtypeStruct((weight.shape[0], cols), BF16)
    return pl.pallas_call(
        pick_kernel,
        in_specs=[pl.BlockSpec(memory_space=pltpu.SMEM), pl.BlockSpec(memory_space=pl.ANY)],
        out_specs=[pl.BlockSpec(memory_space=pltpu.VMEM)] * len(columns),
        out_shape=[shape] * len(columns),
        scratch_shapes=[pltpu.SemaphoreType.DMA((heads.shape[0] * len(columns),))],
        compiler_params=pltpu.CompilerParams(vmem_limit_bytes=8 * 1024 * 1024),
        cost_estimate=cost(1, 1),
    )(where, pltpu.with_memory_space_constraint(weight, pltpu.HBM))


def match(first, count, target):
    rows = first + lax.broadcasted_iota(jnp.int32, (count, target.shape[1]), 0)
    return rows == target


def by_slot(x):
    return x.reshape(x.shape[0] // SLOTS, SLOTS, 128)


def place_pair_kernel(target_ref, q_ref, k_ref, q_out, k_out, p_out, right):
    tokens = q_ref.shape[1]
    slots = q_out.shape[0] * SLOTS
    step = 1024
    right[:, :128] = q_ref[0]
    right[:, 128:] = k_ref[0]
    base = pl.program_id(0) * tokens
    token = (base + lax.broadcasted_iota(jnp.int32, (1, tokens), 1)).astype(F32)
    target = target_ref[0]

    def move(i, carry):
        picked = match(i * step, step, target)
        out = jnp.dot(picked.astype(BF16), right[...], preferred_element_type=F32)
        where = pl.ds(i * (step // SLOTS), step // SLOTS)
        q_out[where] = by_slot(out[:, :128]).astype(BF16)
        k_out[where] = by_slot(out[:, 128:]).astype(BF16)
        at = jnp.min(jnp.where(picked, token, EMPTY), axis=1, keepdims=True)
        p_out[where] = by_slot(jnp.broadcast_to(at, (step, 128)))
        return carry

    lax.fori_loop(0, slots // step, move, 0)


def place_pair(target, first, tokens):
    ranks = first.shape[0]
    spec_out = pl.BlockSpec((CLUSTERS, SLOTS, 128), lambda j: (0, j, 0))
    shape = (CLUSTERS, ranks * SLOTS, 128)
    return pl.pallas_call(
        place_pair_kernel,
        grid=(ranks,),
        in_specs=[
            pl.BlockSpec((1, 1, tokens), lambda j: (j, 0, 0)),
            pl.BlockSpec((1, tokens, 128), lambda j: (j, 0, 0)),
            pl.BlockSpec((1, tokens, 128), lambda j: (j, 1, 0)),
        ],
        out_specs=[spec_out, spec_out, spec_out],
        out_shape=[
            jax.ShapeDtypeStruct(shape, BF16),
            jax.ShapeDtypeStruct(shape, BF16),
            jax.ShapeDtypeStruct(shape, F32),
        ],
        scratch_shapes=[pltpu.VMEM((tokens, 256), BF16)],
        compiler_params=params(16),
        cost_estimate=cost(1, 1),
    )(target, first, first)


def weigh_kernel(tokens, q_ref, k_ref, p_ref, w_out, mean_out, early_out):
    count, rows = q_ref.shape[0], q_ref.shape[1]
    cap = rows // PAIR
    scale = 1.0 / math.sqrt(q_ref.shape[2])
    same = (
        lax.broadcasted_iota(jnp.int32, (rows, rows), 0) // cap
        == lax.broadcasted_iota(jnp.int32, (rows, rows), 1) // cap
    )
    for n in range(count):
        q, k, own = q_ref[n], k_ref[n], p_ref[n]
        scores = lax.dot_general(q, k, (((1,), (1,)), ((), ())), preferred_element_type=F32) * scale
        allowed = same & (jnp.transpose(own) <= own)
        scores = jnp.where(allowed, scores, neg_fill)
        top = jnp.max(scores, axis=1, keepdims=True)
        w_out[n] = jnp.where(allowed, jnp.exp(scores - top), 0.0).astype(BF16)
    share = p_ref[...] * (1.0 / tokens)
    early_out[...] = (share - jnp.floor(share) < 0.5).astype(BF16)
    both = (q_ref[...].astype(F32) + k_ref[...].astype(F32)).reshape(count * PAIR, cap, 128)
    held = (p_ref[...] < EMPTY).astype(F32).reshape(count * PAIR, cap, 128)
    mean_out[...] = jnp.sum(both, axis=1) / (2.0 * jnp.maximum(jnp.sum(held, axis=1), 1.0))


def weigh(q_rows, k_rows, at, tokens):
    groups, rows = q_rows.shape[0], q_rows.shape[1]
    step = 8
    spec = pl.BlockSpec((step, rows, 128), lambda i: (i, 0, 0))
    return pl.pallas_call(
        functools.partial(weigh_kernel, tokens),
        grid=(groups // step,),
        in_specs=[spec, spec, spec],
        out_specs=[
            pl.BlockSpec((step, rows, rows), lambda i: (i, 0, 0)),
            pl.BlockSpec((step * PAIR, 128), lambda i: (i, 0)),
            spec,
        ],
        out_shape=[
            pltpu.HBM((groups, rows, rows), BF16),
            jax.ShapeDtypeStruct((groups * PAIR, 128), F32),
            pltpu.HBM((groups, rows, 128), BF16),
        ],
        compiler_params=params(12),
        cost_estimate=cost(1, 1),
    )(q_rows, k_rows, at)


def mix_kernel(ranks, target_ref, v_ref, early_ref, w_ref, o_out, v_rows):
    i = pl.program_id(0)
    slots = v_rows.shape[0] * SLOTS
    count, rows = w_ref.shape[0], w_ref.shape[1]
    tokens = v_ref.shape[1]
    half = tokens // 2

    @pl.when(i < ranks)
    def _():
        target = target_ref[0]
        picked = match(0, slots, target[:, :half]) | match(0, slots, target[:, half:])
        both = jnp.concatenate([v_ref[0, :half], v_ref[0, half:]], axis=1)
        out = jnp.dot(picked.astype(BF16), both, preferred_element_type=F32)
        early = early_ref[...].astype(F32) > 0.0
        where = pl.ds(pl.multiple_of(i * SLOTS, SLOTS), SLOTS)
        v_rows[:, where, :] = jnp.where(early, by_slot(out[:, :128]), by_slot(out[:, 128:]))

    @pl.when(i >= ranks)
    def _():
        ones = jnp.ones((rows, 128), BF16)
        for n in range(count):
            own = v_rows[pl.ds(((i - ranks) * count + n) * PAIR, PAIR)]
            right = jnp.concatenate([own.reshape(rows, 128).astype(BF16), ones], axis=1)
            out = jnp.dot(w_ref[n], right, preferred_element_type=F32)
            total = out[:, 128:]
            o_out[n] = (out[:, :128] / jnp.where(total > 0.0, total, 1.0)).astype(BF16)


def mix(target, rows_v, early, weights):
    ranks, tokens = rows_v.shape[0], rows_v.shape[1]
    groups, rows = weights.shape[0], weights.shape[1]
    count = groups // ranks

    def sender(i):
        return jnp.minimum(i, ranks - 1)

    def group(i):
        return jnp.maximum(i - ranks, 0)

    return pl.pallas_call(
        functools.partial(mix_kernel, ranks),
        grid=(2 * ranks,),
        in_specs=[
            pl.BlockSpec((1, 1, tokens), lambda i: (sender(i), 0, 0)),
            pl.BlockSpec((1, tokens, 128), lambda i: (sender(i), 0, 0)),
            pl.BlockSpec((CLUSTERS, SLOTS, 128), lambda i: (0, sender(i), 0)),
            pl.BlockSpec((count, rows, rows), lambda i: (group(i), 0, 0)),
        ],
        out_specs=pl.BlockSpec((count, rows, 128), lambda i: (group(i), 0, 0)),
        out_shape=jax.ShapeDtypeStruct((groups, rows, 128), BF16),
        scratch_shapes=[pltpu.VMEM((CLUSTERS, ranks * SLOTS, 128), F32)],
        compiler_params=params(20),
        cost_estimate=cost(1, 1),
    )(target, rows_v, early, weights)


def unplace_kernel(who_ref, target_ref, o_ref, mean_ref, out_ref):
    tokens = target_ref.shape[2]
    half = o_ref.shape[0] // 2 * SLOTS
    right = o_ref[...].astype(F32).reshape(2 * half, 128).astype(BF16)
    right = jnp.concatenate([right[:half], right[half:]], axis=1)
    target = jnp.transpose(jnp.broadcast_to(target_ref[0], (128, tokens)))
    low = jnp.where(target < half, target, target - half)
    columns = lax.broadcasted_iota(jnp.int32, (tokens, half), 1)
    picked = (columns == jnp.tile(low, (1, half // 128))).astype(BF16)
    out = jnp.dot(picked, right, preferred_element_type=F32)
    out_ref[0, :tokens] = jnp.where(target < half, out[:, :128], out[:, 128:]).astype(BF16)
    means = mean_ref[...]
    high = means.astype(BF16)
    count = means.shape[0]
    out_ref[0, tokens : tokens + count] = high
    out_ref[0, tokens + count :] = (means - high.astype(F32)).astype(BF16)


def unplace(who, target, mixed, means):
    tokens, partners = target.shape[2], who.shape[0]
    count = CLUSTERS // target.shape[0]
    return pl.pallas_call(
        unplace_kernel,
        grid_spec=pltpu.PrefetchScalarGridSpec(
            num_scalar_prefetch=1,
            grid=(partners,),
            in_specs=[
                pl.BlockSpec((1, 1, tokens), lambda i, who: (who[i], 0, 0)),
                pl.BlockSpec((CLUSTERS, SLOTS, 128), lambda i, who: (0, who[i], 0)),
                pl.BlockSpec((count, 128), lambda i, who: (who[i], 0)),
            ],
            out_specs=pl.BlockSpec((1, tokens + 2 * count, 128), lambda i, who: (i, 0, 0)),
        ),
        out_shape=jax.ShapeDtypeStruct((partners, tokens + 2 * count, 128), BF16),
        compiler_params=params(12),
        cost_estimate=cost(1, 1),
    )(who, target, mixed, means)


def head_body(queries, keys, values, cluster_of, slot_of, centroids, out_weight):
    ranks = lax.axis_size("ctx")
    me = lax.axis_index("ctx")
    mine = lax.axis_index("head")
    tokens = queries.shape[0]
    cl_dev = CLUSTERS // ranks
    cap = ranks * SLOTS
    y, core = mine // 2, mine % 2

    def swap_y(x):
        return lax.ppermute(x, "head", [(0, 2), (1, 3), (2, 0), (3, 1)])

    def swap_core(x):
        return lax.ppermute(x, "head", [(0, 1), (1, 0), (2, 3), (3, 2)])

    def after(x, *others):
        return lax.optimization_barrier((x, others))[0]

    def swap_ctx(x, d):
        return lax.ppermute(x, "ctx", [(i, i ^ d) for i in range(ranks)])

    def exchange(x):
        return lax.all_to_all(x, "ctx", split_axis=0, concat_axis=0, tiled=True)

    marks = [x.astype(BF16).reshape(ranks, tokens // 128, 128) for x in (cluster_of, slot_of)]
    first = exchange(pack((queries, keys), jnp.concatenate(marks, axis=1)))
    marks = first[:, 2 * tokens :, :].astype(jnp.int32)
    target = marks[:, : tokens // 128, :] * SLOTS + marks[:, tokens // 128 :, :]
    target = target.reshape(ranks, 1, tokens)

    cols = out_weight.shape[1] // 4
    heads = me ^ jnp.array(LANES, jnp.int32)
    far = 2 * (1 - y)
    corner, across = pick(heads, out_weight, (far + 1 - core, far + core), cols)
    corner, across = swap_y(corner), swap_y(across)
    w_own, beside = pick(heads, out_weight, (mine, 2 * y + 1 - core), cols)
    w_beside, w_corner, w_across = swap_core(beside), swap_core(corner), across
    values = after(values, w_beside, w_corner)
    rows_v = exchange(after(pack((values,)), first))

    def paired(x):
        return x.reshape(CLUSTERS // PAIR, PAIR * cap, 128)

    q_rows, k_rows, at = place_pair(target, first, tokens)
    weights, means, early = weigh(paired(q_rows), paired(k_rows), paired(at), tokens)
    early = early.reshape(CLUSTERS, cap, 128)
    early, weights = (pltpu.with_memory_space_constraint(x, pltpu.HBM) for x in (early, weights))
    rows_v = after(rows_v, w_across)
    mixed = mix(target, rows_v, early, weights).reshape(CLUSTERS, cap, 128)

    got, sent = {}, {}

    def leave(d, *others):
        block = unplace(after(jnp.reshape(me ^ d, (1,)), *others), target, mixed, means)
        sent[d] = block.reshape(block.shape[1:])

    def go(d):
        got[d] = swap_ctx(sent[d], d)

    def side(*blocks):
        return jnp.concatenate([block[:tokens] for block in blocks], axis=1)

    plan = (4, 2, 0, 3, 1, 5, 6, 7)
    waits = {5: (0,), 6: (4,), 7: (5, 9)}
    ends = {}
    for n, d in enumerate(plan):
        if d == 7:
            own_near = side(*[got[d] for d in LANES[1:4]])
            ends[9] = own_near
        others = [ends[k] for k in waits.get(d, ())]
        if n:
            others = [sent[plan[n - 1]]] + others
        leave(d, *others)
        if d:
            go(d)
            ends[d] = got[d]
        else:
            got[0] = sent[0]
            y_0 = ends[0] = swap_y(got[0])
    own, there = {}, {}
    y_near = swap_y(own_near)
    own[2] = side(got[4], got[5])
    there[2] = swap_y(own[2])
    own[3] = side(got[6], got[7])
    there[3] = swap_y(own[3])
    own[1], there[1] = side(got[0], own_near), side(y_0, y_near)

    def add(total, left, weight, row):
        more = jnp.dot(left, weight[row : row + left.shape[1]], preferred_element_type=F32)
        return more if total is None else total + more

    total = None
    for n, row in ((1, 0), (2, 512)):
        width = own[n].shape[1]
        total = add(total, own[n], w_own, row)
        total = add(total, there[n], w_across, row)
        moved = swap_core(side(own[n], there[n]))
        total = add(total, moved[:, :width], w_beside, row)
        total = add(total, moved[:, width:], w_corner, row)
    row = 768
    total = add(total, own[3], w_own, row)
    total = add(total, swap_core(own[3]), w_beside, row)
    last = swap_core(after(there[3], total))
    total = add(total, there[3], w_across, row)
    projected = add(total, last, w_corner, row).astype(BF16)

    tails = jnp.stack([got[d][tokens:] for d in range(ranks)]).astype(F32)
    tails = tails[:, :cl_dev] + tails[:, cl_dev:]
    tails = jnp.concatenate(
        [lax.dynamic_slice_in_dim(tails, me ^ d, 1, 0) for d in range(ranks)], axis=0
    )
    new_centroids = mix_rate * centroids + (1.0 - mix_rate) * tails
    return (projected, new_centroids)


def dispatch(queries, keys, values, cluster_of, *rest):
    ranks, heads = lax.axis_size("ctx"), cluster_of.shape[0]
    whole_heads = ranks == heads == 8 and lax.axis_size("head") == 4
    step = head_body if whole_heads else body
    return step(queries, keys, values, cluster_of, *rest)


def solution(mesh):
    in_specs = (
        P("ctx", "head"),
        P("ctx", "head"),
        P("ctx", "head"),
        P("head", "ctx"),
        P("head", "ctx"),
        P("head", "ctx", None),
        P("head", None),
    )
    out_specs = (P("ctx", "head"), P("head", "ctx", None))
    return jax.shard_map(
        dispatch, mesh=mesh, in_specs=in_specs, out_specs=out_specs, check_vma=False
    )
```

```python
import functools
import math

import jax
import jax.numpy as jnp
from jax import lax
from jax.experimental import pallas as pl
from jax.experimental.pallas import tpu as pltpu
from jax.sharding import PartitionSpec as P

CLUSTERS = 256
SLOTS = 8


mix_rate = 0.5
neg_fill = -1e30


def attend(q_rows, k_rows, v_rows, positions):
    scale = 1.0 / math.sqrt(q_rows.shape[-1])
    scores = jnp.einsum("gqd,gkd->gqk", q_rows, k_rows, preferred_element_type=jnp.float32) * scale
    allowed = (positions[:, None, :] >= 0) & (positions[:, None, :] <= positions[:, :, None])
    scores = jnp.where(allowed, scores, neg_fill)
    top = jnp.max(scores, axis=2, keepdims=True)
    weights = jnp.where(allowed, jnp.exp(scores - top), 0.0).astype(jnp.bfloat16)
    total = jnp.sum(weights.astype(jnp.float32), axis=2, keepdims=True)
    mixed = jnp.einsum("gqk,gkd->gqd", weights, v_rows, preferred_element_type=jnp.float32)
    return (mixed / jnp.where(total > 0.0, total, 1.0)).astype(jnp.bfloat16)


def to_clusters(rows, cl_dev):
    senders, width, items = (rows.shape[0], rows.shape[1], rows.shape[2])
    slots = width // cl_dev
    shaped = rows.reshape((senders, cl_dev, slots, items) + rows.shape[3:])
    if rows.ndim == 4:
        order = (3, 1, 0, 2, 4)
    else:
        order = (3, 1, 0, 2)
    return jnp.transpose(shaped, order).reshape((items * cl_dev, senders * slots) + rows.shape[3:])


def from_clusters(mixed, senders, cl_dev, items):
    slots = mixed.shape[1] // senders
    shaped = mixed.reshape(items, cl_dev, senders, slots, mixed.shape[2])
    return jnp.transpose(shaped, (2, 1, 3, 0, 4)).reshape(
        senders, cl_dev * slots, items, mixed.shape[2]
    )


def owner_work(incoming, cl_dev):
    q_in, k_in, v_in, p_in = incoming
    senders, items = (q_in.shape[0], q_in.shape[2])
    q_rows = to_clusters(q_in, cl_dev)
    k_rows = to_clusters(k_in, cl_dev)
    v_rows = to_clusters(v_in, cl_dev)
    p_rows = to_clusters(p_in, cl_dev)
    mixed = attend(q_rows, k_rows, v_rows, p_rows)
    back = from_clusters(mixed, senders, cl_dev, items)
    return back


def body(queries, keys, values, cluster_of, slot_of, centroids, out_weight):
    ranks = lax.axis_size("ctx")
    rank_here = lax.axis_index("ctx")
    tok_rows = queries.shape[0]
    head_rows = cluster_of.shape[0]
    head_size = queries.shape[1] // head_rows
    cl_dev = CLUSTERS // ranks
    width = CLUSTERS * SLOTS
    target = jnp.transpose(cluster_of * SLOTS + slot_of)
    head_ids = jnp.broadcast_to(jnp.arange(head_rows, dtype=jnp.int32)[None, :], target.shape)

    def place(rows):
        shaped = rows.reshape(tok_rows, head_rows, head_size)
        filled = (
            jnp.zeros((width, head_rows, head_size), rows.dtype).at[target, head_ids].set(shaped)
        )
        return filled.reshape(ranks, width // ranks, head_rows, head_size)

    token_pos = rank_here * tok_rows + jnp.arange(tok_rows, dtype=jnp.int32)
    pos_slots = (
        jnp.full((width, head_rows), -1, jnp.int32)
        .at[target, head_ids]
        .set(jnp.broadcast_to(token_pos[:, None], target.shape))
    )
    pos_slots = pos_slots.reshape(ranks, width // ranks, head_rows)
    incoming = (
        lax.all_to_all(place(queries), "ctx", split_axis=0, concat_axis=0, tiled=True),
        lax.all_to_all(place(keys), "ctx", split_axis=0, concat_axis=0, tiled=True),
        lax.all_to_all(place(values), "ctx", split_axis=0, concat_axis=0, tiled=True),
        lax.all_to_all(pos_slots, "ctx", split_axis=0, concat_axis=0, tiled=True),
    )
    worked = owner_work(incoming, cl_dev)
    returned = lax.all_to_all(worked, "ctx", split_axis=0, concat_axis=0, tiled=True)
    rows_back = returned.reshape(width, head_rows, head_size)
    attended = rows_back[target, head_ids].reshape(tok_rows, head_rows * head_size)
    member = (
        cluster_of[:, :, None] == jnp.arange(CLUSTERS, dtype=jnp.int32)[None, None, :]
    ).astype(jnp.bfloat16)
    q_three = queries.reshape(tok_rows, head_rows, head_size)
    k_three = keys.reshape(tok_rows, head_rows, head_size)
    local_sums = jnp.einsum("htc,thd->hcd", member, q_three, preferred_element_type=jnp.float32)
    local_sums = local_sums + jnp.einsum(
        "htc,thd->hcd", member, k_three, preferred_element_type=jnp.float32
    )
    local_counts = jnp.sum(member, axis=1, dtype=jnp.float32)
    totals, counts = (
        lax.psum_scatter(
            local_sums.astype(jnp.bfloat16), "ctx", scatter_dimension=1, tiled=True
        ).astype(jnp.float32),
        lax.psum_scatter(
            local_counts.astype(jnp.bfloat16), "ctx", scatter_dimension=1, tiled=True
        ).astype(jnp.float32),
    )
    means = totals / (2.0 * jnp.maximum(counts, 1.0))[:, :, None]
    new_centroids = mix_rate * centroids + (1.0 - mix_rate) * means
    summed = lax.psum_scatter(
        lax.dot_general(
            out_weight, attended, (((0,), (1,)), ((), ())), preferred_element_type=jnp.float32
        ),
        "head",
        scatter_dimension=0,
        tiled=True,
    )
    projected = jnp.transpose(summed).astype(jnp.bfloat16)
    return (projected, new_centroids)


BF16 = jnp.bfloat16
F32 = jnp.float32
PAIR = 2
EMPTY = 1e9
LANES = (0, 2, 3, 1, 4, 5, 6, 7)


def params(limit):
    return pltpu.CompilerParams(
        dimension_semantics=("arbitrary",), vmem_limit_bytes=limit * 1024 * 1024
    )


def cost(flops, nbytes, transcendentals=0):
    return pl.CostEstimate(
        flops=flops, bytes_accessed=nbytes, transcendentals=transcendentals
    )


def pack_kernel(count, marked, *refs):
    sources = refs[:count]
    out_ref, held, sems_in, sems_out = refs[count + marked :]
    heads = out_ref.shape[0]
    tokens = sources[0].shape[0]
    parts = 2
    rows = tokens // parts
    reads = []
    for n, source in enumerate(sources):
        for p in range(parts):
            here = pl.ds(p * rows, rows)
            reads.append(
                pltpu.make_async_copy(
                    source.at[here], held.at[n, here], sems_in.at[n * parts + p]
                )
            )
    for copy in reads:
        copy.start()
    writes = []
    if marked:
        marks_ref = refs[count]
        there = out_ref.at[:, pl.ds(count * tokens, marks_ref.shape[1])]
        writes.append(pltpu.make_async_copy(marks_ref, there, sems_out.at[0]))
        writes[0].start()
    for n in range(count):
        for p in range(parts):
            reads[n * parts + p].wait()
            for j in range(heads):
                copy = pltpu.make_async_copy(
                    held.at[n, pl.ds(p * rows, rows), pl.ds(j * 128, 128)],
                    out_ref.at[j, pl.ds(n * tokens + p * rows, rows)],
                    sems_out.at[1 + (n * parts + p) * heads + j],
                )
                copy.start()
                writes.append(copy)
    for copy in writes:
        copy.wait()


def pack(sources, marks=None):
    tokens, width = sources[0].shape
    heads, count = width // 128, len(sources)
    marked = marks is not None
    rows = count * tokens + (marks.shape[1] if marked else 0)
    anywhere = pl.BlockSpec(memory_space=pl.ANY)
    args = list(sources)
    in_specs = [anywhere] * count
    if marked:
        args.append(marks)
        in_specs.append(pl.BlockSpec(memory_space=pltpu.VMEM))
    return pl.pallas_call(
        functools.partial(pack_kernel, count, marked),
        in_specs=in_specs,
        out_specs=anywhere,
        out_shape=pltpu.HBM((heads, rows, 128), BF16),
        scratch_shapes=[
            pltpu.VMEM((count, tokens, width), BF16),
            pltpu.SemaphoreType.DMA((2 * count,)),
            pltpu.SemaphoreType.DMA((2 * count * heads + 1,)),
        ],
        compiler_params=pltpu.CompilerParams(vmem_limit_bytes=60 * 1024 * 1024),
        cost_estimate=cost(0, 2 * heads * rows * 256),
    )(*args)


def pick_kernel(count, where_ref, weight_ref, out_ref, sems):
    heads, cols = where_ref.shape[0] - count, out_ref.shape[1]
    copies = []
    for n in range(count):
        column = pl.multiple_of(where_ref[heads + n] * cols, cols)
        for lane in range(heads):
            row = pl.multiple_of(where_ref[lane] * 128, 128)
            copies.append(
                pltpu.make_async_copy(
                    weight_ref.at[pl.ds(row, 128), pl.ds(column, cols)],
                    out_ref.at[pl.ds((n * heads + lane) * 128, 128)],
                    sems.at[len(copies)],
                )
            )
    for copy in copies:
        copy.start()
    for copy in copies:
        copy.wait()


def pick(heads, weight, columns, cols):
    count = len(columns)
    where = jnp.concatenate([heads, jnp.stack(columns)])
    return pl.pallas_call(
        functools.partial(pick_kernel, count),
        in_specs=[pl.BlockSpec(memory_space=pltpu.SMEM), pl.BlockSpec(memory_space=pl.ANY)],
        out_specs=pl.BlockSpec(memory_space=pltpu.VMEM),
        out_shape=pltpu.HBM((count * weight.shape[0], cols), BF16),
        scratch_shapes=[pltpu.SemaphoreType.DMA((heads.shape[0] * count,))],
        compiler_params=pltpu.CompilerParams(vmem_limit_bytes=56 * 1024 * 1024),
        cost_estimate=cost(1, 1),
    )(where, pltpu.with_memory_space_constraint(weight, pltpu.HBM))


def join_kernel(plan, *refs):
    sources, out_ref, sems = refs[:-2], refs[-2], refs[-1]
    copies, row = [], 0
    for part, first, count in plan:
        copies.append(
            pltpu.make_async_copy(
                sources[part].at[pl.ds(first, count)],
                out_ref.at[pl.ds(row, count)],
                sems.at[len(copies)],
            )
        )
        row += count
    for copy in copies:
        copy.start()
    for copy in copies:
        copy.wait()


def join(sources, starts, groups):
    plan = [(part, at + first, count) for first, count in groups for part, at in enumerate(starts)]
    rows, cols = sum(count for _, _, count in plan), sources[0].shape[1]
    return pl.pallas_call(
        functools.partial(join_kernel, plan),
        in_specs=[pl.BlockSpec(memory_space=pl.ANY)] * len(sources),
        out_specs=pl.BlockSpec(memory_space=pltpu.VMEM),
        out_shape=pltpu.HBM((rows, cols), BF16),
        scratch_shapes=[pltpu.SemaphoreType.DMA((len(plan),))],
        compiler_params=pltpu.CompilerParams(vmem_limit_bytes=56 * 1024 * 1024),
        cost_estimate=cost(1, 1),
    )(*sources)


def match(first, count, target):
    rows = first + lax.broadcasted_iota(jnp.int32, (count, target.shape[1]), 0)
    return rows == target


def by_slot(x):
    return x.reshape(x.shape[0] // SLOTS, SLOTS, 128)


def place_pair_kernel(target_ref, q_ref, k_ref, q_out, k_out, p_out, right):
    tokens = q_ref.shape[1]
    slots = q_out.shape[0] * SLOTS
    step = 1024
    right[:, :128] = q_ref[0]
    right[:, 128:] = k_ref[0]
    base = pl.program_id(0) * tokens
    token = (base + lax.broadcasted_iota(jnp.int32, (1, tokens), 1)).astype(F32)
    target = target_ref[0]

    def move(i, carry):
        picked = match(i * step, step, target)
        out = jnp.dot(picked.astype(BF16), right[...], preferred_element_type=F32)
        where = pl.ds(i * (step // SLOTS), step // SLOTS)
        q_out[where] = by_slot(out[:, :128]).astype(BF16)
        k_out[where] = by_slot(out[:, 128:]).astype(BF16)
        at = jnp.min(jnp.where(picked, token, EMPTY), axis=1, keepdims=True)
        p_out[where] = by_slot(jnp.broadcast_to(at, (step, 128)))
        return carry

    lax.fori_loop(0, slots // step, move, 0)


def place_pair(target, first, tokens):
    ranks = first.shape[0]
    spec_out = pl.BlockSpec((CLUSTERS, SLOTS, 128), lambda j: (0, j, 0))
    shape = (CLUSTERS, ranks * SLOTS, 128)
    return pl.pallas_call(
        place_pair_kernel,
        grid=(ranks,),
        in_specs=[
            pl.BlockSpec((1, 1, tokens), lambda j: (j, 0, 0)),
            pl.BlockSpec((1, tokens, 128), lambda j: (j, 0, 0)),
            pl.BlockSpec((1, tokens, 128), lambda j: (j, 1, 0)),
        ],
        out_specs=[spec_out, spec_out, spec_out],
        out_shape=[
            jax.ShapeDtypeStruct(shape, BF16),
            jax.ShapeDtypeStruct(shape, BF16),
            jax.ShapeDtypeStruct(shape, F32),
        ],
        scratch_shapes=[pltpu.VMEM((tokens, 256), BF16)],
        compiler_params=params(16),
        cost_estimate=cost(1, 1),
    )(target, first, first)


def weigh_kernel(tokens, q_ref, k_ref, p_ref, w_out, mean_out, early_out):
    count, rows = q_ref.shape[0], q_ref.shape[1]
    cap = rows // PAIR
    scale = 1.0 / math.sqrt(q_ref.shape[2])
    same = (
        lax.broadcasted_iota(jnp.int32, (rows, rows), 0) // cap
        == lax.broadcasted_iota(jnp.int32, (rows, rows), 1) // cap
    )
    for n in range(count):
        q, k, own = q_ref[n], k_ref[n], p_ref[n]
        scores = lax.dot_general(q, k, (((1,), (1,)), ((), ())), preferred_element_type=F32) * scale
        allowed = same & (jnp.transpose(own) <= own)
        scores = jnp.where(allowed, scores, neg_fill)
        top = jnp.max(scores, axis=1, keepdims=True)
        w_out[n] = jnp.where(allowed, jnp.exp(scores - top), 0.0).astype(BF16)
    share = p_ref[...] * (1.0 / tokens)
    early_out[...] = (share - jnp.floor(share) < 0.5).astype(BF16)
    both = (q_ref[...].astype(F32) + k_ref[...].astype(F32)).reshape(count * PAIR, cap, 128)
    held = (p_ref[...] < EMPTY).astype(F32).reshape(count * PAIR, cap, 128)
    mean_out[...] = jnp.sum(both, axis=1) / (2.0 * jnp.maximum(jnp.sum(held, axis=1), 1.0))


def weigh(q_rows, k_rows, at, tokens):
    groups, rows = q_rows.shape[0], q_rows.shape[1]
    step = 8
    spec = pl.BlockSpec((step, rows, 128), lambda i: (i, 0, 0))
    return pl.pallas_call(
        functools.partial(weigh_kernel, tokens),
        grid=(groups // step,),
        in_specs=[spec, spec, spec],
        out_specs=[
            pl.BlockSpec((step, rows, rows), lambda i: (i, 0, 0)),
            pl.BlockSpec((step * PAIR, 128), lambda i: (i, 0)),
            spec,
        ],
        out_shape=[
            pltpu.HBM((groups, rows, rows), BF16),
            jax.ShapeDtypeStruct((groups * PAIR, 128), F32),
            pltpu.HBM((groups, rows, 128), BF16),
        ],
        compiler_params=params(12),
        cost_estimate=cost(1, 1),
    )(q_rows, k_rows, at)


def mix_kernel(ranks, target_ref, v_ref, early_ref, w_ref, o_out, v_rows):
    i = pl.program_id(0)
    slots = v_rows.shape[0] * SLOTS
    count, rows = w_ref.shape[0], w_ref.shape[1]
    tokens = v_ref.shape[1]
    half = tokens // 2

    @pl.when(i < ranks)
    def _():
        target = target_ref[0]
        picked = match(0, slots, target[:, :half]) | match(0, slots, target[:, half:])
        both = jnp.concatenate([v_ref[0, :half], v_ref[0, half:]], axis=1)
        out = jnp.dot(picked.astype(BF16), both, preferred_element_type=F32)
        early = early_ref[...].astype(F32) > 0.0
        where = pl.ds(pl.multiple_of(i * SLOTS, SLOTS), SLOTS)
        v_rows[:, where, :] = jnp.where(early, by_slot(out[:, :128]), by_slot(out[:, 128:]))

    @pl.when(i >= ranks)
    def _():
        ones = jnp.ones((rows, 128), BF16)
        for n in range(count):
            own = v_rows[pl.ds(((i - ranks) * count + n) * PAIR, PAIR)]
            right = jnp.concatenate([own.reshape(rows, 128).astype(BF16), ones], axis=1)
            out = jnp.dot(w_ref[n], right, preferred_element_type=F32)
            total = out[:, 128:]
            o_out[n] = (out[:, :128] / jnp.where(total > 0.0, total, 1.0)).astype(BF16)


def mix(target, rows_v, early, weights):
    ranks, tokens = rows_v.shape[0], rows_v.shape[1]
    groups, rows = weights.shape[0], weights.shape[1]
    count = groups // ranks

    def sender(i):
        return jnp.minimum(i, ranks - 1)

    def group(i):
        return jnp.maximum(i - ranks, 0)

    return pl.pallas_call(
        functools.partial(mix_kernel, ranks),
        grid=(2 * ranks,),
        in_specs=[
            pl.BlockSpec((1, 1, tokens), lambda i: (sender(i), 0, 0)),
            pl.BlockSpec((1, tokens, 128), lambda i: (sender(i), 0, 0)),
            pl.BlockSpec((CLUSTERS, SLOTS, 128), lambda i: (0, sender(i), 0)),
            pl.BlockSpec((count, rows, rows), lambda i: (group(i), 0, 0)),
        ],
        out_specs=pl.BlockSpec((count, rows, 128), lambda i: (group(i), 0, 0)),
        out_shape=jax.ShapeDtypeStruct((groups, rows, 128), BF16),
        scratch_shapes=[pltpu.VMEM((CLUSTERS, ranks * SLOTS, 128), F32)],
        compiler_params=params(20),
        cost_estimate=cost(1, 1),
    )(target, rows_v, early, weights)


def unplace_kernel(who_ref, target_ref, o_ref, mean_ref, out_ref):
    tokens = target_ref.shape[2]
    half = o_ref.shape[0] // 2 * SLOTS
    right = o_ref[...].astype(F32).reshape(2 * half, 128).astype(BF16)
    right = jnp.concatenate([right[:half], right[half:]], axis=1)
    target = jnp.transpose(jnp.broadcast_to(target_ref[0], (128, tokens)))
    low = jnp.where(target < half, target, target - half)
    columns = lax.broadcasted_iota(jnp.int32, (tokens, half), 1)
    picked = (columns == jnp.tile(low, (1, half // 128))).astype(BF16)
    out = jnp.dot(picked, right, preferred_element_type=F32)
    out_ref[0, :tokens] = jnp.where(target < half, out[:, :128], out[:, 128:]).astype(BF16)
    means = mean_ref[...]
    high = means.astype(BF16)
    count = means.shape[0]
    out_ref[0, tokens : tokens + count] = high
    out_ref[0, tokens + count :] = (means - high.astype(F32)).astype(BF16)


def unplace(who, target, mixed, means):
    tokens, partners = target.shape[2], who.shape[0]
    count = CLUSTERS // target.shape[0]
    return pl.pallas_call(
        unplace_kernel,
        grid_spec=pltpu.PrefetchScalarGridSpec(
            num_scalar_prefetch=1,
            grid=(partners,),
            in_specs=[
                pl.BlockSpec((1, 1, tokens), lambda i, who: (who[i], 0, 0)),
                pl.BlockSpec((CLUSTERS, SLOTS, 128), lambda i, who: (0, who[i], 0)),
                pl.BlockSpec((count, 128), lambda i, who: (who[i], 0)),
            ],
            out_specs=pl.BlockSpec((1, tokens + 2 * count, 128), lambda i, who: (i, 0, 0)),
        ),
        out_shape=jax.ShapeDtypeStruct((partners, tokens + 2 * count, 128), BF16),
        compiler_params=params(12),
        cost_estimate=cost(1, 1),
    )(who, target, mixed, means)


def head_body(queries, keys, values, cluster_of, slot_of, centroids, out_weight):
    ranks = lax.axis_size("ctx")
    me = lax.axis_index("ctx")
    mine = lax.axis_index("head")
    tokens = queries.shape[0]
    cl_dev = CLUSTERS // ranks
    cap = ranks * SLOTS
    y, core = mine // 2, mine % 2

    def swap_y(x):
        return lax.ppermute(x, "head", [(0, 2), (1, 3), (2, 0), (3, 1)])

    def swap_core(x):
        return lax.ppermute(x, "head", [(0, 1), (1, 0), (2, 3), (3, 2)])

    def after(x, *others):
        return lax.optimization_barrier((x, others))[0]

    def swap_ctx(x, d):
        return lax.ppermute(x, "ctx", [(i, i ^ d) for i in range(ranks)])

    def exchange(x):
        return lax.all_to_all(x, "ctx", split_axis=0, concat_axis=0, tiled=True)

    marks = [x.astype(BF16).reshape(ranks, tokens // 128, 128) for x in (cluster_of, slot_of)]
    first = exchange(pack((queries, keys), jnp.concatenate(marks, axis=1)))
    marks = first[:, 2 * tokens :, :].astype(jnp.int32)
    target = marks[:, : tokens // 128, :] * SLOTS + marks[:, tokens // 128 :, :]
    target = target.reshape(ranks, 1, tokens)

    cols = out_weight.shape[1] // 4
    heads = me ^ jnp.array(LANES, jnp.int32)
    far = 2 * (1 - y)
    both = pick(heads, out_weight, (far + 1 - core, far + core), cols)
    both = swap_y(both)
    w_own = pick(heads, out_weight, (mine,), cols)
    beside = pick(heads, out_weight, (2 * y + 1 - core,), cols)
    beside, corner = swap_core(beside), swap_core(both[: both.shape[0] // 2])
    values = after(values, beside, w_own)
    weight = join(
        (w_own, both, beside, corner),
        (0, both.shape[0] // 2, 0, 0),
        ((0, 512), (512, 256), (768, 256)),
    )
    rows_v = exchange(after(pack((values,)), first))

    def paired(x):
        return x.reshape(CLUSTERS // PAIR, PAIR * cap, 128)

    q_rows, k_rows, at = place_pair(target, first, tokens)
    weights, means, early = weigh(paired(q_rows), paired(k_rows), paired(at), tokens)
    early = early.reshape(CLUSTERS, cap, 128)
    early, weights = (pltpu.with_memory_space_constraint(x, pltpu.HBM) for x in (early, weights))
    rows_v = after(rows_v, weight)
    mixed = mix(target, rows_v, early, weights).reshape(CLUSTERS, cap, 128)

    got, sent = {}, {}

    def leave(d, *others):
        block = unplace(after(jnp.reshape(me ^ d, (1,)), *others), target, mixed, means)
        sent[d] = block.reshape(block.shape[1:])

    def go(d):
        got[d] = swap_ctx(sent[d], d)

    def side(*blocks):
        return jnp.concatenate([block[:tokens] for block in blocks], axis=1)

    plan = (4, 2, 0, 3, 1, 5, 6, 7)
    waits = {5: (0,), 6: (4,), 7: (5, 9)}
    ends = {}
    for n, d in enumerate(plan):
        if d == 7:
            own_near = side(*[got[d] for d in LANES[1:4]])
            ends[9] = own_near
        others = [ends[k] for k in waits.get(d, ())]
        if n:
            others = [sent[plan[n - 1]]] + others
        leave(d, *others)
        if d:
            go(d)
            ends[d] = got[d]
        else:
            got[0] = sent[0]
            y_0 = ends[0] = swap_y(got[0])
    own, there = {}, {}
    y_near = swap_y(own_near)
    own[2] = side(got[4], got[5])
    there[2] = swap_y(own[2])
    own[3] = side(got[6], got[7])
    there[3] = swap_y(own[3])
    same = {1: side(got[0], own_near, y_0, y_near), 2: side(own[2], there[2])}

    def add(total, left, row):
        more = jnp.dot(left, weight[row : row + left.shape[1]], preferred_element_type=F32)
        return more if total is None else total + more

    total = None
    for n, row in ((1, 0), (2, 2048)):
        total = add(total, jnp.concatenate([same[n], swap_core(same[n])], axis=1), row)
    row = 3072
    total = add(total, swap_core(own[3]), row + 512)
    last = swap_core(after(there[3], total))
    total = add(total, side(own[3], there[3]), row)
    projected = add(total, last, row + 768).astype(BF16)

    tails = jnp.stack([got[d][tokens:] for d in range(ranks)]).astype(F32)
    tails = tails[:, :cl_dev] + tails[:, cl_dev:]
    tails = jnp.concatenate(
        [lax.dynamic_slice_in_dim(tails, me ^ d, 1, 0) for d in range(ranks)], axis=0
    )
    new_centroids = mix_rate * centroids + (1.0 - mix_rate) * tails
    return (projected, new_centroids)


def dispatch(queries, keys, values, cluster_of, *rest):
    ranks, heads = lax.axis_size("ctx"), cluster_of.shape[0]
    whole_heads = ranks == heads == 8 and lax.axis_size("head") == 4
    step = head_body if whole_heads else body
    return step(queries, keys, values, cluster_of, *rest)


def solution(mesh):
    in_specs = (
        P("ctx", "head"),
        P("ctx", "head"),
        P("ctx", "head"),
        P("head", "ctx"),
        P("head", "ctx"),
        P("head", "ctx", None),
        P("head", None),
    )
    out_specs = (P("ctx", "head"), P("head", "ctx", None))
    return jax.shard_map(
        dispatch, mesh=mesh, in_specs=in_specs, out_specs=out_specs, check_vma=False
    )
```

```python
import functools
import math

import jax
import jax.numpy as jnp
from jax import lax
from jax.experimental import pallas as pl
from jax.experimental.pallas import tpu as pltpu
from jax.sharding import PartitionSpec as P

CLUSTERS = 256
SLOTS = 8


mix_rate = 0.5
neg_fill = -1e30


def attend(q_rows, k_rows, v_rows, positions):
    scale = 1.0 / math.sqrt(q_rows.shape[-1])
    scores = jnp.einsum("gqd,gkd->gqk", q_rows, k_rows, preferred_element_type=jnp.float32) * scale
    allowed = (positions[:, None, :] >= 0) & (positions[:, None, :] <= positions[:, :, None])
    scores = jnp.where(allowed, scores, neg_fill)
    top = jnp.max(scores, axis=2, keepdims=True)
    weights = jnp.where(allowed, jnp.exp(scores - top), 0.0).astype(jnp.bfloat16)
    total = jnp.sum(weights.astype(jnp.float32), axis=2, keepdims=True)
    mixed = jnp.einsum("gqk,gkd->gqd", weights, v_rows, preferred_element_type=jnp.float32)
    return (mixed / jnp.where(total > 0.0, total, 1.0)).astype(jnp.bfloat16)


def to_clusters(rows, cl_dev):
    senders, width, items = (rows.shape[0], rows.shape[1], rows.shape[2])
    slots = width // cl_dev
    shaped = rows.reshape((senders, cl_dev, slots, items) + rows.shape[3:])
    if rows.ndim == 4:
        order = (3, 1, 0, 2, 4)
    else:
        order = (3, 1, 0, 2)
    return jnp.transpose(shaped, order).reshape((items * cl_dev, senders * slots) + rows.shape[3:])


def from_clusters(mixed, senders, cl_dev, items):
    slots = mixed.shape[1] // senders
    shaped = mixed.reshape(items, cl_dev, senders, slots, mixed.shape[2])
    return jnp.transpose(shaped, (2, 1, 3, 0, 4)).reshape(
        senders, cl_dev * slots, items, mixed.shape[2]
    )


def owner_work(incoming, cl_dev):
    q_in, k_in, v_in, p_in = incoming
    senders, items = (q_in.shape[0], q_in.shape[2])
    q_rows = to_clusters(q_in, cl_dev)
    k_rows = to_clusters(k_in, cl_dev)
    v_rows = to_clusters(v_in, cl_dev)
    p_rows = to_clusters(p_in, cl_dev)
    mixed = attend(q_rows, k_rows, v_rows, p_rows)
    back = from_clusters(mixed, senders, cl_dev, items)
    return back


def body(queries, keys, values, cluster_of, slot_of, centroids, out_weight):
    ranks = lax.axis_size("ctx")
    rank_here = lax.axis_index("ctx")
    tok_rows = queries.shape[0]
    head_rows = cluster_of.shape[0]
    head_size = queries.shape[1] // head_rows
    cl_dev = CLUSTERS // ranks
    width = CLUSTERS * SLOTS
    target = jnp.transpose(cluster_of * SLOTS + slot_of)
    head_ids = jnp.broadcast_to(jnp.arange(head_rows, dtype=jnp.int32)[None, :], target.shape)

    def place(rows):
        shaped = rows.reshape(tok_rows, head_rows, head_size)
        filled = (
            jnp.zeros((width, head_rows, head_size), rows.dtype).at[target, head_ids].set(shaped)
        )
        return filled.reshape(ranks, width // ranks, head_rows, head_size)

    token_pos = rank_here * tok_rows + jnp.arange(tok_rows, dtype=jnp.int32)
    pos_slots = (
        jnp.full((width, head_rows), -1, jnp.int32)
        .at[target, head_ids]
        .set(jnp.broadcast_to(token_pos[:, None], target.shape))
    )
    pos_slots = pos_slots.reshape(ranks, width // ranks, head_rows)
    incoming = (
        lax.all_to_all(place(queries), "ctx", split_axis=0, concat_axis=0, tiled=True),
        lax.all_to_all(place(keys), "ctx", split_axis=0, concat_axis=0, tiled=True),
        lax.all_to_all(place(values), "ctx", split_axis=0, concat_axis=0, tiled=True),
        lax.all_to_all(pos_slots, "ctx", split_axis=0, concat_axis=0, tiled=True),
    )
    worked = owner_work(incoming, cl_dev)
    returned = lax.all_to_all(worked, "ctx", split_axis=0, concat_axis=0, tiled=True)
    rows_back = returned.reshape(width, head_rows, head_size)
    attended = rows_back[target, head_ids].reshape(tok_rows, head_rows * head_size)
    member = (
        cluster_of[:, :, None] == jnp.arange(CLUSTERS, dtype=jnp.int32)[None, None, :]
    ).astype(jnp.bfloat16)
    q_three = queries.reshape(tok_rows, head_rows, head_size)
    k_three = keys.reshape(tok_rows, head_rows, head_size)
    local_sums = jnp.einsum("htc,thd->hcd", member, q_three, preferred_element_type=jnp.float32)
    local_sums = local_sums + jnp.einsum(
        "htc,thd->hcd", member, k_three, preferred_element_type=jnp.float32
    )
    local_counts = jnp.sum(member, axis=1, dtype=jnp.float32)
    totals, counts = (
        lax.psum_scatter(
            local_sums.astype(jnp.bfloat16), "ctx", scatter_dimension=1, tiled=True
        ).astype(jnp.float32),
        lax.psum_scatter(
            local_counts.astype(jnp.bfloat16), "ctx", scatter_dimension=1, tiled=True
        ).astype(jnp.float32),
    )
    means = totals / (2.0 * jnp.maximum(counts, 1.0))[:, :, None]
    new_centroids = mix_rate * centroids + (1.0 - mix_rate) * means
    summed = lax.psum_scatter(
        lax.dot_general(
            out_weight, attended, (((0,), (1,)), ((), ())), preferred_element_type=jnp.float32
        ),
        "head",
        scatter_dimension=0,
        tiled=True,
    )
    projected = jnp.transpose(summed).astype(jnp.bfloat16)
    return (projected, new_centroids)


BF16 = jnp.bfloat16
F32 = jnp.float32
PAIR = 2
EMPTY = 1e9
LANES = (0, 2, 3, 1, 4, 5, 6, 7)


def params(limit):
    return pltpu.CompilerParams(
        dimension_semantics=("arbitrary",), vmem_limit_bytes=limit * 1024 * 1024
    )


def cost(flops, nbytes, transcendentals=0):
    return pl.CostEstimate(
        flops=flops, bytes_accessed=nbytes, transcendentals=transcendentals
    )


def pack_kernel(count, marked, *refs):
    sources = refs[:count]
    out_ref, held, sems_in, sems_out = refs[count + marked :]
    heads = out_ref.shape[0]
    tokens = sources[0].shape[0]
    parts = 2
    rows = tokens // parts
    reads = []
    for n, source in enumerate(sources):
        for p in range(parts):
            here = pl.ds(p * rows, rows)
            reads.append(
                pltpu.make_async_copy(
                    source.at[here], held.at[n, here], sems_in.at[n * parts + p]
                )
            )
    for copy in reads:
        copy.start()
    writes = []
    if marked:
        marks_ref = refs[count]
        there = out_ref.at[:, pl.ds(count * tokens, marks_ref.shape[1])]
        writes.append(pltpu.make_async_copy(marks_ref, there, sems_out.at[0]))
        writes[0].start()
    for n in range(count):
        for p in range(parts):
            reads[n * parts + p].wait()
            for j in range(heads):
                copy = pltpu.make_async_copy(
                    held.at[n, pl.ds(p * rows, rows), pl.ds(j * 128, 128)],
                    out_ref.at[j, pl.ds(n * tokens + p * rows, rows)],
                    sems_out.at[1 + (n * parts + p) * heads + j],
                )
                copy.start()
                writes.append(copy)
    for copy in writes:
        copy.wait()


def pack(sources, marks=None):
    tokens, width = sources[0].shape
    heads, count = width // 128, len(sources)
    marked = marks is not None
    rows = count * tokens + (marks.shape[1] if marked else 0)
    anywhere = pl.BlockSpec(memory_space=pl.ANY)
    args = list(sources)
    in_specs = [anywhere] * count
    if marked:
        args.append(marks)
        in_specs.append(pl.BlockSpec(memory_space=pltpu.VMEM))
    return pl.pallas_call(
        functools.partial(pack_kernel, count, marked),
        in_specs=in_specs,
        out_specs=anywhere,
        out_shape=pltpu.HBM((heads, rows, 128), BF16),
        scratch_shapes=[
            pltpu.VMEM((count, tokens, width), BF16),
            pltpu.SemaphoreType.DMA((2 * count,)),
            pltpu.SemaphoreType.DMA((2 * count * heads + 1,)),
        ],
        compiler_params=pltpu.CompilerParams(vmem_limit_bytes=60 * 1024 * 1024),
        cost_estimate=cost(0, 2 * heads * rows * 256),
    )(*args)


def pick_kernel(count, where_ref, weight_ref, out_ref, sems):
    heads, cols = where_ref.shape[0] - count, out_ref.shape[1]
    copies = []
    for n in range(count):
        column = pl.multiple_of(where_ref[heads + n] * cols, cols)
        for lane in range(heads):
            row = pl.multiple_of(where_ref[lane] * 128, 128)
            copies.append(
                pltpu.make_async_copy(
                    weight_ref.at[pl.ds(row, 128), pl.ds(column, cols)],
                    out_ref.at[pl.ds((n * heads + lane) * 128, 128)],
                    sems.at[len(copies)],
                )
            )
    for copy in copies:
        copy.start()
    for copy in copies:
        copy.wait()


def pick(heads, weight, columns, cols):
    count = len(columns)
    where = jnp.concatenate([heads, jnp.stack(columns)])
    return pl.pallas_call(
        functools.partial(pick_kernel, count),
        in_specs=[pl.BlockSpec(memory_space=pltpu.SMEM), pl.BlockSpec(memory_space=pl.ANY)],
        out_specs=pl.BlockSpec(memory_space=pltpu.VMEM),
        out_shape=pltpu.HBM((count * weight.shape[0], cols), BF16),
        scratch_shapes=[pltpu.SemaphoreType.DMA((heads.shape[0] * count,))],
        compiler_params=pltpu.CompilerParams(vmem_limit_bytes=56 * 1024 * 1024),
        cost_estimate=cost(1, 1),
    )(where, pltpu.with_memory_space_constraint(weight, pltpu.HBM))


def join_kernel(plan, *refs):
    sources, out_ref, sems = refs[:-2], refs[-2], refs[-1]
    copies, row = [], 0
    for part, first, count in plan:
        copies.append(
            pltpu.make_async_copy(
                sources[part].at[pl.ds(first, count)],
                out_ref.at[pl.ds(row, count)],
                sems.at[len(copies)],
            )
        )
        row += count
    for copy in copies:
        copy.start()
    for copy in copies:
        copy.wait()


def join(sources, starts, groups):
    plan = [(part, at + first, count) for first, count in groups for part, at in enumerate(starts)]
    rows, cols = sum(count for _, _, count in plan), sources[0].shape[1]
    return pl.pallas_call(
        functools.partial(join_kernel, plan),
        in_specs=[pl.BlockSpec(memory_space=pl.ANY)] * len(sources),
        out_specs=pl.BlockSpec(memory_space=pltpu.VMEM),
        out_shape=pltpu.HBM((rows, cols), BF16),
        scratch_shapes=[pltpu.SemaphoreType.DMA((len(plan),))],
        compiler_params=pltpu.CompilerParams(vmem_limit_bytes=56 * 1024 * 1024),
        cost_estimate=cost(1, 1),
    )(*sources)


def match(first, count, target):
    rows = first + lax.broadcasted_iota(jnp.int32, (count, target.shape[1]), 0)
    return rows == target


def by_slot(x):
    return x.reshape(x.shape[0] // SLOTS, SLOTS, 128)


def place_pair_kernel(target_ref, q_ref, k_ref, q_out, k_out, p_out, right):
    tokens = q_ref.shape[1]
    slots = q_out.shape[0] * SLOTS
    step = 1024
    right[:, :128] = q_ref[0]
    right[:, 128:] = k_ref[0]
    base = pl.program_id(0) * tokens
    token = (base + lax.broadcasted_iota(jnp.int32, (1, tokens), 1)).astype(F32)
    target = target_ref[0]

    def move(i, carry):
        picked = match(i * step, step, target)
        out = jnp.dot(picked.astype(BF16), right[...], preferred_element_type=F32)
        where = pl.ds(i * (step // SLOTS), step // SLOTS)
        q_out[where] = by_slot(out[:, :128]).astype(BF16)
        k_out[where] = by_slot(out[:, 128:]).astype(BF16)
        at = jnp.min(jnp.where(picked, token, EMPTY), axis=1, keepdims=True)
        p_out[where] = by_slot(jnp.broadcast_to(at, (step, 128)))
        return carry

    lax.fori_loop(0, slots // step, move, 0)


def place_pair(target, first, tokens):
    ranks = first.shape[0]
    spec_out = pl.BlockSpec((CLUSTERS, SLOTS, 128), lambda j: (0, j, 0))
    shape = (CLUSTERS, ranks * SLOTS, 128)
    return pl.pallas_call(
        place_pair_kernel,
        grid=(ranks,),
        in_specs=[
            pl.BlockSpec((1, 1, tokens), lambda j: (j, 0, 0)),
            pl.BlockSpec((1, tokens, 128), lambda j: (j, 0, 0)),
            pl.BlockSpec((1, tokens, 128), lambda j: (j, 1, 0)),
        ],
        out_specs=[spec_out, spec_out, spec_out],
        out_shape=[
            jax.ShapeDtypeStruct(shape, BF16),
            jax.ShapeDtypeStruct(shape, BF16),
            jax.ShapeDtypeStruct(shape, F32),
        ],
        scratch_shapes=[pltpu.VMEM((tokens, 256), BF16)],
        compiler_params=params(16),
        cost_estimate=cost(1, 1),
    )(target, first, first)


def weigh_kernel(tokens, q_ref, k_ref, p_ref, w_out, mean_out, early_out):
    count, rows = q_ref.shape[0], q_ref.shape[1]
    cap = rows // PAIR
    scale = 1.0 / math.sqrt(q_ref.shape[2])
    same = (
        lax.broadcasted_iota(jnp.int32, (rows, rows), 0) // cap
        == lax.broadcasted_iota(jnp.int32, (rows, rows), 1) // cap
    )
    for n in range(count):
        q, k, own = q_ref[n], k_ref[n], p_ref[n]
        scores = lax.dot_general(q, k, (((1,), (1,)), ((), ())), preferred_element_type=F32) * scale
        allowed = same & (jnp.transpose(own) <= own)
        scores = jnp.where(allowed, scores, neg_fill)
        top = jnp.max(scores, axis=1, keepdims=True)
        w_out[n] = jnp.where(allowed, jnp.exp(scores - top), 0.0).astype(BF16)
    share = p_ref[...] * (1.0 / tokens)
    early_out[...] = (share - jnp.floor(share) < 0.5).astype(BF16)
    both = (q_ref[...].astype(F32) + k_ref[...].astype(F32)).reshape(count * PAIR, cap, 128)
    held = (p_ref[...] < EMPTY).astype(F32).reshape(count * PAIR, cap, 128)
    mean_out[...] = jnp.sum(both, axis=1) / (2.0 * jnp.maximum(jnp.sum(held, axis=1), 1.0))


def weigh(q_rows, k_rows, at, tokens, step=16):
    groups, rows = q_rows.shape[0], q_rows.shape[1]
    spec = pl.BlockSpec((step, rows, 128), lambda i: (i, 0, 0))
    return pl.pallas_call(
        functools.partial(weigh_kernel, tokens),
        grid=(groups // step,),
        in_specs=[spec, spec, spec],
        out_specs=[
            pl.BlockSpec((step, rows, rows), lambda i: (i, 0, 0)),
            pl.BlockSpec((step * PAIR, 128), lambda i: (i, 0)),
            spec,
        ],
        out_shape=[
            pltpu.HBM((groups, rows, rows), BF16),
            jax.ShapeDtypeStruct((groups * PAIR, 128), F32),
            pltpu.HBM((groups, rows, 128), BF16),
        ],
        compiler_params=params(16),
        cost_estimate=cost(1, 1),
    )(q_rows, k_rows, at)


def mix_kernel(steps, target_ref, v_ref, early_ref, w_ref, o_out, v_rows):
    i = pl.program_id(0)
    slots = v_rows.shape[0] * SLOTS
    senders, tokens = v_ref.shape[0], v_ref.shape[1]
    count, rows = w_ref.shape[0], w_ref.shape[1]
    half = tokens // 2

    @pl.when(i < steps)
    def _():
        for n in range(senders):
            target = target_ref[n]
            picked = match(0, slots, target[:, :half]) | match(0, slots, target[:, half:])
            both = jnp.concatenate([v_ref[n, :half], v_ref[n, half:]], axis=1)
            out = jnp.dot(picked.astype(BF16), both, preferred_element_type=F32)
            early = early_ref[:, n * SLOTS : (n + 1) * SLOTS].astype(F32) > 0.0
            where = pl.ds(pl.multiple_of((i * senders + n) * SLOTS, SLOTS), SLOTS)
            v_rows[:, where, :] = jnp.where(early, by_slot(out[:, :128]), by_slot(out[:, 128:]))

    @pl.when(i >= steps)
    def _():
        ones = jnp.ones((rows, 128), BF16)
        for n in range(count):
            own = v_rows[pl.ds(((i - steps) * count + n) * PAIR, PAIR)]
            right = jnp.concatenate([own.reshape(rows, 128).astype(BF16), ones], axis=1)
            out = jnp.dot(w_ref[n], right, preferred_element_type=F32)
            total = out[:, 128:]
            o_out[n] = (out[:, :128] / jnp.where(total > 0.0, total, 1.0)).astype(BF16)


def mix(target, rows_v, early, weights, senders=4, count=32):
    ranks, tokens = rows_v.shape[0], rows_v.shape[1]
    groups, rows = weights.shape[0], weights.shape[1]
    steps = ranks // senders

    def sender(i):
        return jnp.minimum(i, steps - 1)

    def group(i):
        return jnp.maximum(i - steps, 0)

    return pl.pallas_call(
        functools.partial(mix_kernel, steps),
        grid=(steps + groups // count,),
        in_specs=[
            pl.BlockSpec((senders, 1, tokens), lambda i: (sender(i), 0, 0)),
            pl.BlockSpec((senders, tokens, 128), lambda i: (sender(i), 0, 0)),
            pl.BlockSpec((CLUSTERS, senders * SLOTS, 128), lambda i: (0, sender(i), 0)),
            pl.BlockSpec((count, rows, rows), lambda i: (group(i), 0, 0)),
        ],
        out_specs=pl.BlockSpec((count, rows, 128), lambda i: (group(i), 0, 0)),
        out_shape=jax.ShapeDtypeStruct((groups, rows, 128), BF16),
        scratch_shapes=[pltpu.VMEM((CLUSTERS, ranks * SLOTS, 128), F32)],
        compiler_params=params(22),
        cost_estimate=cost(1, 1),
    )(target, rows_v, early, weights)


def unplace_kernel(who_ref, target_ref, o_ref, mean_ref, out_ref):
    tokens = target_ref.shape[2]
    half = o_ref.shape[0] // 2 * SLOTS
    right = o_ref[...].astype(F32).reshape(2 * half, 128).astype(BF16)
    right = jnp.concatenate([right[:half], right[half:]], axis=1)
    target = jnp.transpose(jnp.broadcast_to(target_ref[0], (128, tokens)))
    low = jnp.where(target < half, target, target - half)
    columns = lax.broadcasted_iota(jnp.int32, (tokens, half), 1)
    picked = (columns == jnp.tile(low, (1, half // 128))).astype(BF16)
    out = jnp.dot(picked, right, preferred_element_type=F32)
    out_ref[0, :tokens] = jnp.where(target < half, out[:, :128], out[:, 128:]).astype(BF16)
    means = mean_ref[...]
    high = means.astype(BF16)
    count = means.shape[0]
    out_ref[0, tokens : tokens + count] = high
    out_ref[0, tokens + count :] = (means - high.astype(F32)).astype(BF16)


def unplace(who, target, mixed, means):
    tokens, partners = target.shape[2], who.shape[0]
    count = CLUSTERS // target.shape[0]
    return pl.pallas_call(
        unplace_kernel,
        grid_spec=pltpu.PrefetchScalarGridSpec(
            num_scalar_prefetch=1,
            grid=(partners,),
            in_specs=[
                pl.BlockSpec((1, 1, tokens), lambda i, who: (who[i], 0, 0)),
                pl.BlockSpec((CLUSTERS, SLOTS, 128), lambda i, who: (0, who[i], 0)),
                pl.BlockSpec((count, 128), lambda i, who: (who[i], 0)),
            ],
            out_specs=pl.BlockSpec((1, tokens + 2 * count, 128), lambda i, who: (i, 0, 0)),
        ),
        out_shape=jax.ShapeDtypeStruct((partners, tokens + 2 * count, 128), BF16),
        compiler_params=params(12),
        cost_estimate=cost(1, 1),
    )(who, target, mixed, means)


def head_body(queries, keys, values, cluster_of, slot_of, centroids, out_weight):
    ranks = lax.axis_size("ctx")
    me = lax.axis_index("ctx")
    mine = lax.axis_index("head")
    tokens = queries.shape[0]
    cl_dev = CLUSTERS // ranks
    cap = ranks * SLOTS
    y, core = mine // 2, mine % 2

    def swap_y(x):
        return lax.ppermute(x, "head", [(0, 2), (1, 3), (2, 0), (3, 1)])

    def swap_core(x):
        return lax.ppermute(x, "head", [(0, 1), (1, 0), (2, 3), (3, 2)])

    def after(x, *others):
        return lax.optimization_barrier((x, others))[0]

    def swap_ctx(x, d):
        return lax.ppermute(x, "ctx", [(i, i ^ d) for i in range(ranks)])

    def exchange(x):
        return lax.all_to_all(x, "ctx", split_axis=0, concat_axis=0, tiled=True)

    marks = [x.astype(BF16).reshape(ranks, tokens // 128, 128) for x in (cluster_of, slot_of)]
    first = exchange(pack((queries, keys), jnp.concatenate(marks, axis=1)))
    marks = first[:, 2 * tokens :, :].astype(jnp.int32)
    target = marks[:, : tokens // 128, :] * SLOTS + marks[:, tokens // 128 :, :]
    target = target.reshape(ranks, 1, tokens)

    cols = out_weight.shape[1] // 4
    heads = me ^ jnp.array(LANES, jnp.int32)
    far = 2 * (1 - y)
    both = pick(heads, out_weight, (far + 1 - core, far + core), cols)
    both = swap_y(both)
    w_own = pick(heads, out_weight, (mine,), cols)
    beside = pick(heads, out_weight, (2 * y + 1 - core,), cols)
    beside, corner = swap_core(beside), swap_core(both[: both.shape[0] // 2])
    values = after(values, beside, w_own)
    weight = join(
        (w_own, both, beside, corner),
        (0, both.shape[0] // 2, 0, 0),
        ((0, 512), (512, 256), (768, 256)),
    )
    rows_v = exchange(after(pack((values,)), first))

    def paired(x):
        return x.reshape(CLUSTERS // PAIR, PAIR * cap, 128)

    q_rows, k_rows, at = place_pair(target, first, tokens)
    weights, means, early = weigh(paired(q_rows), paired(k_rows), paired(at), tokens)
    early = early.reshape(CLUSTERS, cap, 128)
    early, weights = (pltpu.with_memory_space_constraint(x, pltpu.HBM) for x in (early, weights))
    rows_v = after(rows_v, weight)
    mixed = mix(target, rows_v, early, weights).reshape(CLUSTERS, cap, 128)

    got, sent = {}, {}

    def leave(d, *others):
        block = unplace(after(jnp.reshape(me ^ d, (1,)), *others), target, mixed, means)
        sent[d] = block.reshape(block.shape[1:])

    def go(d):
        got[d] = swap_ctx(sent[d], d)

    def side(*blocks):
        return jnp.concatenate([block[:tokens] for block in blocks], axis=1)

    plan = (4, 2, 0, 3, 1, 5, 6, 7)
    waits = {5: (0,), 6: (4,), 7: (5, 9)}
    ends = {}
    for n, d in enumerate(plan):
        if d == 7:
            own_near = side(*[got[d] for d in LANES[1:4]])
            ends[9] = own_near
        others = [ends[k] for k in waits.get(d, ())]
        if n:
            others = [sent[plan[n - 1]]] + others
        leave(d, *others)
        if d:
            go(d)
            ends[d] = got[d]
        else:
            got[0] = sent[0]
            y_0 = ends[0] = swap_y(got[0])
    own, there = {}, {}
    y_near = swap_y(own_near)
    own[2] = side(got[4], got[5])
    there[2] = swap_y(own[2])
    own[3] = side(got[6], got[7])
    there[3] = swap_y(own[3])
    same = {1: side(got[0], own_near, y_0, y_near), 2: side(own[2], there[2])}

    def add(total, left, row):
        more = jnp.dot(left, weight[row : row + left.shape[1]], preferred_element_type=F32)
        return more if total is None else total + more

    total = None
    for n, row in ((1, 0), (2, 2048)):
        total = add(total, jnp.concatenate([same[n], swap_core(same[n])], axis=1), row)
    row = 3072
    total = add(total, swap_core(own[3]), row + 512)
    last = swap_core(after(there[3], total))
    total = add(total, side(own[3], there[3]), row)
    projected = add(total, last, row + 768).astype(BF16)

    tails = jnp.stack([got[d][tokens:] for d in range(ranks)]).astype(F32)
    tails = tails[:, :cl_dev] + tails[:, cl_dev:]
    tails = jnp.concatenate(
        [lax.dynamic_slice_in_dim(tails, me ^ d, 1, 0) for d in range(ranks)], axis=0
    )
    new_centroids = mix_rate * centroids + (1.0 - mix_rate) * tails
    return (projected, new_centroids)


def dispatch(queries, keys, values, cluster_of, *rest):
    ranks, heads = lax.axis_size("ctx"), cluster_of.shape[0]
    whole_heads = ranks == heads == 8 and lax.axis_size("head") == 4
    step = head_body if whole_heads else body
    return step(queries, keys, values, cluster_of, *rest)


def solution(mesh):
    in_specs = (
        P("ctx", "head"),
        P("ctx", "head"),
        P("ctx", "head"),
        P("head", "ctx"),
        P("head", "ctx"),
        P("head", "ctx", None),
        P("head", None),
    )
    out_specs = (P("ctx", "head"), P("head", "ctx", None))
    return jax.shard_map(
        dispatch, mesh=mesh, in_specs=in_specs, out_specs=out_specs, check_vma=False
    )
```

```python
import functools
import math

import jax
import jax.numpy as jnp
from jax import lax
from jax.experimental import pallas as pl
from jax.experimental.pallas import tpu as pltpu
from jax.sharding import PartitionSpec as P

CLUSTERS = 256
SLOTS = 8


mix_rate = 0.5
neg_fill = -1e30


def attend(q_rows, k_rows, v_rows, positions):
    scale = 1.0 / math.sqrt(q_rows.shape[-1])
    scores = jnp.einsum("gqd,gkd->gqk", q_rows, k_rows, preferred_element_type=jnp.float32) * scale
    allowed = (positions[:, None, :] >= 0) & (positions[:, None, :] <= positions[:, :, None])
    scores = jnp.where(allowed, scores, neg_fill)
    top = jnp.max(scores, axis=2, keepdims=True)
    weights = jnp.where(allowed, jnp.exp(scores - top), 0.0).astype(jnp.bfloat16)
    total = jnp.sum(weights.astype(jnp.float32), axis=2, keepdims=True)
    mixed = jnp.einsum("gqk,gkd->gqd", weights, v_rows, preferred_element_type=jnp.float32)
    return (mixed / jnp.where(total > 0.0, total, 1.0)).astype(jnp.bfloat16)


def to_clusters(rows, cl_dev):
    senders, width, items = (rows.shape[0], rows.shape[1], rows.shape[2])
    slots = width // cl_dev
    shaped = rows.reshape((senders, cl_dev, slots, items) + rows.shape[3:])
    if rows.ndim == 4:
        order = (3, 1, 0, 2, 4)
    else:
        order = (3, 1, 0, 2)
    return jnp.transpose(shaped, order).reshape((items * cl_dev, senders * slots) + rows.shape[3:])


def from_clusters(mixed, senders, cl_dev, items):
    slots = mixed.shape[1] // senders
    shaped = mixed.reshape(items, cl_dev, senders, slots, mixed.shape[2])
    return jnp.transpose(shaped, (2, 1, 3, 0, 4)).reshape(
        senders, cl_dev * slots, items, mixed.shape[2]
    )


def owner_work(incoming, cl_dev):
    q_in, k_in, v_in, p_in = incoming
    senders, items = (q_in.shape[0], q_in.shape[2])
    q_rows = to_clusters(q_in, cl_dev)
    k_rows = to_clusters(k_in, cl_dev)
    v_rows = to_clusters(v_in, cl_dev)
    p_rows = to_clusters(p_in, cl_dev)
    mixed = attend(q_rows, k_rows, v_rows, p_rows)
    back = from_clusters(mixed, senders, cl_dev, items)
    return back


def body(queries, keys, values, cluster_of, slot_of, centroids, out_weight):
    ranks = lax.axis_size("ctx")
    rank_here = lax.axis_index("ctx")
    tok_rows = queries.shape[0]
    head_rows = cluster_of.shape[0]
    head_size = queries.shape[1] // head_rows
    cl_dev = CLUSTERS // ranks
    width = CLUSTERS * SLOTS
    target = jnp.transpose(cluster_of * SLOTS + slot_of)
    head_ids = jnp.broadcast_to(jnp.arange(head_rows, dtype=jnp.int32)[None, :], target.shape)

    def place(rows):
        shaped = rows.reshape(tok_rows, head_rows, head_size)
        filled = (
            jnp.zeros((width, head_rows, head_size), rows.dtype).at[target, head_ids].set(shaped)
        )
        return filled.reshape(ranks, width // ranks, head_rows, head_size)

    token_pos = rank_here * tok_rows + jnp.arange(tok_rows, dtype=jnp.int32)
    pos_slots = (
        jnp.full((width, head_rows), -1, jnp.int32)
        .at[target, head_ids]
        .set(jnp.broadcast_to(token_pos[:, None], target.shape))
    )
    pos_slots = pos_slots.reshape(ranks, width // ranks, head_rows)
    incoming = (
        lax.all_to_all(place(queries), "ctx", split_axis=0, concat_axis=0, tiled=True),
        lax.all_to_all(place(keys), "ctx", split_axis=0, concat_axis=0, tiled=True),
        lax.all_to_all(place(values), "ctx", split_axis=0, concat_axis=0, tiled=True),
        lax.all_to_all(pos_slots, "ctx", split_axis=0, concat_axis=0, tiled=True),
    )
    worked = owner_work(incoming, cl_dev)
    returned = lax.all_to_all(worked, "ctx", split_axis=0, concat_axis=0, tiled=True)
    rows_back = returned.reshape(width, head_rows, head_size)
    attended = rows_back[target, head_ids].reshape(tok_rows, head_rows * head_size)
    member = (
        cluster_of[:, :, None] == jnp.arange(CLUSTERS, dtype=jnp.int32)[None, None, :]
    ).astype(jnp.bfloat16)
    q_three = queries.reshape(tok_rows, head_rows, head_size)
    k_three = keys.reshape(tok_rows, head_rows, head_size)
    local_sums = jnp.einsum("htc,thd->hcd", member, q_three, preferred_element_type=jnp.float32)
    local_sums = local_sums + jnp.einsum(
        "htc,thd->hcd", member, k_three, preferred_element_type=jnp.float32
    )
    local_counts = jnp.sum(member, axis=1, dtype=jnp.float32)
    totals, counts = (
        lax.psum_scatter(
            local_sums.astype(jnp.bfloat16), "ctx", scatter_dimension=1, tiled=True
        ).astype(jnp.float32),
        lax.psum_scatter(
            local_counts.astype(jnp.bfloat16), "ctx", scatter_dimension=1, tiled=True
        ).astype(jnp.float32),
    )
    means = totals / (2.0 * jnp.maximum(counts, 1.0))[:, :, None]
    new_centroids = mix_rate * centroids + (1.0 - mix_rate) * means
    summed = lax.psum_scatter(
        lax.dot_general(
            out_weight, attended, (((0,), (1,)), ((), ())), preferred_element_type=jnp.float32
        ),
        "head",
        scatter_dimension=0,
        tiled=True,
    )
    projected = jnp.transpose(summed).astype(jnp.bfloat16)
    return (projected, new_centroids)


BF16 = jnp.bfloat16
F32 = jnp.float32
PAIR = 2
EMPTY = 1e9
LANES = (0, 2, 3, 1, 4, 5, 6, 7)


def params(limit):
    return pltpu.CompilerParams(
        dimension_semantics=("arbitrary",), vmem_limit_bytes=limit * 1024 * 1024
    )


def cost(flops, nbytes, transcendentals=0):
    return pl.CostEstimate(
        flops=flops, bytes_accessed=nbytes, transcendentals=transcendentals
    )


def pack_kernel(count, marked, *refs):
    sources = refs[:count]
    out_ref, held, wide, marks, sems_in, sems_out = refs[count + 2 * marked :]
    heads = out_ref.shape[0]
    tokens = sources[0].shape[0]
    parts = 2
    rows = tokens // parts
    reads = []
    for n, source in enumerate(sources):
        for p in range(parts):
            here = pl.ds(p * rows, rows)
            reads.append(
                pltpu.make_async_copy(
                    source.at[here], held.at[n, here], sems_in.at[n * parts + p]
                )
            )
    for copy in reads:
        copy.start()
    writes = []
    if marked:
        lines = marks.shape[1] // 2
        for n in range(2):
            mark = refs[count + n][...].astype(F32)
            for line in range(lines):
                wide[:, n * lines + line, :] = mark[:, line * 128 : (line + 1) * 128]
        marks[...] = wide[...].astype(BF16)
        there = out_ref.at[:, pl.ds(count * tokens, 2 * lines)]
        writes.append(pltpu.make_async_copy(marks, there, sems_out.at[0]))
        writes[0].start()
    for n in range(count):
        for p in range(parts):
            reads[n * parts + p].wait()
            for j in range(heads):
                copy = pltpu.make_async_copy(
                    held.at[n, pl.ds(p * rows, rows), pl.ds(j * 128, 128)],
                    out_ref.at[j, pl.ds(n * tokens + p * rows, rows)],
                    sems_out.at[1 + (n * parts + p) * heads + j],
                )
                copy.start()
                writes.append(copy)
    for copy in writes:
        copy.wait()


def pack(sources, marks=()):
    tokens, width = sources[0].shape
    heads, count = width // 128, len(sources)
    marked = len(marks) > 0
    lines = len(marks) * (tokens // 128)
    rows = count * tokens + lines
    anywhere = pl.BlockSpec(memory_space=pl.ANY)
    args = list(sources)
    in_specs = [anywhere] * count
    for mark in marks:
        args.append(mark)
        in_specs.append(pl.BlockSpec(memory_space=pltpu.VMEM))
    return pl.pallas_call(
        functools.partial(pack_kernel, count, marked),
        in_specs=in_specs,
        out_specs=anywhere,
        out_shape=pltpu.HBM((heads, rows, 128), BF16),
        scratch_shapes=[
            pltpu.VMEM((count, tokens, width), BF16),
            pltpu.VMEM((heads, max(lines, 16), 128), F32),
            pltpu.VMEM((heads, max(lines, 16), 128), BF16),
            pltpu.SemaphoreType.DMA((2 * count,)),
            pltpu.SemaphoreType.DMA((2 * count * heads + 1,)),
        ],
        compiler_params=pltpu.CompilerParams(vmem_limit_bytes=60 * 1024 * 1024),
        cost_estimate=cost(0, 2 * heads * rows * 256),
    )(*args)


def pick_kernel(count, where_ref, weight_ref, out_ref, sems):
    heads, cols = where_ref.shape[0] - count, out_ref.shape[1]
    copies = []
    for n in range(count):
        column = pl.multiple_of(where_ref[heads + n] * cols, cols)
        for lane in range(heads):
            row = pl.multiple_of(where_ref[lane] * 128, 128)
            copies.append(
                pltpu.make_async_copy(
                    weight_ref.at[pl.ds(row, 128), pl.ds(column, cols)],
                    out_ref.at[pl.ds((n * heads + lane) * 128, 128)],
                    sems.at[len(copies)],
                )
            )
    for copy in copies:
        copy.start()
    for copy in copies:
        copy.wait()


def pick(heads, weight, columns, cols):
    count = len(columns)
    where = jnp.concatenate([heads, jnp.stack(columns)])
    return pl.pallas_call(
        functools.partial(pick_kernel, count),
        in_specs=[pl.BlockSpec(memory_space=pltpu.SMEM), pl.BlockSpec(memory_space=pl.ANY)],
        out_specs=pl.BlockSpec(memory_space=pltpu.VMEM),
        out_shape=pltpu.HBM((count * weight.shape[0], cols), BF16),
        scratch_shapes=[pltpu.SemaphoreType.DMA((heads.shape[0] * count,))],
        compiler_params=pltpu.CompilerParams(vmem_limit_bytes=56 * 1024 * 1024),
        cost_estimate=cost(1, 1),
    )(where, pltpu.with_memory_space_constraint(weight, pltpu.HBM))


def join_kernel(plan, *refs):
    sources, out_ref, sems = refs[:-2], refs[-2], refs[-1]
    copies, row = [], 0
    for part, first, count in plan:
        copies.append(
            pltpu.make_async_copy(
                sources[part].at[pl.ds(first, count)],
                out_ref.at[pl.ds(row, count)],
                sems.at[len(copies)],
            )
        )
        row += count
    for copy in copies:
        copy.start()
    for copy in copies:
        copy.wait()


def join(sources, starts, groups):
    plan = [(part, at + first, count) for first, count in groups for part, at in enumerate(starts)]
    rows, cols = sum(count for _, _, count in plan), sources[0].shape[1]
    return pl.pallas_call(
        functools.partial(join_kernel, plan),
        in_specs=[pl.BlockSpec(memory_space=pl.ANY)] * len(sources),
        out_specs=pl.BlockSpec(memory_space=pltpu.VMEM),
        out_shape=pltpu.HBM((rows, cols), BF16),
        scratch_shapes=[pltpu.SemaphoreType.DMA((len(plan),))],
        compiler_params=pltpu.CompilerParams(vmem_limit_bytes=56 * 1024 * 1024),
        cost_estimate=cost(1, 1),
    )(*sources)


def match(first, count, target):
    rows = first + lax.broadcasted_iota(jnp.int32, (count, target.shape[1]), 0)
    return rows == target


def by_slot(x):
    return x.reshape(x.shape[0] // SLOTS, SLOTS, 128)


def place_pair_kernel(target_ref, q_ref, k_ref, q_out, k_out, p_out, right):
    tokens = q_ref.shape[1]
    slots = q_out.shape[0] * SLOTS
    step = 1024
    right[:, :128] = q_ref[0]
    right[:, 128:] = k_ref[0]
    base = pl.program_id(0) * tokens
    token = (base + lax.broadcasted_iota(jnp.int32, (1, tokens), 1)).astype(F32)
    target = target_ref[0]

    def move(i, carry):
        picked = match(i * step, step, target)
        out = jnp.dot(picked.astype(BF16), right[...], preferred_element_type=F32)
        where = pl.ds(i * (step // SLOTS), step // SLOTS)
        q_out[where] = by_slot(out[:, :128]).astype(BF16)
        k_out[where] = by_slot(out[:, 128:]).astype(BF16)
        at = jnp.min(jnp.where(picked, token, EMPTY), axis=1, keepdims=True)
        p_out[where] = by_slot(jnp.broadcast_to(at, (step, 128)))
        return carry

    lax.fori_loop(0, slots // step, move, 0)


def place_pair(target, first, tokens):
    ranks = first.shape[0]
    spec_out = pl.BlockSpec((CLUSTERS, SLOTS, 128), lambda j: (0, j, 0))
    shape = (CLUSTERS, ranks * SLOTS, 128)
    return pl.pallas_call(
        place_pair_kernel,
        grid=(ranks,),
        in_specs=[
            pl.BlockSpec((1, 1, tokens), lambda j: (j, 0, 0)),
            pl.BlockSpec((1, tokens, 128), lambda j: (j, 0, 0)),
            pl.BlockSpec((1, tokens, 128), lambda j: (j, 1, 0)),
        ],
        out_specs=[spec_out, spec_out, spec_out],
        out_shape=[
            jax.ShapeDtypeStruct(shape, BF16),
            jax.ShapeDtypeStruct(shape, BF16),
            jax.ShapeDtypeStruct(shape, F32),
        ],
        scratch_shapes=[pltpu.VMEM((tokens, 256), BF16)],
        compiler_params=params(16),
        cost_estimate=cost(1, 1),
    )(target, first, first)


def weigh_kernel(tokens, q_ref, k_ref, p_ref, w_out, mean_out, early_out):
    count, rows = q_ref.shape[0], q_ref.shape[1]
    cap = rows // PAIR
    scale = 1.0 / math.sqrt(q_ref.shape[2])
    same = (
        lax.broadcasted_iota(jnp.int32, (rows, rows), 0) // cap
        == lax.broadcasted_iota(jnp.int32, (rows, rows), 1) // cap
    )
    for n in range(count):
        q, k, own = q_ref[n], k_ref[n], p_ref[n]
        scores = lax.dot_general(q, k, (((1,), (1,)), ((), ())), preferred_element_type=F32) * scale
        allowed = same & (jnp.transpose(own) <= own)
        scores = jnp.where(allowed, scores, neg_fill)
        top = jnp.max(scores, axis=1, keepdims=True)
        w_out[n] = jnp.where(allowed, jnp.exp(scores - top), 0.0).astype(BF16)
    share = p_ref[...] * (1.0 / tokens)
    early_out[...] = (share - jnp.floor(share) < 0.5).astype(BF16)
    both = (q_ref[...].astype(F32) + k_ref[...].astype(F32)).reshape(count * PAIR, cap, 128)
    held = (p_ref[...] < EMPTY).astype(F32).reshape(count * PAIR, cap, 128)
    mean_out[...] = jnp.sum(both, axis=1) / (2.0 * jnp.maximum(jnp.sum(held, axis=1), 1.0))


def weigh(q_rows, k_rows, at, tokens, step=16):
    groups, rows = q_rows.shape[0], q_rows.shape[1]
    spec = pl.BlockSpec((step, rows, 128), lambda i: (i, 0, 0))
    return pl.pallas_call(
        functools.partial(weigh_kernel, tokens),
        grid=(groups // step,),
        in_specs=[spec, spec, spec],
        out_specs=[
            pl.BlockSpec((step, rows, rows), lambda i: (i, 0, 0)),
            pl.BlockSpec((step * PAIR, 128), lambda i: (i, 0)),
            spec,
        ],
        out_shape=[
            pltpu.HBM((groups, rows, rows), BF16),
            jax.ShapeDtypeStruct((groups * PAIR, 128), F32),
            pltpu.HBM((groups, rows, 128), BF16),
        ],
        compiler_params=params(16),
        cost_estimate=cost(1, 1),
    )(q_rows, k_rows, at)


def mix_kernel(steps, target_ref, v_ref, early_ref, w_ref, o_out, v_rows):
    i = pl.program_id(0)
    slots = v_rows.shape[0] * SLOTS
    senders, tokens = v_ref.shape[0], v_ref.shape[1]
    count, rows = w_ref.shape[0], w_ref.shape[1]
    half = tokens // 2

    @pl.when(i < steps)
    def _():
        for n in range(senders):
            target = target_ref[n]
            picked = match(0, slots, target[:, :half]) | match(0, slots, target[:, half:])
            both = jnp.concatenate([v_ref[n, :half], v_ref[n, half:]], axis=1)
            out = jnp.dot(picked.astype(BF16), both, preferred_element_type=F32)
            early = early_ref[:, n * SLOTS : (n + 1) * SLOTS].astype(F32) > 0.0
            where = pl.ds(pl.multiple_of((i * senders + n) * SLOTS, SLOTS), SLOTS)
            v_rows[:, where, :] = jnp.where(early, by_slot(out[:, :128]), by_slot(out[:, 128:]))

    @pl.when(i >= steps)
    def _():
        ones = jnp.ones((rows, 128), BF16)
        for n in range(count):
            own = v_rows[pl.ds(((i - steps) * count + n) * PAIR, PAIR)]
            right = jnp.concatenate([own.reshape(rows, 128).astype(BF16), ones], axis=1)
            out = jnp.dot(w_ref[n], right, preferred_element_type=F32)
            total = out[:, 128:]
            o_out[n] = (out[:, :128] / jnp.where(total > 0.0, total, 1.0)).astype(BF16)


def mix(target, rows_v, early, weights, senders=4, count=32):
    ranks, tokens = rows_v.shape[0], rows_v.shape[1]
    groups, rows = weights.shape[0], weights.shape[1]
    steps = ranks // senders

    def sender(i):
        return jnp.minimum(i, steps - 1)

    def group(i):
        return jnp.maximum(i - steps, 0)

    return pl.pallas_call(
        functools.partial(mix_kernel, steps),
        grid=(steps + groups // count,),
        in_specs=[
            pl.BlockSpec((senders, 1, tokens), lambda i: (sender(i), 0, 0)),
            pl.BlockSpec((senders, tokens, 128), lambda i: (sender(i), 0, 0)),
            pl.BlockSpec((CLUSTERS, senders * SLOTS, 128), lambda i: (0, sender(i), 0)),
            pl.BlockSpec((count, rows, rows), lambda i: (group(i), 0, 0)),
        ],
        out_specs=pl.BlockSpec((count, rows, 128), lambda i: (group(i), 0, 0)),
        out_shape=jax.ShapeDtypeStruct((groups, rows, 128), BF16),
        scratch_shapes=[pltpu.VMEM((CLUSTERS, ranks * SLOTS, 128), F32)],
        compiler_params=params(22),
        cost_estimate=cost(1, 1),
    )(target, rows_v, early, weights)


def unplace_kernel(who_ref, target_ref, o_ref, mean_ref, out_ref):
    tokens = target_ref.shape[2]
    half = o_ref.shape[0] // 2 * SLOTS
    right = o_ref[...].astype(F32).reshape(2 * half, 128).astype(BF16)
    right = jnp.concatenate([right[:half], right[half:]], axis=1)
    target = jnp.transpose(jnp.broadcast_to(target_ref[0], (128, tokens)))
    low = jnp.where(target < half, target, target - half)
    columns = lax.broadcasted_iota(jnp.int32, (tokens, half), 1)
    picked = (columns == jnp.tile(low, (1, half // 128))).astype(BF16)
    out = jnp.dot(picked, right, preferred_element_type=F32)
    out_ref[0, :tokens] = jnp.where(target < half, out[:, :128], out[:, 128:]).astype(BF16)
    means = mean_ref[...]
    high = means.astype(BF16)
    count = means.shape[0]
    out_ref[0, tokens : tokens + count] = high
    out_ref[0, tokens + count :] = (means - high.astype(F32)).astype(BF16)


def unplace(who, target, mixed, means):
    tokens, partners = target.shape[2], who.shape[0]
    count = CLUSTERS // target.shape[0]
    return pl.pallas_call(
        unplace_kernel,
        grid_spec=pltpu.PrefetchScalarGridSpec(
            num_scalar_prefetch=1,
            grid=(partners,),
            in_specs=[
                pl.BlockSpec((1, 1, tokens), lambda i, who: (who[i], 0, 0)),
                pl.BlockSpec((CLUSTERS, SLOTS, 128), lambda i, who: (0, who[i], 0)),
                pl.BlockSpec((count, 128), lambda i, who: (who[i], 0)),
            ],
            out_specs=pl.BlockSpec((1, tokens + 2 * count, 128), lambda i, who: (i, 0, 0)),
        ),
        out_shape=jax.ShapeDtypeStruct((partners, tokens + 2 * count, 128), BF16),
        compiler_params=params(12),
        cost_estimate=cost(1, 1),
    )(who, target, mixed, means)


def head_body(queries, keys, values, cluster_of, slot_of, centroids, out_weight):
    ranks = lax.axis_size("ctx")
    me = lax.axis_index("ctx")
    mine = lax.axis_index("head")
    tokens = queries.shape[0]
    cl_dev = CLUSTERS // ranks
    cap = ranks * SLOTS
    y, core = mine // 2, mine % 2

    def swap_y(x):
        return lax.ppermute(x, "head", [(0, 2), (1, 3), (2, 0), (3, 1)])

    def swap_core(x):
        return lax.ppermute(x, "head", [(0, 1), (1, 0), (2, 3), (3, 2)])

    def after(x, *others):
        return lax.optimization_barrier((x, others))[0]

    def swap_ctx(x, d):
        return lax.ppermute(x, "ctx", [(i, i ^ d) for i in range(ranks)])

    def exchange(x):
        return lax.all_to_all(x, "ctx", split_axis=0, concat_axis=0, tiled=True)

    first = exchange(pack((queries, keys), (cluster_of, slot_of)))
    marks = first[:, 2 * tokens :, :].astype(jnp.int32)
    target = marks[:, : tokens // 128, :] * SLOTS + marks[:, tokens // 128 :, :]
    target = target.reshape(ranks, 1, tokens)

    cols = out_weight.shape[1] // 4
    heads = me ^ jnp.array(LANES, jnp.int32)
    far = 2 * (1 - y)
    both = pick(heads, out_weight, (far + 1 - core, far + core), cols)
    both = swap_y(both)
    w_own = pick(heads, out_weight, (mine,), cols)
    beside = pick(heads, out_weight, (2 * y + 1 - core,), cols)
    beside, corner = swap_core(beside), swap_core(both[: both.shape[0] // 2])
    values = after(values, beside, w_own)
    weight = join(
        (w_own, both, beside, corner),
        (0, both.shape[0] // 2, 0, 0),
        ((0, 512), (512, 256), (768, 256)),
    )
    rows_v = exchange(after(pack((values,)), first))

    def paired(x):
        return x.reshape(CLUSTERS // PAIR, PAIR * cap, 128)

    q_rows, k_rows, at = place_pair(target, first, tokens)
    weights, means, early = weigh(paired(q_rows), paired(k_rows), paired(at), tokens)
    early = early.reshape(CLUSTERS, cap, 128)
    early, weights = (pltpu.with_memory_space_constraint(x, pltpu.HBM) for x in (early, weights))
    rows_v = after(rows_v, weight)
    mixed = mix(target, rows_v, early, weights).reshape(CLUSTERS, cap, 128)

    got, sent = {}, {}

    def leave(d, *others):
        block = unplace(after(jnp.reshape(me ^ d, (1,)), *others), target, mixed, means)
        sent[d] = block.reshape(block.shape[1:])

    def go(d):
        got[d] = swap_ctx(sent[d], d)

    def side(*blocks):
        return jnp.concatenate([block[:tokens] for block in blocks], axis=1)

    plan = (4, 2, 0, 3, 1, 5, 6, 7)
    waits = {5: (0,), 6: (4,), 7: (5, 9)}
    ends = {}
    for n, d in enumerate(plan):
        if d == 7:
            own_near = side(*[got[d] for d in LANES[1:4]])
            ends[9] = own_near
        others = [ends[k] for k in waits.get(d, ())]
        if n:
            others = [sent[plan[n - 1]]] + others
        leave(d, *others)
        if d:
            go(d)
            ends[d] = got[d]
        else:
            got[0] = sent[0]
            y_0 = ends[0] = swap_y(got[0])
    own, there = {}, {}
    y_near = swap_y(own_near)
    own[2] = side(got[4], got[5])
    there[2] = swap_y(own[2])
    own[3] = side(got[6], got[7])
    there[3] = swap_y(own[3])
    same = {1: side(got[0], own_near, y_0, y_near), 2: side(own[2], there[2])}

    def add(total, left, row):
        more = jnp.dot(left, weight[row : row + left.shape[1]], preferred_element_type=F32)
        return more if total is None else total + more

    total = None
    for n, row in ((1, 0), (2, 2048)):
        total = add(total, jnp.concatenate([same[n], swap_core(same[n])], axis=1), row)
    row = 3072
    total = add(total, swap_core(own[3]), row + 512)
    last = swap_core(after(there[3], total))
    total = add(total, side(own[3], there[3]), row)
    projected = add(total, last, row + 768).astype(BF16)

    tails = jnp.stack([got[d][tokens:] for d in range(ranks)]).astype(F32)
    tails = tails[:, :cl_dev] + tails[:, cl_dev:]
    tails = jnp.concatenate(
        [lax.dynamic_slice_in_dim(tails, me ^ d, 1, 0) for d in range(ranks)], axis=0
    )
    new_centroids = mix_rate * centroids + (1.0 - mix_rate) * tails
    return (projected, new_centroids)


def dispatch(queries, keys, values, cluster_of, *rest):
    ranks, heads = lax.axis_size("ctx"), cluster_of.shape[0]
    whole_heads = ranks == heads == 8 and lax.axis_size("head") == 4
    step = head_body if whole_heads else body
    return step(queries, keys, values, cluster_of, *rest)


def solution(mesh):
    in_specs = (
        P("ctx", "head"),
        P("ctx", "head"),
        P("ctx", "head"),
        P("head", "ctx"),
        P("head", "ctx"),
        P("head", "ctx", None),
        P("head", None),
    )
    out_specs = (P("ctx", "head"), P("head", "ctx", None))
    return jax.shard_map(
        dispatch, mesh=mesh, in_specs=in_specs, out_specs=out_specs, check_vma=False
    )
```

```python
import functools
import math

import jax
import jax.numpy as jnp
from jax import lax
from jax.experimental import pallas as pl
from jax.experimental.pallas import tpu as pltpu
from jax.sharding import PartitionSpec as P

CLUSTERS = 256
SLOTS = 8


mix_rate = 0.5
neg_fill = -1e30


def attend(q_rows, k_rows, v_rows, positions):
    scale = 1.0 / math.sqrt(q_rows.shape[-1])
    scores = jnp.einsum("gqd,gkd->gqk", q_rows, k_rows, preferred_element_type=jnp.float32) * scale
    allowed = (positions[:, None, :] >= 0) & (positions[:, None, :] <= positions[:, :, None])
    scores = jnp.where(allowed, scores, neg_fill)
    top = jnp.max(scores, axis=2, keepdims=True)
    weights = jnp.where(allowed, jnp.exp(scores - top), 0.0).astype(jnp.bfloat16)
    total = jnp.sum(weights.astype(jnp.float32), axis=2, keepdims=True)
    mixed = jnp.einsum("gqk,gkd->gqd", weights, v_rows, preferred_element_type=jnp.float32)
    return (mixed / jnp.where(total > 0.0, total, 1.0)).astype(jnp.bfloat16)


def to_clusters(rows, cl_dev):
    senders, width, items = (rows.shape[0], rows.shape[1], rows.shape[2])
    slots = width // cl_dev
    shaped = rows.reshape((senders, cl_dev, slots, items) + rows.shape[3:])
    if rows.ndim == 4:
        order = (3, 1, 0, 2, 4)
    else:
        order = (3, 1, 0, 2)
    return jnp.transpose(shaped, order).reshape((items * cl_dev, senders * slots) + rows.shape[3:])


def from_clusters(mixed, senders, cl_dev, items):
    slots = mixed.shape[1] // senders
    shaped = mixed.reshape(items, cl_dev, senders, slots, mixed.shape[2])
    return jnp.transpose(shaped, (2, 1, 3, 0, 4)).reshape(
        senders, cl_dev * slots, items, mixed.shape[2]
    )


def owner_work(incoming, cl_dev):
    q_in, k_in, v_in, p_in = incoming
    senders, items = (q_in.shape[0], q_in.shape[2])
    q_rows = to_clusters(q_in, cl_dev)
    k_rows = to_clusters(k_in, cl_dev)
    v_rows = to_clusters(v_in, cl_dev)
    p_rows = to_clusters(p_in, cl_dev)
    mixed = attend(q_rows, k_rows, v_rows, p_rows)
    back = from_clusters(mixed, senders, cl_dev, items)
    return back


def body(queries, keys, values, cluster_of, slot_of, centroids, out_weight):
    ranks = lax.axis_size("ctx")
    rank_here = lax.axis_index("ctx")
    tok_rows = queries.shape[0]
    head_rows = cluster_of.shape[0]
    head_size = queries.shape[1] // head_rows
    cl_dev = CLUSTERS // ranks
    width = CLUSTERS * SLOTS
    target = jnp.transpose(cluster_of * SLOTS + slot_of)
    head_ids = jnp.broadcast_to(jnp.arange(head_rows, dtype=jnp.int32)[None, :], target.shape)

    def place(rows):
        shaped = rows.reshape(tok_rows, head_rows, head_size)
        filled = (
            jnp.zeros((width, head_rows, head_size), rows.dtype).at[target, head_ids].set(shaped)
        )
        return filled.reshape(ranks, width // ranks, head_rows, head_size)

    token_pos = rank_here * tok_rows + jnp.arange(tok_rows, dtype=jnp.int32)
    pos_slots = (
        jnp.full((width, head_rows), -1, jnp.int32)
        .at[target, head_ids]
        .set(jnp.broadcast_to(token_pos[:, None], target.shape))
    )
    pos_slots = pos_slots.reshape(ranks, width // ranks, head_rows)
    incoming = (
        lax.all_to_all(place(queries), "ctx", split_axis=0, concat_axis=0, tiled=True),
        lax.all_to_all(place(keys), "ctx", split_axis=0, concat_axis=0, tiled=True),
        lax.all_to_all(place(values), "ctx", split_axis=0, concat_axis=0, tiled=True),
        lax.all_to_all(pos_slots, "ctx", split_axis=0, concat_axis=0, tiled=True),
    )
    worked = owner_work(incoming, cl_dev)
    returned = lax.all_to_all(worked, "ctx", split_axis=0, concat_axis=0, tiled=True)
    rows_back = returned.reshape(width, head_rows, head_size)
    attended = rows_back[target, head_ids].reshape(tok_rows, head_rows * head_size)
    member = (
        cluster_of[:, :, None] == jnp.arange(CLUSTERS, dtype=jnp.int32)[None, None, :]
    ).astype(jnp.bfloat16)
    q_three = queries.reshape(tok_rows, head_rows, head_size)
    k_three = keys.reshape(tok_rows, head_rows, head_size)
    local_sums = jnp.einsum("htc,thd->hcd", member, q_three, preferred_element_type=jnp.float32)
    local_sums = local_sums + jnp.einsum(
        "htc,thd->hcd", member, k_three, preferred_element_type=jnp.float32
    )
    local_counts = jnp.sum(member, axis=1, dtype=jnp.float32)
    totals, counts = (
        lax.psum_scatter(
            local_sums.astype(jnp.bfloat16), "ctx", scatter_dimension=1, tiled=True
        ).astype(jnp.float32),
        lax.psum_scatter(
            local_counts.astype(jnp.bfloat16), "ctx", scatter_dimension=1, tiled=True
        ).astype(jnp.float32),
    )
    means = totals / (2.0 * jnp.maximum(counts, 1.0))[:, :, None]
    new_centroids = mix_rate * centroids + (1.0 - mix_rate) * means
    summed = lax.psum_scatter(
        lax.dot_general(
            out_weight, attended, (((0,), (1,)), ((), ())), preferred_element_type=jnp.float32
        ),
        "head",
        scatter_dimension=0,
        tiled=True,
    )
    projected = jnp.transpose(summed).astype(jnp.bfloat16)
    return (projected, new_centroids)


BF16 = jnp.bfloat16
F32 = jnp.float32
PAIR = 2
EMPTY = 1e9
LANES = (0, 2, 3, 1, 4, 5, 6, 7)


def params(limit):
    return pltpu.CompilerParams(
        dimension_semantics=("arbitrary",), vmem_limit_bytes=limit * 1024 * 1024
    )


def cost(flops, nbytes, transcendentals=0):
    return pl.CostEstimate(
        flops=flops, bytes_accessed=nbytes, transcendentals=transcendentals
    )


def pack_kernel(count, marked, *refs):
    sources = refs[:count]
    out_ref, held, wide, marks, sems_in, sems_out = refs[count + 2 * marked :]
    heads = out_ref.shape[0]
    tokens = sources[0].shape[0]
    parts = 2
    rows = tokens // parts
    reads = []
    for n, source in enumerate(sources):
        for p in range(parts):
            here = pl.ds(p * rows, rows)
            reads.append(
                pltpu.make_async_copy(
                    source.at[here], held.at[n, here], sems_in.at[n * parts + p]
                )
            )
    for copy in reads:
        copy.start()
    writes = []
    if marked:
        lines = marks.shape[1] // 2
        for n in range(2):
            mark = refs[count + n][...].astype(F32)
            for line in range(lines):
                wide[:, n * lines + line, :] = mark[:, line * 128 : (line + 1) * 128]
        marks[...] = wide[...].astype(BF16)
        there = out_ref.at[:, pl.ds(count * tokens, 2 * lines)]
        writes.append(pltpu.make_async_copy(marks, there, sems_out.at[0]))
        writes[0].start()
    for n in range(count):
        for p in range(parts):
            reads[n * parts + p].wait()
            for j in range(heads):
                copy = pltpu.make_async_copy(
                    held.at[n, pl.ds(p * rows, rows), pl.ds(j * 128, 128)],
                    out_ref.at[j, pl.ds(n * tokens + p * rows, rows)],
                    sems_out.at[1 + (n * parts + p) * heads + j],
                )
                copy.start()
                writes.append(copy)
    for copy in writes:
        copy.wait()


def pack(sources, marks=()):
    tokens, width = sources[0].shape
    heads, count = width // 128, len(sources)
    marked = len(marks) > 0
    lines = len(marks) * (tokens // 128)
    rows = count * tokens + lines
    anywhere = pl.BlockSpec(memory_space=pl.ANY)
    args = list(sources)
    in_specs = [anywhere] * count
    for mark in marks:
        args.append(mark)
        in_specs.append(pl.BlockSpec(memory_space=pltpu.VMEM))
    return pl.pallas_call(
        functools.partial(pack_kernel, count, marked),
        in_specs=in_specs,
        out_specs=anywhere,
        out_shape=pltpu.HBM((heads, rows, 128), BF16),
        scratch_shapes=[
            pltpu.VMEM((count, tokens, width), BF16),
            pltpu.VMEM((heads, max(lines, 16), 128), F32),
            pltpu.VMEM((heads, max(lines, 16), 128), BF16),
            pltpu.SemaphoreType.DMA((2 * count,)),
            pltpu.SemaphoreType.DMA((2 * count * heads + 1,)),
        ],
        compiler_params=pltpu.CompilerParams(vmem_limit_bytes=60 * 1024 * 1024),
        cost_estimate=cost(0, 2 * heads * rows * 256),
    )(*args)


def pick_kernel(count, where_ref, weight_ref, out_ref, sems):
    heads, cols = where_ref.shape[0] - count, out_ref.shape[1]
    copies = []
    for n in range(count):
        column = pl.multiple_of(where_ref[heads + n] * cols, cols)
        for lane in range(heads):
            row = pl.multiple_of(where_ref[lane] * 128, 128)
            copies.append(
                pltpu.make_async_copy(
                    weight_ref.at[pl.ds(row, 128), pl.ds(column, cols)],
                    out_ref.at[pl.ds((n * heads + lane) * 128, 128)],
                    sems.at[len(copies)],
                )
            )
    for copy in copies:
        copy.start()
    for copy in copies:
        copy.wait()


def pick(heads, weight, columns, cols):
    count = len(columns)
    where = jnp.concatenate([heads, jnp.stack(columns)])
    return pl.pallas_call(
        functools.partial(pick_kernel, count),
        in_specs=[pl.BlockSpec(memory_space=pltpu.SMEM), pl.BlockSpec(memory_space=pl.ANY)],
        out_specs=pl.BlockSpec(memory_space=pltpu.VMEM),
        out_shape=pltpu.HBM((count * weight.shape[0], cols), BF16),
        scratch_shapes=[pltpu.SemaphoreType.DMA((heads.shape[0] * count,))],
        compiler_params=pltpu.CompilerParams(vmem_limit_bytes=56 * 1024 * 1024),
        cost_estimate=cost(1, 1),
    )(where, pltpu.with_memory_space_constraint(weight, pltpu.HBM))


def join_kernel(plan, *refs):
    sources, out_ref, sems = refs[:-2], refs[-2], refs[-1]
    copies, row = [], 0
    for part, first, count in plan:
        copies.append(
            pltpu.make_async_copy(
                sources[part].at[pl.ds(first, count)],
                out_ref.at[pl.ds(row, count)],
                sems.at[len(copies)],
            )
        )
        row += count
    for copy in copies:
        copy.start()
    for copy in copies:
        copy.wait()


def join(sources, starts, groups):
    plan = [(part, at + first, count) for first, count in groups for part, at in enumerate(starts)]
    rows, cols = sum(count for _, _, count in plan), sources[0].shape[1]
    return pl.pallas_call(
        functools.partial(join_kernel, plan),
        in_specs=[pl.BlockSpec(memory_space=pl.ANY)] * len(sources),
        out_specs=pl.BlockSpec(memory_space=pltpu.VMEM),
        out_shape=pltpu.HBM((rows, cols), BF16),
        scratch_shapes=[pltpu.SemaphoreType.DMA((len(plan),))],
        compiler_params=pltpu.CompilerParams(vmem_limit_bytes=56 * 1024 * 1024),
        cost_estimate=cost(1, 1),
    )(*sources)


def match(first, count, target):
    rows = first + lax.broadcasted_iota(jnp.int32, (count, target.shape[1]), 0)
    return rows == target


def by_slot(x):
    return x.reshape(x.shape[0] // SLOTS, SLOTS, 128)


def place_pair_kernel(target_ref, q_ref, k_ref, q_out, k_out, p_out, right):
    tokens = q_ref.shape[1]
    slots = q_out.shape[0] * SLOTS
    step = 1024
    right[:, :128] = q_ref[0]
    right[:, 128:] = k_ref[0]
    base = pl.program_id(0) * tokens
    token = (base + lax.broadcasted_iota(jnp.int32, (1, tokens), 1)).astype(F32)
    target = target_ref[0]

    def move(i, carry):
        picked = match(i * step, step, target)
        out = jnp.dot(picked.astype(BF16), right[...], preferred_element_type=F32)
        where = pl.ds(i * (step // SLOTS), step // SLOTS)
        q_out[where] = by_slot(out[:, :128]).astype(BF16)
        k_out[where] = by_slot(out[:, 128:]).astype(BF16)
        at = jnp.min(jnp.where(picked, token, EMPTY), axis=1, keepdims=True)
        p_out[where] = by_slot(jnp.broadcast_to(at, (step, 128)))
        return carry

    lax.fori_loop(0, slots // step, move, 0)


def place_pair(target, first, tokens):
    ranks = first.shape[0]
    spec_out = pl.BlockSpec((CLUSTERS, SLOTS, 128), lambda j: (0, j, 0))
    shape = (CLUSTERS, ranks * SLOTS, 128)
    return pl.pallas_call(
        place_pair_kernel,
        grid=(ranks,),
        in_specs=[
            pl.BlockSpec((1, 1, tokens), lambda j: (j, 0, 0)),
            pl.BlockSpec((1, tokens, 128), lambda j: (j, 0, 0)),
            pl.BlockSpec((1, tokens, 128), lambda j: (j, 1, 0)),
        ],
        out_specs=[spec_out, spec_out, spec_out],
        out_shape=[
            jax.ShapeDtypeStruct(shape, BF16),
            jax.ShapeDtypeStruct(shape, BF16),
            jax.ShapeDtypeStruct(shape, F32),
        ],
        scratch_shapes=[pltpu.VMEM((tokens, 256), BF16)],
        compiler_params=params(16),
        cost_estimate=cost(1, 1),
    )(target, first, first)


def weigh_kernel(tokens, q_ref, k_ref, p_ref, w_out, mean_out, early_out):
    count, rows = q_ref.shape[0], q_ref.shape[1]
    cap = rows // PAIR
    scale = 1.0 / math.sqrt(q_ref.shape[2])
    same = (
        lax.broadcasted_iota(jnp.int32, (rows, rows), 0) // cap
        == lax.broadcasted_iota(jnp.int32, (rows, rows), 1) // cap
    )
    for n in range(count):
        q, k, own = q_ref[n], k_ref[n], p_ref[n]
        scores = lax.dot_general(q, k, (((1,), (1,)), ((), ())), preferred_element_type=F32) * scale
        allowed = same & (jnp.transpose(own) <= own)
        scores = jnp.where(allowed, scores, neg_fill)
        top = jnp.max(scores, axis=1, keepdims=True)
        w_out[n] = jnp.where(allowed, jnp.exp(scores - top), 0.0).astype(BF16)
    share = p_ref[...] * (1.0 / tokens)
    early_out[...] = (share - jnp.floor(share) < 0.5).astype(BF16)
    both = (q_ref[...].astype(F32) + k_ref[...].astype(F32)).reshape(count * PAIR, cap, 128)
    held = (p_ref[...] < EMPTY).astype(F32).reshape(count * PAIR, cap, 128)
    mean_out[...] = jnp.sum(both, axis=1) / (2.0 * jnp.maximum(jnp.sum(held, axis=1), 1.0))


def weigh(q_rows, k_rows, at, tokens, step=16):
    groups, rows = q_rows.shape[0], q_rows.shape[1]
    spec = pl.BlockSpec((step, rows, 128), lambda i: (i, 0, 0))
    return pl.pallas_call(
        functools.partial(weigh_kernel, tokens),
        grid=(groups // step,),
        in_specs=[spec, spec, spec],
        out_specs=[
            pl.BlockSpec((step, rows, rows), lambda i: (i, 0, 0)),
            pl.BlockSpec((step * PAIR, 128), lambda i: (i, 0)),
            spec,
        ],
        out_shape=[
            pltpu.HBM((groups, rows, rows), BF16),
            jax.ShapeDtypeStruct((groups * PAIR, 128), F32),
            pltpu.HBM((groups, rows, 128), BF16),
        ],
        compiler_params=params(16),
        cost_estimate=cost(1, 1),
    )(q_rows, k_rows, at)


def mix_kernel(steps, target_ref, v_ref, early_ref, w_ref, o_out, v_rows):
    i = pl.program_id(0)
    slots = v_rows.shape[0] * SLOTS
    senders, tokens = v_ref.shape[0], v_ref.shape[1]
    count, rows = w_ref.shape[0], w_ref.shape[1]
    half = tokens // 2

    @pl.when(i < steps)
    def _():
        for n in range(senders):
            target = target_ref[n]
            picked = match(0, slots, target[:, :half]) | match(0, slots, target[:, half:])
            both = jnp.concatenate([v_ref[n, :half], v_ref[n, half:]], axis=1)
            out = jnp.dot(picked.astype(BF16), both, preferred_element_type=F32)
            early = early_ref[:, n * SLOTS : (n + 1) * SLOTS].astype(F32) > 0.0
            where = pl.ds(pl.multiple_of((i * senders + n) * SLOTS, SLOTS), SLOTS)
            v_rows[:, where, :] = jnp.where(early, by_slot(out[:, :128]), by_slot(out[:, 128:]))

    @pl.when(i >= steps)
    def _():
        ones = jnp.ones((rows, 128), BF16)
        for n in range(count):
            own = v_rows[pl.ds(((i - steps) * count + n) * PAIR, PAIR)]
            right = jnp.concatenate([own.reshape(rows, 128).astype(BF16), ones], axis=1)
            out = jnp.dot(w_ref[n], right, preferred_element_type=F32)
            total = out[:, 128:]
            o_out[n] = (out[:, :128] / jnp.where(total > 0.0, total, 1.0)).astype(BF16)


def mix(target, rows_v, early, weights, senders=4, count=32):
    ranks, tokens = rows_v.shape[0], rows_v.shape[1]
    groups, rows = weights.shape[0], weights.shape[1]
    steps = ranks // senders

    def sender(i):
        return jnp.minimum(i, steps - 1)

    def group(i):
        return jnp.maximum(i - steps, 0)

    return pl.pallas_call(
        functools.partial(mix_kernel, steps),
        grid=(steps + groups // count,),
        in_specs=[
            pl.BlockSpec((senders, 1, tokens), lambda i: (sender(i), 0, 0)),
            pl.BlockSpec((senders, tokens, 128), lambda i: (sender(i), 0, 0)),
            pl.BlockSpec((CLUSTERS, senders * SLOTS, 128), lambda i: (0, sender(i), 0)),
            pl.BlockSpec((count, rows, rows), lambda i: (group(i), 0, 0)),
        ],
        out_specs=pl.BlockSpec((count, rows, 128), lambda i: (group(i), 0, 0)),
        out_shape=jax.ShapeDtypeStruct((groups, rows, 128), BF16),
        scratch_shapes=[pltpu.VMEM((CLUSTERS, ranks * SLOTS, 128), F32)],
        compiler_params=params(22),
        cost_estimate=cost(1, 1),
    )(target, rows_v, early, weights)


def unplace_kernel(who_ref, target_ref, o_ref, mean_ref, out_ref):
    tokens = target_ref.shape[2]
    half = o_ref.shape[0] // 2 * SLOTS
    right = o_ref[...].astype(F32).reshape(2 * half, 128).astype(BF16)
    right = jnp.concatenate([right[:half], right[half:]], axis=1)
    target = jnp.transpose(jnp.broadcast_to(target_ref[0], (128, tokens)))
    low = jnp.where(target < half, target, target - half)
    columns = lax.broadcasted_iota(jnp.int32, (tokens, half), 1)
    picked = (columns == jnp.tile(low, (1, half // 128))).astype(BF16)
    out = jnp.dot(picked, right, preferred_element_type=F32)
    out_ref[0, :tokens] = jnp.where(target < half, out[:, :128], out[:, 128:]).astype(BF16)
    means = mean_ref[...]
    high = means.astype(BF16)
    count = means.shape[0]
    out_ref[0, tokens : tokens + count] = high
    out_ref[0, tokens + count :] = (means - high.astype(F32)).astype(BF16)


def unplace(who, target, mixed, means):
    tokens, partners = target.shape[2], who.shape[0]
    count = CLUSTERS // target.shape[0]
    return pl.pallas_call(
        unplace_kernel,
        grid_spec=pltpu.PrefetchScalarGridSpec(
            num_scalar_prefetch=1,
            grid=(partners,),
            in_specs=[
                pl.BlockSpec((1, 1, tokens), lambda i, who: (who[i], 0, 0)),
                pl.BlockSpec((CLUSTERS, SLOTS, 128), lambda i, who: (0, who[i], 0)),
                pl.BlockSpec((count, 128), lambda i, who: (who[i], 0)),
            ],
            out_specs=pl.BlockSpec((1, tokens + 2 * count, 128), lambda i, who: (i, 0, 0)),
        ),
        out_shape=jax.ShapeDtypeStruct((partners, tokens + 2 * count, 128), BF16),
        compiler_params=params(12),
        cost_estimate=cost(1, 1),
    )(who, target, mixed, means)


def head_body(queries, keys, values, cluster_of, slot_of, centroids, out_weight):
    ranks = lax.axis_size("ctx")
    me = lax.axis_index("ctx")
    mine = lax.axis_index("head")
    tokens = queries.shape[0]
    cl_dev = CLUSTERS // ranks
    cap = ranks * SLOTS
    y, core = mine // 2, mine % 2

    def swap_y(x):
        return lax.ppermute(x, "head", [(0, 2), (1, 3), (2, 0), (3, 1)])

    def swap_core(x):
        return lax.ppermute(x, "head", [(0, 1), (1, 0), (2, 3), (3, 2)])

    def after(x, *others):
        return lax.optimization_barrier((x, others))[0]

    def swap_ctx(x, d):
        return lax.ppermute(x, "ctx", [(i, i ^ d) for i in range(ranks)])

    def exchange(x):
        return lax.all_to_all(x, "ctx", split_axis=0, concat_axis=0, tiled=True)

    first = exchange(pack((queries, keys), (cluster_of, slot_of)))
    marks = first[:, 2 * tokens :, :].astype(jnp.int32)
    target = marks[:, : tokens // 128, :] * SLOTS + marks[:, tokens // 128 :, :]
    target = target.reshape(ranks, 1, tokens)

    cols = out_weight.shape[1] // 4
    heads = me ^ jnp.array(LANES, jnp.int32)
    far = 2 * (1 - y)
    both = pick(heads, out_weight, (far + 1 - core, far + core), cols)
    both = swap_y(both)
    w_own = pick(heads, out_weight, (mine,), cols)
    beside = pick(heads, out_weight, (2 * y + 1 - core,), cols)
    beside, corner = swap_core(beside), swap_core(both[: both.shape[0] // 2])
    values = after(values, beside, w_own)
    rows_v = exchange(after(pack((values,)), first))

    def paired(x):
        return x.reshape(CLUSTERS // PAIR, PAIR * cap, 128)

    q_rows, k_rows, at = place_pair(target, first, tokens)
    weights, means, early = weigh(paired(q_rows), paired(k_rows), paired(at), tokens)
    early = early.reshape(CLUSTERS, cap, 128)
    early, weights = (pltpu.with_memory_space_constraint(x, pltpu.HBM) for x in (early, weights))
    weight = join(
        (after(w_own, means), both, beside, corner),
        (0, both.shape[0] // 2, 0, 0),
        ((0, 512), (512, 256), (768, 256)),
    )
    rows_v = after(rows_v, weight)
    mixed = mix(target, rows_v, early, weights).reshape(CLUSTERS, cap, 128)

    got, sent = {}, {}

    def leave(d, *others):
        block = unplace(after(jnp.reshape(me ^ d, (1,)), *others), target, mixed, means)
        sent[d] = block.reshape(block.shape[1:])

    def go(d):
        got[d] = swap_ctx(sent[d], d)

    def side(*blocks):
        return jnp.concatenate([block[:tokens] for block in blocks], axis=1)

    plan = (4, 2, 0, 3, 1, 5, 6, 7)
    waits = {1: (0,), 6: (4,), 7: (5, 9)}
    ends = {}
    for n, d in enumerate(plan):
        if d == 7:
            own_near = side(*[got[d] for d in LANES[1:4]])
            ends[9] = own_near
        others = [ends[k] for k in waits.get(d, ())]
        if n:
            others = [sent[plan[n - 1]]] + others
        leave(d, *others)
        if d:
            go(d)
            ends[d] = got[d]
        else:
            got[0] = sent[0]
            y_0 = ends[0] = swap_y(got[0])
    own, there = {}, {}
    y_near = swap_y(own_near)
    own[2] = side(got[4], got[5])
    there[2] = swap_y(own[2])
    own[3] = side(got[6], got[7])
    there[3] = swap_y(own[3])
    same = {1: side(got[0], own_near, y_0, y_near), 2: side(own[2], there[2])}

    def add(total, left, row):
        more = jnp.dot(left, weight[row : row + left.shape[1]], preferred_element_type=F32)
        return more if total is None else total + more

    total = None
    for n, row in ((1, 0), (2, 2048)):
        total = add(total, jnp.concatenate([same[n], swap_core(same[n])], axis=1), row)
    row = 3072
    total = add(total, swap_core(own[3]), row + 512)
    last = swap_core(after(there[3], total))
    total = add(total, side(own[3], there[3]), row)
    projected = add(total, last, row + 768).astype(BF16)

    tails = jnp.stack([got[d][tokens:] for d in range(ranks)]).astype(F32)
    tails = tails[:, :cl_dev] + tails[:, cl_dev:]
    tails = jnp.concatenate(
        [lax.dynamic_slice_in_dim(tails, me ^ d, 1, 0) for d in range(ranks)], axis=0
    )
    new_centroids = mix_rate * centroids + (1.0 - mix_rate) * tails
    return (projected, new_centroids)


def dispatch(queries, keys, values, cluster_of, *rest):
    ranks, heads = lax.axis_size("ctx"), cluster_of.shape[0]
    whole_heads = ranks == heads == 8 and lax.axis_size("head") == 4
    step = head_body if whole_heads else body
    return step(queries, keys, values, cluster_of, *rest)


def solution(mesh):
    in_specs = (
        P("ctx", "head"),
        P("ctx", "head"),
        P("ctx", "head"),
        P("head", "ctx"),
        P("head", "ctx"),
        P("head", "ctx", None),
        P("head", None),
    )
    out_specs = (P("ctx", "head"), P("head", "ctx", None))
    return jax.shard_map(
        dispatch, mesh=mesh, in_specs=in_specs, out_specs=out_specs, check_vma=False
    )
```

```python
import functools
import math

import jax
import jax.numpy as jnp
from jax import lax
from jax.experimental import pallas as pl
from jax.experimental.pallas import tpu as pltpu
from jax.sharding import PartitionSpec as P

CLUSTERS = 256
SLOTS = 8


mix_rate = 0.5
neg_fill = -1e30


def attend(q_rows, k_rows, v_rows, positions):
    scale = 1.0 / math.sqrt(q_rows.shape[-1])
    scores = jnp.einsum("gqd,gkd->gqk", q_rows, k_rows, preferred_element_type=jnp.float32) * scale
    allowed = (positions[:, None, :] >= 0) & (positions[:, None, :] <= positions[:, :, None])
    scores = jnp.where(allowed, scores, neg_fill)
    top = jnp.max(scores, axis=2, keepdims=True)
    weights = jnp.where(allowed, jnp.exp(scores - top), 0.0).astype(jnp.bfloat16)
    total = jnp.sum(weights.astype(jnp.float32), axis=2, keepdims=True)
    mixed = jnp.einsum("gqk,gkd->gqd", weights, v_rows, preferred_element_type=jnp.float32)
    return (mixed / jnp.where(total > 0.0, total, 1.0)).astype(jnp.bfloat16)


def to_clusters(rows, cl_dev):
    senders, width, items = (rows.shape[0], rows.shape[1], rows.shape[2])
    slots = width // cl_dev
    shaped = rows.reshape((senders, cl_dev, slots, items) + rows.shape[3:])
    if rows.ndim == 4:
        order = (3, 1, 0, 2, 4)
    else:
        order = (3, 1, 0, 2)
    return jnp.transpose(shaped, order).reshape((items * cl_dev, senders * slots) + rows.shape[3:])


def from_clusters(mixed, senders, cl_dev, items):
    slots = mixed.shape[1] // senders
    shaped = mixed.reshape(items, cl_dev, senders, slots, mixed.shape[2])
    return jnp.transpose(shaped, (2, 1, 3, 0, 4)).reshape(
        senders, cl_dev * slots, items, mixed.shape[2]
    )


def owner_work(incoming, cl_dev):
    q_in, k_in, v_in, p_in = incoming
    senders, items = (q_in.shape[0], q_in.shape[2])
    q_rows = to_clusters(q_in, cl_dev)
    k_rows = to_clusters(k_in, cl_dev)
    v_rows = to_clusters(v_in, cl_dev)
    p_rows = to_clusters(p_in, cl_dev)
    mixed = attend(q_rows, k_rows, v_rows, p_rows)
    back = from_clusters(mixed, senders, cl_dev, items)
    return back


def body(queries, keys, values, cluster_of, slot_of, centroids, out_weight):
    ranks = lax.axis_size("ctx")
    rank_here = lax.axis_index("ctx")
    tok_rows = queries.shape[0]
    head_rows = cluster_of.shape[0]
    head_size = queries.shape[1] // head_rows
    cl_dev = CLUSTERS // ranks
    width = CLUSTERS * SLOTS
    target = jnp.transpose(cluster_of * SLOTS + slot_of)
    head_ids = jnp.broadcast_to(jnp.arange(head_rows, dtype=jnp.int32)[None, :], target.shape)

    def place(rows):
        shaped = rows.reshape(tok_rows, head_rows, head_size)
        filled = (
            jnp.zeros((width, head_rows, head_size), rows.dtype).at[target, head_ids].set(shaped)
        )
        return filled.reshape(ranks, width // ranks, head_rows, head_size)

    token_pos = rank_here * tok_rows + jnp.arange(tok_rows, dtype=jnp.int32)
    pos_slots = (
        jnp.full((width, head_rows), -1, jnp.int32)
        .at[target, head_ids]
        .set(jnp.broadcast_to(token_pos[:, None], target.shape))
    )
    pos_slots = pos_slots.reshape(ranks, width // ranks, head_rows)
    incoming = (
        lax.all_to_all(place(queries), "ctx", split_axis=0, concat_axis=0, tiled=True),
        lax.all_to_all(place(keys), "ctx", split_axis=0, concat_axis=0, tiled=True),
        lax.all_to_all(place(values), "ctx", split_axis=0, concat_axis=0, tiled=True),
        lax.all_to_all(pos_slots, "ctx", split_axis=0, concat_axis=0, tiled=True),
    )
    worked = owner_work(incoming, cl_dev)
    returned = lax.all_to_all(worked, "ctx", split_axis=0, concat_axis=0, tiled=True)
    rows_back = returned.reshape(width, head_rows, head_size)
    attended = rows_back[target, head_ids].reshape(tok_rows, head_rows * head_size)
    member = (
        cluster_of[:, :, None] == jnp.arange(CLUSTERS, dtype=jnp.int32)[None, None, :]
    ).astype(jnp.bfloat16)
    q_three = queries.reshape(tok_rows, head_rows, head_size)
    k_three = keys.reshape(tok_rows, head_rows, head_size)
    local_sums = jnp.einsum("htc,thd->hcd", member, q_three, preferred_element_type=jnp.float32)
    local_sums = local_sums + jnp.einsum(
        "htc,thd->hcd", member, k_three, preferred_element_type=jnp.float32
    )
    local_counts = jnp.sum(member, axis=1, dtype=jnp.float32)
    totals, counts = (
        lax.psum_scatter(
            local_sums.astype(jnp.bfloat16), "ctx", scatter_dimension=1, tiled=True
        ).astype(jnp.float32),
        lax.psum_scatter(
            local_counts.astype(jnp.bfloat16), "ctx", scatter_dimension=1, tiled=True
        ).astype(jnp.float32),
    )
    means = totals / (2.0 * jnp.maximum(counts, 1.0))[:, :, None]
    new_centroids = mix_rate * centroids + (1.0 - mix_rate) * means
    summed = lax.psum_scatter(
        lax.dot_general(
            out_weight, attended, (((0,), (1,)), ((), ())), preferred_element_type=jnp.float32
        ),
        "head",
        scatter_dimension=0,
        tiled=True,
    )
    projected = jnp.transpose(summed).astype(jnp.bfloat16)
    return (projected, new_centroids)


BF16 = jnp.bfloat16
F32 = jnp.float32
PAIR = 2
EMPTY = 1e9
LANES = (0, 2, 3, 1, 4, 5, 6, 7)


def params(limit):
    return pltpu.CompilerParams(
        dimension_semantics=("arbitrary",), vmem_limit_bytes=limit * 1024 * 1024
    )


def cost(flops, nbytes, transcendentals=0):
    return pl.CostEstimate(
        flops=flops, bytes_accessed=nbytes, transcendentals=transcendentals
    )


def pack_kernel(count, marked, *refs):
    sources = refs[:count]
    out_ref, held, wide, marks, sems_in, sems_out = refs[count + 2 * marked :]
    heads = out_ref.shape[0]
    tokens = sources[0].shape[0]
    parts = 2
    rows = tokens // parts
    reads = []
    for n, source in enumerate(sources):
        for p in range(parts):
            here = pl.ds(p * rows, rows)
            reads.append(
                pltpu.make_async_copy(
                    source.at[here], held.at[n, here], sems_in.at[n * parts + p]
                )
            )
    for copy in reads:
        copy.start()
    writes = []
    if marked:
        lines = marks.shape[1] // 2
        for n in range(2):
            mark = refs[count + n][...].astype(F32)
            for line in range(lines):
                wide[:, n * lines + line, :] = mark[:, line * 128 : (line + 1) * 128]
        marks[...] = wide[...].astype(BF16)
        there = out_ref.at[:, pl.ds(count * tokens, 2 * lines)]
        writes.append(pltpu.make_async_copy(marks, there, sems_out.at[0]))
        writes[0].start()
    for n in range(count):
        for p in range(parts):
            reads[n * parts + p].wait()
            for j in range(heads):
                copy = pltpu.make_async_copy(
                    held.at[n, pl.ds(p * rows, rows), pl.ds(j * 128, 128)],
                    out_ref.at[j, pl.ds(n * tokens + p * rows, rows)],
                    sems_out.at[1 + (n * parts + p) * heads + j],
                )
                copy.start()
                writes.append(copy)
    for copy in writes:
        copy.wait()


def pack(sources, marks=()):
    tokens, width = sources[0].shape
    heads, count = width // 128, len(sources)
    marked = len(marks) > 0
    lines = len(marks) * (tokens // 128)
    rows = count * tokens + lines
    anywhere = pl.BlockSpec(memory_space=pl.ANY)
    args = list(sources)
    in_specs = [anywhere] * count
    for mark in marks:
        args.append(mark)
        in_specs.append(pl.BlockSpec(memory_space=pltpu.VMEM))
    return pl.pallas_call(
        functools.partial(pack_kernel, count, marked),
        in_specs=in_specs,
        out_specs=anywhere,
        out_shape=pltpu.HBM((heads, rows, 128), BF16),
        scratch_shapes=[
            pltpu.VMEM((count, tokens, width), BF16),
            pltpu.VMEM((heads, max(lines, 16), 128), F32),
            pltpu.VMEM((heads, max(lines, 16), 128), BF16),
            pltpu.SemaphoreType.DMA((2 * count,)),
            pltpu.SemaphoreType.DMA((2 * count * heads + 1,)),
        ],
        compiler_params=pltpu.CompilerParams(vmem_limit_bytes=60 * 1024 * 1024),
        cost_estimate=cost(0, 2 * heads * rows * 256),
    )(*args)


def pick_kernel(count, where_ref, weight_ref, out_ref, sems):
    heads, cols = where_ref.shape[0] - count, out_ref.shape[1]
    copies = []
    for n in range(count):
        column = pl.multiple_of(where_ref[heads + n] * cols, cols)
        for lane in range(heads):
            row = pl.multiple_of(where_ref[lane] * 128, 128)
            copies.append(
                pltpu.make_async_copy(
                    weight_ref.at[pl.ds(row, 128), pl.ds(column, cols)],
                    out_ref.at[pl.ds((n * heads + lane) * 128, 128)],
                    sems.at[len(copies)],
                )
            )
    for copy in copies:
        copy.start()
    for copy in copies:
        copy.wait()


def pick(heads, weight, columns, cols):
    count = len(columns)
    where = jnp.concatenate([heads, jnp.stack(columns)])
    return pl.pallas_call(
        functools.partial(pick_kernel, count),
        in_specs=[pl.BlockSpec(memory_space=pltpu.SMEM), pl.BlockSpec(memory_space=pl.ANY)],
        out_specs=pl.BlockSpec(memory_space=pltpu.VMEM),
        out_shape=pltpu.HBM((count * weight.shape[0], cols), BF16),
        scratch_shapes=[pltpu.SemaphoreType.DMA((heads.shape[0] * count,))],
        compiler_params=pltpu.CompilerParams(vmem_limit_bytes=56 * 1024 * 1024),
        cost_estimate=cost(1, 1),
    )(where, pltpu.with_memory_space_constraint(weight, pltpu.HBM))


def join_kernel(plan, *refs):
    sources, out_ref, sems = refs[:-2], refs[-2], refs[-1]
    copies, row = [], 0
    for part, first, count in plan:
        copies.append(
            pltpu.make_async_copy(
                sources[part].at[pl.ds(first, count)],
                out_ref.at[pl.ds(row, count)],
                sems.at[len(copies)],
            )
        )
        row += count
    for copy in copies:
        copy.start()
    for copy in copies:
        copy.wait()


def join(sources, starts, groups):
    plan = [(part, at + first, count) for first, count in groups for part, at in enumerate(starts)]
    rows, cols = sum(count for _, _, count in plan), sources[0].shape[1]
    return pl.pallas_call(
        functools.partial(join_kernel, plan),
        in_specs=[pl.BlockSpec(memory_space=pl.ANY)] * len(sources),
        out_specs=pl.BlockSpec(memory_space=pltpu.VMEM),
        out_shape=pltpu.HBM((rows, cols), BF16),
        scratch_shapes=[pltpu.SemaphoreType.DMA((len(plan),))],
        compiler_params=pltpu.CompilerParams(vmem_limit_bytes=56 * 1024 * 1024),
        cost_estimate=cost(1, 1),
    )(*sources)


def match(first, count, target):
    rows = first + lax.broadcasted_iota(jnp.int32, (count, target.shape[1]), 0)
    return rows == target


def by_slot(x):
    return x.reshape(x.shape[0] // SLOTS, SLOTS, 128)


def place_pair_kernel(target_ref, q_ref, k_ref, q_out, k_out, p_out, right):
    tokens = q_ref.shape[1]
    slots = q_out.shape[0] * SLOTS
    step = 1024
    right[:, :128] = q_ref[0]
    right[:, 128:] = k_ref[0]
    base = pl.program_id(0) * tokens
    token = (base + lax.broadcasted_iota(jnp.int32, (1, tokens), 1)).astype(F32)
    target = target_ref[0]

    def move(i, carry):
        picked = match(i * step, step, target)
        out = jnp.dot(picked.astype(BF16), right[...], preferred_element_type=F32)
        where = pl.ds(i * (step // SLOTS), step // SLOTS)
        q_out[where] = by_slot(out[:, :128]).astype(BF16)
        k_out[where] = by_slot(out[:, 128:]).astype(BF16)
        at = jnp.min(jnp.where(picked, token, EMPTY), axis=1, keepdims=True)
        p_out[where] = by_slot(jnp.broadcast_to(at, (step, 128)))
        return carry

    lax.fori_loop(0, slots // step, move, 0)


def place_pair(target, first, tokens):
    ranks = first.shape[0]
    spec_out = pl.BlockSpec((CLUSTERS, SLOTS, 128), lambda j: (0, j, 0))
    shape = (CLUSTERS, ranks * SLOTS, 128)
    return pl.pallas_call(
        place_pair_kernel,
        grid=(ranks,),
        in_specs=[
            pl.BlockSpec((1, 1, tokens), lambda j: (j, 0, 0)),
            pl.BlockSpec((1, tokens, 128), lambda j: (j, 0, 0)),
            pl.BlockSpec((1, tokens, 128), lambda j: (j, 1, 0)),
        ],
        out_specs=[spec_out, spec_out, spec_out],
        out_shape=[
            jax.ShapeDtypeStruct(shape, BF16),
            jax.ShapeDtypeStruct(shape, BF16),
            jax.ShapeDtypeStruct(shape, F32),
        ],
        scratch_shapes=[pltpu.VMEM((tokens, 256), BF16)],
        compiler_params=params(16),
        cost_estimate=cost(1, 1),
    )(target, first, first)


def weigh_kernel(tokens, q_ref, k_ref, p_ref, w_out, mean_out, early_out):
    count, rows = q_ref.shape[0], q_ref.shape[1]
    cap = rows // PAIR
    scale = 1.0 / math.sqrt(q_ref.shape[2])
    same = (
        lax.broadcasted_iota(jnp.int32, (rows, rows), 0) // cap
        == lax.broadcasted_iota(jnp.int32, (rows, rows), 1) // cap
    )
    for n in range(count):
        q, k, own = q_ref[n], k_ref[n], p_ref[n]
        scores = lax.dot_general(q, k, (((1,), (1,)), ((), ())), preferred_element_type=F32) * scale
        allowed = same & (jnp.transpose(own) <= own)
        scores = jnp.where(allowed, scores, neg_fill)
        top = jnp.max(scores, axis=1, keepdims=True)
        w_out[n] = jnp.where(allowed, jnp.exp(scores - top), 0.0).astype(BF16)
    share = p_ref[...] * (1.0 / tokens)
    early_out[...] = (share - jnp.floor(share) < 0.5).astype(BF16)
    both = (q_ref[...].astype(F32) + k_ref[...].astype(F32)).reshape(count * PAIR, cap, 128)
    held = (p_ref[...] < EMPTY).astype(F32).reshape(count * PAIR, cap, 128)
    mean_out[...] = jnp.sum(both, axis=1) / (2.0 * jnp.maximum(jnp.sum(held, axis=1), 1.0))


def weigh(q_rows, k_rows, at, tokens, step=16):
    groups, rows = q_rows.shape[0], q_rows.shape[1]
    spec = pl.BlockSpec((step, rows, 128), lambda i: (i, 0, 0))
    return pl.pallas_call(
        functools.partial(weigh_kernel, tokens),
        grid=(groups // step,),
        in_specs=[spec, spec, spec],
        out_specs=[
            pl.BlockSpec((step, rows, rows), lambda i: (i, 0, 0)),
            pl.BlockSpec((step * PAIR, 128), lambda i: (i, 0)),
            spec,
        ],
        out_shape=[
            pltpu.HBM((groups, rows, rows), BF16),
            jax.ShapeDtypeStruct((groups * PAIR, 128), F32),
            pltpu.HBM((groups, rows, 128), BF16),
        ],
        compiler_params=params(16),
        cost_estimate=cost(1, 1),
    )(q_rows, k_rows, at)


def mix_kernel(steps, target_ref, v_ref, early_ref, w_ref, o_out, v_rows):
    i = pl.program_id(0)
    slots = v_rows.shape[0] * SLOTS
    senders, tokens = v_ref.shape[0], v_ref.shape[1]
    count, rows = w_ref.shape[0], w_ref.shape[1]
    half = tokens // 2

    @pl.when(i < steps)
    def _():
        for n in range(senders):
            target = target_ref[n]
            picked = match(0, slots, target[:, :half]) | match(0, slots, target[:, half:])
            both = jnp.concatenate([v_ref[n, :half], v_ref[n, half:]], axis=1)
            out = jnp.dot(picked.astype(BF16), both, preferred_element_type=F32)
            early = early_ref[:, n * SLOTS : (n + 1) * SLOTS].astype(F32) > 0.0
            where = pl.ds(pl.multiple_of((i * senders + n) * SLOTS, SLOTS), SLOTS)
            v_rows[:, where, :] = jnp.where(early, by_slot(out[:, :128]), by_slot(out[:, 128:]))

    @pl.when(i >= steps)
    def _():
        ones = jnp.ones((rows, 128), BF16)
        for n in range(count):
            own = v_rows[pl.ds(((i - steps) * count + n) * PAIR, PAIR)]
            right = jnp.concatenate([own.reshape(rows, 128).astype(BF16), ones], axis=1)
            out = jnp.dot(w_ref[n], right, preferred_element_type=F32)
            total = out[:, 128:]
            o_out[n] = (out[:, :128] / jnp.where(total > 0.0, total, 1.0)).astype(BF16)


def mix(target, rows_v, early, weights, senders=4, count=64):
    ranks, tokens = rows_v.shape[0], rows_v.shape[1]
    groups, rows = weights.shape[0], weights.shape[1]
    steps = ranks // senders

    def sender(i):
        return jnp.minimum(i, steps - 1)

    def group(i):
        return jnp.maximum(i - steps, 0)

    return pl.pallas_call(
        functools.partial(mix_kernel, steps),
        grid=(steps + groups // count,),
        in_specs=[
            pl.BlockSpec((senders, 1, tokens), lambda i: (sender(i), 0, 0)),
            pl.BlockSpec((senders, tokens, 128), lambda i: (sender(i), 0, 0)),
            pl.BlockSpec((CLUSTERS, senders * SLOTS, 128), lambda i: (0, sender(i), 0)),
            pl.BlockSpec((count, rows, rows), lambda i: (group(i), 0, 0)),
        ],
        out_specs=pl.BlockSpec((count, rows, 128), lambda i: (group(i), 0, 0)),
        out_shape=jax.ShapeDtypeStruct((groups, rows, 128), BF16),
        scratch_shapes=[pltpu.VMEM((CLUSTERS, ranks * SLOTS, 128), F32)],
        compiler_params=params(22),
        cost_estimate=cost(1, 1),
    )(target, rows_v, early, weights)


def unplace_kernel(who_ref, target_ref, o_ref, mean_ref, out_ref):
    tokens = target_ref.shape[2]
    half = o_ref.shape[0] // 2 * SLOTS
    right = o_ref[...].astype(F32).reshape(2 * half, 128).astype(BF16)
    right = jnp.concatenate([right[:half], right[half:]], axis=1)
    target = jnp.transpose(jnp.broadcast_to(target_ref[0], (128, tokens)))
    low = jnp.where(target < half, target, target - half)
    columns = lax.broadcasted_iota(jnp.int32, (tokens, half), 1)
    picked = (columns == jnp.tile(low, (1, half // 128))).astype(BF16)
    out = jnp.dot(picked, right, preferred_element_type=F32)
    out_ref[0, :tokens] = jnp.where(target < half, out[:, :128], out[:, 128:]).astype(BF16)
    means = mean_ref[...]
    high = means.astype(BF16)
    count = means.shape[0]
    out_ref[0, tokens : tokens + count] = high
    out_ref[0, tokens + count :] = (means - high.astype(F32)).astype(BF16)


def unplace(who, target, mixed, means):
    tokens, partners = target.shape[2], who.shape[0]
    count = CLUSTERS // target.shape[0]
    return pl.pallas_call(
        unplace_kernel,
        grid_spec=pltpu.PrefetchScalarGridSpec(
            num_scalar_prefetch=1,
            grid=(partners,),
            in_specs=[
                pl.BlockSpec((1, 1, tokens), lambda i, who: (who[i], 0, 0)),
                pl.BlockSpec((CLUSTERS, SLOTS, 128), lambda i, who: (0, who[i], 0)),
                pl.BlockSpec((count, 128), lambda i, who: (who[i], 0)),
            ],
            out_specs=pl.BlockSpec((1, tokens + 2 * count, 128), lambda i, who: (i, 0, 0)),
        ),
        out_shape=jax.ShapeDtypeStruct((partners, tokens + 2 * count, 128), BF16),
        compiler_params=params(12),
        cost_estimate=cost(1, 1),
    )(who, target, mixed, means)


def head_body(queries, keys, values, cluster_of, slot_of, centroids, out_weight):
    ranks = lax.axis_size("ctx")
    me = lax.axis_index("ctx")
    mine = lax.axis_index("head")
    tokens = queries.shape[0]
    cl_dev = CLUSTERS // ranks
    cap = ranks * SLOTS
    y, core = mine // 2, mine % 2

    def swap_y(x):
        return lax.ppermute(x, "head", [(0, 2), (1, 3), (2, 0), (3, 1)])

    def swap_core(x):
        return lax.ppermute(x, "head", [(0, 1), (1, 0), (2, 3), (3, 2)])

    def after(x, *others):
        return lax.optimization_barrier((x, others))[0]

    def swap_ctx(x, d):
        return lax.ppermute(x, "ctx", [(i, i ^ d) for i in range(ranks)])

    def exchange(x):
        return lax.all_to_all(x, "ctx", split_axis=0, concat_axis=0, tiled=True)

    first = exchange(pack((queries, keys), (cluster_of, slot_of)))
    marks = first[:, 2 * tokens :, :].astype(jnp.int32)
    target = marks[:, : tokens // 128, :] * SLOTS + marks[:, tokens // 128 :, :]
    target = target.reshape(ranks, 1, tokens)

    cols = out_weight.shape[1] // 4
    heads = me ^ jnp.array(LANES, jnp.int32)
    far = 2 * (1 - y)
    both = pick(heads, out_weight, (far + 1 - core, far + core), cols)
    both = swap_y(both)
    w_own = pick(heads, out_weight, (mine,), cols)
    beside = pick(heads, out_weight, (2 * y + 1 - core,), cols)
    beside, corner = swap_core(beside), swap_core(both[: both.shape[0] // 2])
    values = after(values, beside, w_own)
    weight = join(
        (w_own, both, beside, corner),
        (0, both.shape[0] // 2, 0, 0),
        ((0, 512), (512, 256), (768, 256)),
    )
    rows_v = exchange(after(pack((values,)), first))

    def paired(x):
        return x.reshape(CLUSTERS // PAIR, PAIR * cap, 128)

    q_rows, k_rows, at = place_pair(target, first, tokens)
    weights, means, early = weigh(paired(q_rows), paired(k_rows), paired(at), tokens)
    early = early.reshape(CLUSTERS, cap, 128)
    early, weights = (pltpu.with_memory_space_constraint(x, pltpu.HBM) for x in (early, weights))
    rows_v = after(rows_v, weight)
    mixed = mix(target, rows_v, early, weights).reshape(CLUSTERS, cap, 128)

    got, sent = {}, {}

    def leave(d, *others):
        block = unplace(after(jnp.reshape(me ^ d, (1,)), *others), target, mixed, means)
        sent[d] = block.reshape(block.shape[1:])

    def go(d):
        got[d] = swap_ctx(sent[d], d)

    def side(*blocks):
        return jnp.concatenate([block[:tokens] for block in blocks], axis=1)

    plan = (4, 2, 0, 3, 1, 5, 6, 7)
    waits = {5: (0,), 6: (4,), 7: (5, 9)}
    ends = {}
    for n, d in enumerate(plan):
        if d == 7:
            own_near = side(*[got[d] for d in LANES[1:4]])
            ends[9] = own_near
        others = [ends[k] for k in waits.get(d, ())]
        if n:
            others = [sent[plan[n - 1]]] + others
        leave(d, *others)
        if d:
            go(d)
            ends[d] = got[d]
        else:
            got[0] = sent[0]
            y_0 = ends[0] = swap_y(got[0])
    own, there = {}, {}
    y_near = swap_y(own_near)
    own[2] = side(got[4], got[5])
    there[2] = swap_y(own[2])
    own[3] = side(got[6], got[7])
    there[3] = swap_y(own[3])
    same = {1: side(got[0], own_near, y_0, y_near), 2: side(own[2], there[2])}

    def add(total, left, row):
        more = jnp.dot(left, weight[row : row + left.shape[1]], preferred_element_type=F32)
        return more if total is None else total + more

    total = None
    for n, row in ((1, 0), (2, 2048)):
        total = add(total, jnp.concatenate([same[n], swap_core(same[n])], axis=1), row)
    row = 3072
    total = add(total, swap_core(own[3]), row + 512)
    last = swap_core(after(there[3], total))
    total = add(total, side(own[3], there[3]), row)
    projected = add(total, last, row + 768).astype(BF16)

    tails = jnp.stack([got[d][tokens:] for d in range(ranks)]).astype(F32)
    tails = tails[:, :cl_dev] + tails[:, cl_dev:]
    tails = jnp.concatenate(
        [lax.dynamic_slice_in_dim(tails, me ^ d, 1, 0) for d in range(ranks)], axis=0
    )
    new_centroids = mix_rate * centroids + (1.0 - mix_rate) * tails
    return (projected, new_centroids)


def dispatch(queries, keys, values, cluster_of, *rest):
    ranks, heads = lax.axis_size("ctx"), cluster_of.shape[0]
    whole_heads = ranks == heads == 8 and lax.axis_size("head") == 4
    step = head_body if whole_heads else body
    return step(queries, keys, values, cluster_of, *rest)


def solution(mesh):
    in_specs = (
        P("ctx", "head"),
        P("ctx", "head"),
        P("ctx", "head"),
        P("head", "ctx"),
        P("head", "ctx"),
        P("head", "ctx", None),
        P("head", None),
    )
    out_specs = (P("ctx", "head"), P("head", "ctx", None))
    return jax.shard_map(
        dispatch, mesh=mesh, in_specs=in_specs, out_specs=out_specs, check_vma=False
    )
```
